32 devices in a mesh: dp: 4 (over y, x), fsdp: 8 (over z, core).
Axes of the slice: x: 2, y: 2, z: 4, core: 2. Of those that a mesh axis runs over, the one named last changes fastest.
Arguments:
- inputs: bfloat16 [4096, 2048], P(('dp', 'fsdp')), may hold values from -6 to 6
- segment_ids: int32 [4096], P(('dp', 'fsdp')), may hold values from 0 to 95, as said below
- attn_gain: bfloat16 [2048], P(('dp', 'fsdp')), may hold values from 0.25 to 1.75
- query_weight: bfloat16 [2048, 2048], P(('dp', 'fsdp')), may hold values from -0.125 to 0.125
- key_weight: bfloat16 [2048, 256], P(('dp', 'fsdp')), may hold values from -0.125 to 0.125
- value_weight: bfloat16 [2048, 256], P(('dp', 'fsdp')), may hold values from -0.125 to 0.125
- output_weight: bfloat16 [2048, 2048], P(('dp', 'fsdp')), may hold values from -1 to 1
- mlp_gain: bfloat16 [2048], P(('dp', 'fsdp')), may hold values from 0.25 to 1.75
- gate_weight: bfloat16 [2048, 5632], P(('dp', 'fsdp')), may hold values from -0.125 to 0.125
- up_weight: bfloat16 [2048, 5632], P(('dp', 'fsdp')), may hold values from -0.125 to 0.125
- down_weight: bfloat16 [5632, 2048], P(('dp', 'fsdp')), may hold values from -0.078125 to 0.078125
- cotangent: bfloat16 [4096, 2048], P(('dp', 'fsdp')), may hold values from -6 to 6
Outputs:
- outputs: bfloat16 [4096, 2048], P(('dp', 'fsdp'))
- input_grad: bfloat16 [4096, 2048], P(('dp', 'fsdp'))
- attn_gain_grad: float32 [2048], P(('dp', 'fsdp'))
- query_grad: float32 [2048, 2048], P(('dp', 'fsdp'))
- key_grad: float32 [2048, 256], P(('dp', 'fsdp'))
- value_grad: float32 [2048, 256], P(('dp', 'fsdp'))
- output_grad: float32 [2048, 2048], P(('dp', 'fsdp'))
- mlp_gain_grad: float32 [2048], P(('dp', 'fsdp'))
- gate_grad: float32 [2048, 5632], P(('dp', 'fsdp'))
- up_grad: float32 [2048, 5632], P(('dp', 'fsdp'))
- down_grad: float32 [5632, 2048], P(('dp', 'fsdp'))
The draws below stay inside these ranges and needn't reach their ends.
Inputs may be any that keep to these rules, and one draw needn't show every extreme that they name: `segment_ids`: the rows come in blocks of 128 (one device's rows), each holding one to three whole sequences; in block p the ids lie in 3 p to 3 p + 2 and never fall, some ids are skipped, and the block's last row has id 3 p + 2. Block 0 holds three sequences.
All inputs are finite; a program needn't handle non-finite values.
Results may differ from the reference program's by a relative error of at most 0.014.
Values may be sent and summed in bfloat16 or wider, within the bound.
A program may use at most 384 MiB of HBM per device.

```python
import jax
import jax.numpy as jnp
from jax import lax

D = 2048
FF = 5632
HEADS = 32
HEAD_DIM = 64
KV_HEADS = 4
TOK_DEV = 128
QW = 2048
KW = 256
TOKENS = 4096


def draw_segment_ids(key, part):
    pack_count = TOKENS // TOK_DEV
    first_key, second_key, third_key, fourth_key = jax.random.split(key, 4)
    cut_rows = jax.random.randint(first_key, (pack_count, 2), 1, TOK_DEV)
    chosen = jax.random.randint(second_key, (pack_count, 2), 0, 2)
    cut_rows = jnp.where(chosen == 1, cut_rows, 0)
    early_cut = jax.random.randint(third_key, (1,), 1, TOK_DEV // 2)
    late_cut = jax.random.randint(fourth_key, (1,), TOK_DEV // 2, TOK_DEV)
    first_block = jnp.concatenate([early_cut, late_cut])[None, :]
    block_index = jnp.arange(pack_count, dtype=jnp.int32)[:, None]
    cut_rows = jnp.where(block_index == 0, first_block, cut_rows)
    row_index = jnp.arange(TOK_DEV, dtype=jnp.int32)
    cuts_after = jnp.sum((cut_rows[:, :, None] > row_index[None, None, :]).astype(jnp.int32), axis=1)
    segment_rows = 3 * jnp.arange(pack_count, dtype=jnp.int32)[:, None] + 2 - cuts_after
    return segment_rows.reshape(pack_count * TOK_DEV).astype(jnp.int32)


def block_scale(own_key, extent, cuts, low, top_value):
    gain = 1.0
    for position, parts in cuts:
        steps = jax.random.uniform(jax.random.fold_in(jax.random.fold_in(own_key, 6), position), (parts,), jnp.float32, low / len(cuts), top_value / len(cuts))
        gain = gain * jnp.repeat(jnp.exp(steps), extent[position] // parts).reshape((-1,) + (1,) * (len(extent) - 1 - position))
    return gain


def centred(own_key, shape, deviation, limit, cuts=(), held_as=jnp.bfloat16):
    array = deviation * jax.random.normal(own_key, shape, jnp.float32)
    if cuts:
        array = array * block_scale(own_key, shape, cuts, -0.22, 0.18)
    return jnp.clip(array, -limit, limit).astype(held_as)


def setup_inputs(seed: int = 0) -> dict:
    key_of = jax.random.split(jax.random.key(seed), 13)
    inputs = centred(key_of[0], (TOKENS, D), 1.0, 6.0, ((0, 32),))
    segment_ids = draw_segment_ids(jax.random.fold_in(key_of[12], 71), 0)
    attn_gain = jnp.clip(1.0 + 0.15 * jax.random.normal(key_of[2], (D,), jnp.float32), 0.25, 1.75).astype(jnp.bfloat16)
    query_weight = centred(key_of[3], (D, QW), D ** -0.5, 0.125, ((0, 32),))
    key_weight = centred(key_of[4], (D, KW), D ** -0.5, 0.125, ((0, 32),))
    value_weight = centred(key_of[5], (D, KW), D ** -0.5, 0.125, ((0, 32),))
    output_weight = centred(key_of[6], (QW, D), (QW // 64) ** -0.5, 1.0, ((0, 32),))
    mlp_gain = jnp.clip(1.0 + 0.15 * jax.random.normal(key_of[7], (D,), jnp.float32), 0.25, 1.75).astype(jnp.bfloat16)
    gate_weight = centred(key_of[8], (D, FF), D ** -0.5, 0.125, ((0, 32),))
    up_weight = centred(key_of[9], (D, FF), D ** -0.5, 0.125, ((0, 32),))
    down_weight = centred(key_of[10], (FF, D), FF ** -0.5, 0.078125, ((0, 32),))
    cotangent = centred(key_of[11], (TOKENS, D), 1.0, 6.0, ((0, 32),))
    return {"inputs": inputs, "segment_ids": segment_ids, "attn_gain": attn_gain, "query_weight": query_weight, "key_weight": key_weight, "value_weight": value_weight, "output_weight": output_weight, "mlp_gain": mlp_gain, "gate_weight": gate_weight, "up_weight": up_weight, "down_weight": down_weight, "cotangent": cotangent}


EPSILON = 1e-05
HIGHEST = lax.Precision.HIGHEST

@jax.custom_vjp
def low(v):
    return lax.optimization_barrier(v.astype(jnp.bfloat16)).astype(jnp.float32)

@jax.custom_vjp
def low_back(v):
    return v

def low_keep(v):
    return (low(v), None)

def low_pass(kept, grad):
    return (grad,)

def back_keep(v):
    return (v, None)

def back_low(kept, grad):
    return (low(grad),)
low.defvjp(low_keep, low_pass)
low_back.defvjp(back_keep, back_low)

def product(left_side, right_side):
    return jnp.dot(left_side, right_side, precision=HIGHEST, preferred_element_type=jnp.float32)

def rms_normed(values):
    return values * lax.rsqrt(lax.optimization_barrier(jnp.mean(values * values, axis=1, keepdims=True)) + EPSILON)

def rotary_tables(segments):
    row_count = segments.shape[0]
    row_index = jnp.arange(row_count, dtype=jnp.int32)
    earlier = lax.optimization_barrier(jnp.sum((segments[None, :] < segments[:, None]).astype(jnp.int32), axis=1))
    places = (row_index - earlier).astype(jnp.float32)
    halfway = HEAD_DIM // 2
    frequency = 10000.0 ** (jnp.arange(halfway, dtype=jnp.float32) * (-2.0 / HEAD_DIM))
    angles = places[:, None] * frequency[None, :]
    cosine_table = jnp.concatenate([jnp.cos(angles), jnp.cos(angles)], axis=1)
    sine_table = jnp.concatenate([jnp.sin(angles), jnp.sin(angles)], axis=1)
    return (cosine_table[:, None, :], sine_table[:, None, :])

def rotate(values, cosine_table, sine_table):
    halfway = values.shape[-1] // 2
    turned = jnp.concatenate([-values[..., halfway:], values[..., :halfway]], axis=-1)
    return values * cosine_table + turned * sine_table

def attend(packed):
    query_rows, key_rows, value_rows, segments = packed
    cosine_table, sine_table = rotary_tables(segments)
    row_count = segments.shape[0]
    groups = HEADS // KV_HEADS
    query_rot = low(rotate(low_back(query_rows), cosine_table, sine_table))
    query_rot = query_rot.reshape(row_count, KV_HEADS, groups, HEAD_DIM)
    key_rot = low(rotate(low_back(key_rows), cosine_table, sine_table))
    value_low = low(low_back(value_rows))
    raw = jnp.einsum('qhgd,khd->hgqk', query_rot, key_rot, precision=HIGHEST)
    scores = low_back(raw) * HEAD_DIM ** (-0.5)
    row_index = jnp.arange(row_count, dtype=jnp.int32)
    allowed = (segments[:, None] == segments[None, :]) & (row_index[:, None] >= row_index[None, :])
    scores = jnp.where(allowed, scores, -1e+30)
    attn_probs = jax.nn.softmax(scores, axis=-1)
    mixed_rows = jnp.einsum('hgqk,khd->qhgd', low(attn_probs), value_low, precision=HIGHEST)
    return low(low_back(mixed_rows.reshape(row_count, HEADS * HEAD_DIM)))

def decoder_layer(inputs, attn_gain, query_weight, key_weight, value_weight, output_weight, mlp_gain, gate_weight, up_weight, down_weight, segment_ids):
    pack_count = TOKENS // TOK_DEV
    act_one = low(rms_normed(inputs) * attn_gain)
    query_rows = product(act_one, query_weight).reshape(pack_count, TOK_DEV, HEADS, HEAD_DIM)
    key_rows = product(act_one, key_weight).reshape(pack_count, TOK_DEV, KV_HEADS, HEAD_DIM)
    value_rows = product(act_one, value_weight).reshape(pack_count, TOK_DEV, KV_HEADS, HEAD_DIM)
    mixed_rows = lax.map(jax.checkpoint(attend), (query_rows, key_rows, value_rows, segment_ids.reshape(pack_count, TOK_DEV)))
    residual = inputs + low_back(product(mixed_rows.reshape(TOKENS, HEADS * HEAD_DIM), output_weight))
    act_two = low(rms_normed(residual) * mlp_gain)
    gate_value = low_back(product(act_two, gate_weight))
    up_value = low_back(product(act_two, up_weight))
    hidden = low(jax.nn.silu(gate_value) * up_value)
    return residual + product(hidden, down_weight)

def reference(inputs, segment_ids, attn_gain, query_weight, key_weight, value_weight, output_weight, mlp_gain, gate_weight, up_weight, down_weight, cotangent):
    floats = [weight.astype(jnp.float32) for weight in (inputs, attn_gain, query_weight, key_weight, value_weight, output_weight, mlp_gain, gate_weight, up_weight, down_weight)]

    def forward(*params):
        return decoder_layer(*params, segment_ids)
    outputs, pullback = jax.vjp(forward, *floats)
    gradients = pullback(cotangent.astype(jnp.float32))
    return (outputs.astype(jnp.bfloat16), gradients[0].astype(jnp.bfloat16), gradients[1], gradients[2], gradients[3], gradients[4], gradients[5], gradients[6], gradients[7], gradients[8], gradients[9])
```

```python
import jax
import jax.numpy as jnp
from jax import lax
from jax.sharding import PartitionSpec as P

HEADS = 32
HEAD_DIM = 64
KV_HEADS = 4
EPSILON = 1e-05
ALL = ("dp", "fsdp")
BF = jnp.bfloat16
F32 = jnp.float32


def matmul(left_side, right_side):
    return jnp.dot(left_side, right_side, preferred_element_type=F32)


def outer_sum(left_side, right_side):
    return lax.dot_general(
        left_side, right_side, (((0,), (0,)), ((), ())), preferred_element_type=F32
    )


def times_trans(left_side, right_side):
    return lax.dot_general(
        left_side, right_side, (((1,), (1,)), ((), ())), preferred_element_type=F32
    )


def rotary_tables(segments):
    row_count = segments.shape[0]
    row_index = jnp.arange(row_count, dtype=jnp.int32)
    earlier = jnp.sum((segments[None, :] < segments[:, None]).astype(jnp.int32), axis=1)
    places = (row_index - earlier).astype(F32)
    halfway = HEAD_DIM // 2
    frequency = 10000.0 ** (jnp.arange(halfway, dtype=F32) * (-2.0 / HEAD_DIM))
    angles = places[:, None] * frequency[None, :]
    cosine_table = jnp.concatenate([jnp.cos(angles), jnp.cos(angles)], axis=1)
    sine_table = jnp.concatenate([jnp.sin(angles), jnp.sin(angles)], axis=1)
    return (cosine_table[:, None, :], sine_table[:, None, :])


def rotate(values, cosine_table, sine_table):
    halfway = values.shape[-1] // 2
    turned = jnp.concatenate([-values[..., halfway:], values[..., :halfway]], axis=-1)
    return values * cosine_table + turned * sine_table


def rotate_back(upstream, cosine_table, sine_table):
    halfway = upstream.shape[-1] // 2
    scaled = upstream * sine_table
    turned = jnp.concatenate([scaled[..., halfway:], -scaled[..., :halfway]], axis=-1)
    return upstream * cosine_table + turned


def norm_back(upstream, normed, inverse, gain_vec):
    scaled = upstream * gain_vec
    return inverse * (scaled - normed * jnp.mean(scaled * normed, axis=1, keepdims=True))


def gather(value, axes):
    return lax.all_gather(value, axes, axis=0, tiled=True)


def scatter_sum(value, axes):
    return lax.psum_scatter(value, axes, scatter_dimension=0, tiled=True)


def swap(value):
    return lax.all_to_all(value, "fsdp", 0, 0, tiled=True)


def split_pair(vector):
    high = vector.astype(BF)
    low = (vector - high.astype(F32)).astype(BF)
    return high, low


def local(
    dp_size,
    fs_size,
    inputs,
    segment_ids,
    attn_gain,
    query_weight,
    key_weight,
    value_weight,
    output_weight,
    mlp_gain,
    gate_weight,
    up_weight,
    down_weight,
    cotangent,
):
    row_count = inputs.shape[0]
    weight_rows, ff_width = gate_weight.shape
    unit = down_weight.shape[0]
    share = dp_size * unit
    groups = HEADS // KV_HEADS
    query_width = HEADS * HEAD_DIM
    key_width = KV_HEADS * HEAD_DIM
    qkv_width = query_width + 2 * key_width
    score_scale = HEAD_DIM ** (-0.5)

    gains = jnp.concatenate(
        [attn_gain[:, None], mlp_gain[:, None], jnp.zeros((weight_rows, 126), BF)], axis=1
    )
    qkv_full = gather(
        jnp.concatenate([query_weight, key_weight, value_weight, gains], axis=1), ALL
    )
    gain_one = qkv_full[:, qkv_width].astype(F32)
    gain_two = qkv_full[:, qkv_width + 1].astype(F32)
    qkv_full = qkv_full[:, :qkv_width]
    output_full = gather(output_weight, ALL)

    def by_share(weight):
        return weight.reshape(weight_rows, dp_size, fs_size, unit).transpose(2, 0, 1, 3)

    pair = jnp.concatenate(
        [
            by_share(gate_weight).reshape(fs_size, weight_rows, share),
            by_share(up_weight).reshape(fs_size, weight_rows, share),
        ],
        axis=2,
    )
    pair = swap(pair.reshape(fs_size * weight_rows, 2 * share))
    pair_full = gather(pair, "dp")
    down_full = gather(down_weight, "dp")
    cot_full = gather(cotangent, "fsdp")

    source = inputs.astype(F32)
    inverse_one = lax.rsqrt(jnp.mean(source * source, axis=1, keepdims=True) + EPSILON)
    normed_one = source * inverse_one
    act_one = (normed_one * gain_one).astype(BF)
    qkv_rows = matmul(act_one, qkv_full)
    query_rows = qkv_rows[:, :query_width].reshape(row_count, HEADS, HEAD_DIM)
    key_rows = qkv_rows[:, query_width : query_width + key_width]
    key_rows = key_rows.reshape(row_count, KV_HEADS, HEAD_DIM)
    value_low = qkv_rows[:, query_width + key_width :].astype(BF)
    value_low = value_low.reshape(row_count, KV_HEADS, HEAD_DIM)
    cosine_table, sine_table = rotary_tables(segment_ids)
    query_rot = rotate(query_rows, cosine_table, sine_table).astype(BF)
    query_rot = query_rot.reshape(row_count, KV_HEADS, groups, HEAD_DIM)
    key_rot = rotate(key_rows, cosine_table, sine_table).astype(BF)
    row_index = jnp.arange(row_count, dtype=jnp.int32)
    allowed = (segment_ids[:, None] == segment_ids[None, :]) & (
        row_index[:, None] >= row_index[None, :]
    )
    raw = jnp.einsum("qhgd,khd->hgqk", query_rot, key_rot, preferred_element_type=F32)
    scores = jnp.where(allowed, raw * score_scale, -1e30)
    row_max = jnp.max(scores, axis=-1, keepdims=True)
    log_total = row_max + jnp.log(jnp.sum(jnp.exp(scores - row_max), axis=-1, keepdims=True))
    attn_probs = jnp.exp(scores - log_total)
    probs_low = attn_probs.astype(BF)
    mixed_low = jnp.einsum("hgqk,khd->qhgd", probs_low, value_low, preferred_element_type=F32)
    mixed_low = mixed_low.reshape(row_count, query_width).astype(BF)
    residual = source + matmul(mixed_low, output_full)
    inverse_two = lax.rsqrt(jnp.mean(residual * residual, axis=1, keepdims=True) + EPSILON)
    normed_two = residual * inverse_two
    act_two = (normed_two * gain_two).astype(BF)

    act_full = gather(act_two, "fsdp")
    both = matmul(act_full, pair_full)
    gate_value, up_value = both[:, :share], both[:, share:]
    sigmoid_gate = jax.nn.sigmoid(gate_value)
    hidden_low = (gate_value * sigmoid_gate * up_value).astype(BF)
    grad_hidden = times_trans(cot_full, down_full)
    grad_gate = (
        grad_hidden * up_value * sigmoid_gate * (1.0 + gate_value * (1.0 - sigmoid_gate))
    ).astype(BF)
    grad_up = (grad_hidden * gate_value * sigmoid_gate).astype(BF)
    grad_both = jnp.concatenate([grad_gate, grad_up], axis=1)
    grad_act_two = scatter_sum(times_trans(grad_both, pair_full).astype(BF), "fsdp").astype(F32)
    mlp_out = scatter_sum(matmul(hidden_low, down_full).astype(BF), "fsdp")
    outputs = (residual + mlp_out.astype(F32)).astype(BF)
    down_grad = scatter_sum(outer_sum(hidden_low, cot_full).astype(BF), "dp").astype(F32)
    pair_grad = scatter_sum(outer_sum(act_full, grad_both).astype(BF), "dp")
    pair_grad = swap(pair_grad).reshape(fs_size, weight_rows, 2, dp_size, unit)
    pair_grad = pair_grad.transpose(2, 1, 3, 0, 4).reshape(2, weight_rows, ff_width)
    gate_grad = pair_grad[0].astype(F32)
    up_grad = pair_grad[1].astype(F32)

    mlp_gain_grad = jnp.sum(normed_two * grad_act_two, axis=0)
    grad_residual = cotangent.astype(F32) + norm_back(
        grad_act_two, normed_two, inverse_two, gain_two
    )
    grad_attn = grad_residual.astype(BF)
    output_grad = scatter_sum(outer_sum(mixed_low, grad_attn).astype(BF), ALL).astype(F32)
    grad_mixed = times_trans(grad_attn, output_full).astype(BF)
    grad_mixed = grad_mixed.reshape(row_count, KV_HEADS, groups, HEAD_DIM)
    grad_probs = jnp.einsum("qhgd,khd->hgqk", grad_mixed, value_low, preferred_element_type=F32)
    grad_value = jnp.einsum("hgqk,qhgd->khd", probs_low, grad_mixed, preferred_element_type=F32)
    grad_value = grad_value.astype(BF).reshape(row_count, key_width)
    grad_raw = (
        score_scale
        * attn_probs
        * (grad_probs - jnp.sum(attn_probs * grad_probs, axis=-1, keepdims=True))
    )
    grad_raw = grad_raw.astype(BF)
    grad_qrot = jnp.einsum("hgqk,khd->qhgd", grad_raw, key_rot, preferred_element_type=F32)
    grad_qrot = grad_qrot.reshape(row_count, HEADS, HEAD_DIM)
    grad_krot = jnp.einsum("hgqk,qhgd->khd", grad_raw, query_rot, preferred_element_type=F32)
    grad_query = rotate_back(grad_qrot, cosine_table, sine_table).astype(BF)
    grad_key = rotate_back(grad_krot, cosine_table, sine_table).astype(BF)
    grad_qkv = jnp.concatenate(
        [
            grad_query.reshape(row_count, query_width),
            grad_key.reshape(row_count, key_width),
            grad_value,
        ],
        axis=1,
    )
    grad_act_one = times_trans(grad_qkv, qkv_full)
    attn_gain_grad = jnp.sum(normed_one * grad_act_one, axis=0)
    input_grad = (
        grad_residual + norm_back(grad_act_one, normed_one, inverse_one, gain_one)
    ).astype(BF)
    pairs = jnp.stack(split_pair(attn_gain_grad) + split_pair(mlp_gain_grad), axis=1)
    pairs = jnp.pad(pairs, ((0, 0), (0, 124)))
    qkv_grad = scatter_sum(
        jnp.concatenate([outer_sum(act_one, grad_qkv).astype(BF), pairs], axis=1), ALL
    ).astype(F32)
    return (
        outputs,
        input_grad,
        qkv_grad[:, qkv_width] + qkv_grad[:, qkv_width + 1],
        qkv_grad[:, :query_width],
        qkv_grad[:, query_width : query_width + key_width],
        qkv_grad[:, query_width + key_width : qkv_width],
        output_grad,
        qkv_grad[:, qkv_width + 2] + qkv_grad[:, qkv_width + 3],
        gate_grad,
        up_grad,
        down_grad,
    )


def solution(mesh):
    dp_size, fs_size = mesh.shape["dp"], mesh.shape["fsdp"]
    row = P(ALL, None)
    flat = P(ALL)

    def step(*args):
        return local(dp_size, fs_size, *args)

    return jax.shard_map(
        step,
        mesh=mesh,
        in_specs=(row, flat, flat, row, row, row, row, flat, row, row, row, row),
        out_specs=(row, row, flat, row, row, row, row, flat, row, row, row),
        check_vma=False,
    )
```

```python
import functools

import jax
import jax.numpy as jnp
from jax import lax
from jax.experimental import pallas as pl
from jax.experimental.pallas import tpu as pltpu
from jax.sharding import PartitionSpec as P

HEADS = 32
HEAD_DIM = 64
KV_HEADS = 4
EPSILON = 1e-05
ALL = ("dp", "fsdp")
BF = jnp.bfloat16
F32 = jnp.float32
MESH = pl.DeviceIdType.MESH


def matmul(left_side, right_side):
    return jnp.dot(left_side, right_side, preferred_element_type=F32)


def outer_sum(left_side, right_side):
    return lax.dot_general(
        left_side, right_side, (((0,), (0,)), ((), ())), preferred_element_type=F32
    )


def times_trans(left_side, right_side):
    return lax.dot_general(
        left_side, right_side, (((1,), (1,)), ((), ())), preferred_element_type=F32
    )


def rotary_tables(segments):
    row_count = segments.shape[0]
    row_index = jnp.arange(row_count, dtype=jnp.int32)
    earlier = jnp.sum((segments[None, :] < segments[:, None]).astype(jnp.int32), axis=1)
    places = (row_index - earlier).astype(F32)
    halfway = HEAD_DIM // 2
    frequency = 10000.0 ** (jnp.arange(halfway, dtype=F32) * (-2.0 / HEAD_DIM))
    angles = places[:, None] * frequency[None, :]
    cosine_table = jnp.concatenate([jnp.cos(angles), jnp.cos(angles)], axis=1)
    sine_table = jnp.concatenate([jnp.sin(angles), jnp.sin(angles)], axis=1)
    return (cosine_table[:, None, :], sine_table[:, None, :])


def rotate(values, cosine_table, sine_table):
    halfway = values.shape[-1] // 2
    turned = jnp.concatenate([-values[..., halfway:], values[..., :halfway]], axis=-1)
    return values * cosine_table + turned * sine_table


def rotate_back(upstream, cosine_table, sine_table):
    halfway = upstream.shape[-1] // 2
    scaled = upstream * sine_table
    turned = jnp.concatenate([scaled[..., halfway:], -scaled[..., :halfway]], axis=-1)
    return upstream * cosine_table + turned


def norm_back(upstream, normed, inverse, gain_vec):
    scaled = upstream * gain_vec
    return inverse * (scaled - normed * jnp.mean(scaled * normed, axis=1, keepdims=True))


def gather(value, axes):
    return lax.all_gather(value, axes, axis=0, tiled=True)


def scatter_sum(value, axes):
    return lax.psum_scatter(value, axes, scatter_dimension=0, tiled=True)


def place():
    d, f = lax.axis_index("dp"), lax.axis_index("fsdp")
    return d, f // 2, f % 2


def device(d, z, c):
    return {"dp": d, "fsdp": 2 * z + c}


def remote(src, dst, sems, index, target):
    return pltpu.make_async_remote_copy(
        src_ref=src,
        dst_ref=dst,
        send_sem=sems.at[0, index],
        recv_sem=sems.at[1, index],
        device_id=target,
        device_id_type=MESH,
    )


def loop(low, high, body):
    def step(index, carry):
        body(index)
        return carry

    lax.fori_loop(low, high, step, 0)


def greet(sizes, same_core=False, along_dp=False, along_fsdp=False, partner=False):
    dp_size, z_size = sizes
    d, z, c = place()
    barrier = pltpu.get_barrier_semaphore()

    def signal(target):
        pl.semaphore_signal(barrier, inc=1, device_id=target, device_id_type=MESH)

    count = 0
    if same_core:

        def to_chip(p):
            signal(device((d + p // z_size) % dp_size, (z + p % z_size) % z_size, c))

        loop(1, dp_size * z_size, to_chip)
        count += dp_size * z_size - 1
    if along_dp:
        loop(1, dp_size, lambda p: signal(device((d + p) % dp_size, z, c)))
        count += dp_size - 1
    if along_fsdp:
        f_size = 2 * z_size

        def to_line(p):
            signal({"dp": d, "fsdp": (2 * z + c + p) % f_size})

        loop(1, f_size, to_line)
        count += f_size - 1
    if partner:
        signal(device(d, z, 1 - c))
        count += 1
    pl.semaphore_wait(barrier, count)


def call(kernel, sizes, number, micros, outs, scratch, spaces, *args):
    return pl.pallas_call(
        functools.partial(kernel, sizes),
        out_shape=tuple(jax.ShapeDtypeStruct(shape, dtype) for shape, dtype in outs),
        in_specs=[pl.BlockSpec(memory_space=space) for space in spaces],
        out_specs=tuple(pl.BlockSpec(memory_space=pltpu.HBM) for _ in outs),
        scratch_shapes=scratch,
        compiler_params=pltpu.CompilerParams(collective_id=number, has_side_effects=True),
        cost_estimate=pl.CostEstimate(
            flops=int(micros * 1e9), bytes_accessed=0, transcendentals=0
        ),
        name=kernel.__name__,
    )(*args)


def dma(*shape):
    return pltpu.SemaphoreType.DMA(shape)


def start_kernel(sizes, x, seg, gain, wide, out, xs, segs, gains, wides, outs, *sems):
    x_sem, seg_sem, gain_sem, wide_sem, out_sem, gain_fwd, wide_fwd, out_fwd, own_sem = sems
    dp_size, z_size = sizes
    chips = dp_size * z_size
    d, z, c = place()
    f = 2 * z + c
    greet(sizes, same_core=True, partner=True)
    other = device(d, z, 1 - c)

    def out_copy(p):
        return remote(out, outs.at[f], out_sem, p, device(d, (z + p) % z_size, c))

    def wide_copy(p):
        to_d, to_z = (d + p // z_size) % dp_size, (z + p % z_size) % z_size
        return remote(wide.at[to_d], wides.at[d, f], wide_sem, p, device(to_d, to_z, c))

    def gain_copy(p):
        to_d, to_z = (d + p // z_size) % dp_size, (z + p % z_size) % z_size
        return remote(gain, gains.at[d, f], gain_sem, p, device(to_d, to_z, c))

    def x_copy(p):
        return remote(x, xs.at[d], x_sem, p, device((d + p) % dp_size, z, c))

    def seg_copy(p):
        return remote(seg, segs.at[d], seg_sem, p, device((d + p) % dp_size, z, c))

    def out_pass(p):
        slot = 2 * ((z - p + z_size) % z_size) + c
        return remote(outs.at[slot], outs.at[slot], out_fwd, p, other)

    def from_chip(p):
        return (d - p // z_size + dp_size) % dp_size, 2 * ((z - p % z_size + z_size) % z_size) + c

    def wide_pass(p):
        slot = from_chip(p)
        return remote(wides.at[slot], wides.at[slot], wide_fwd, p, other)

    def gain_pass(p):
        slot = from_chip(p)
        return remote(gains.at[slot], gains.at[slot], gain_fwd, p, other)

    loop(1, chips, lambda p: gain_copy(p).start())
    loop(1, dp_size, lambda p: seg_copy(p).start())
    loop(1, z_size, lambda p: out_copy(p).start())
    loop(1, chips, lambda p: wide_copy(p).start())
    loop(1, dp_size, lambda p: x_copy(p).start())
    own = [
        pltpu.make_async_copy(x, xs.at[d], own_sem.at[0]),
        pltpu.make_async_copy(seg, segs.at[d], own_sem.at[1]),
        pltpu.make_async_copy(gain, gains.at[d, f], own_sem.at[2]),
        pltpu.make_async_copy(wide.at[d], wides.at[d, f], own_sem.at[3]),
        pltpu.make_async_copy(out, outs.at[f], own_sem.at[4]),
    ]
    for copy in own:
        copy.start()
    passed = [
        remote(gain, gains.at[d, f], gain_fwd, 0, other),
        remote(wide.at[d], wides.at[d, f], wide_fwd, 0, other),
        remote(out, outs.at[f], out_fwd, 0, other),
    ]
    for copy in passed:
        copy.start()

    def pass_gain(p):
        gain_copy(p).wait_recv()
        gain_pass(p).start()

    def pass_out(p):
        out_copy(p).wait_recv()
        out_pass(p).start()

    def pass_wide(p):
        wide_copy(p).wait_recv()
        wide_pass(p).start()

    loop(1, chips, pass_gain)
    loop(1, z_size, pass_out)
    loop(1, chips, pass_wide)
    loop(1, dp_size, lambda p: seg_copy(p).wait())
    loop(1, dp_size, lambda p: x_copy(p).wait())
    for copy in own:
        copy.wait()
    for copy in passed:
        copy.wait()
    loop(1, chips, lambda p: gain_pass(p).wait())
    loop(1, z_size, lambda p: out_pass(p).wait())
    loop(1, chips, lambda p: wide_pass(p).wait())
    loop(1, chips, lambda p: gain_copy(p).wait_send())
    loop(1, z_size, lambda p: out_copy(p).wait_send())
    loop(1, chips, lambda p: wide_copy(p).wait_send())


def cross_kernel(spread, sizes, rows, pair, rows_out, pair_out, *scratch):
    rows_own, pair_own, rows_sem, pair_sem, own_sem = scratch
    dp_size, z_size = sizes
    f_size = 2 * z_size
    d, z, c = place()
    f = 2 * z + c
    greet(sizes, along_dp=True, along_fsdp=True)

    def rows_copy(p):
        to = (d + p) % dp_size
        piece = rows if spread else rows.at[to]
        return remote(piece, rows_out.at[d], rows_sem, p, device(to, z, c))

    def pair_copy(p):
        to = (f + p) % f_size
        return remote(
            pair.at[to], pair_out.at[f], pair_sem, p, {"dp": d, "fsdp": to}
        )

    loop(1, dp_size, lambda p: rows_copy(p).start())
    loop(1, f_size, lambda p: pair_copy(p).start())
    first = pltpu.make_async_copy(rows if spread else rows.at[d], rows_own, own_sem.at[0])
    second = pltpu.make_async_copy(pair.at[f], pair_own, own_sem.at[1])
    first.start()
    second.start()
    first.wait()
    second.wait()
    third = pltpu.make_async_copy(rows_own, rows_out.at[d], own_sem.at[2])
    fourth = pltpu.make_async_copy(pair_own, pair_out.at[f], own_sem.at[3])
    third.start()
    fourth.start()
    third.wait()
    fourth.wait()
    loop(1, dp_size, lambda p: rows_copy(p).wait())
    loop(1, f_size, lambda p: pair_copy(p).wait())


def scatter_cross(sizes, *refs):
    cross_kernel(False, sizes, *refs)


def gather_cross(sizes, *refs):
    cross_kernel(True, sizes, *refs)


def gather_line(sizes, rows, rows_out, rows_sem, pass_sem, own_sem):
    dp_size, z_size = sizes
    d, z, c = place()
    f = 2 * z + c
    greet((1, z_size), along_fsdp=True)
    other = device(d, z, 1 - c)

    def rows_copy(p):
        return remote(rows, rows_out.at[f], rows_sem, p, device(d, (z + p) % z_size, c))

    def rows_pass(p):
        slot = 2 * ((z - p + z_size) % z_size) + c
        return remote(rows_out.at[slot], rows_out.at[slot], pass_sem, p, other)

    loop(1, z_size, lambda p: rows_copy(p).start())
    own = pltpu.make_async_copy(rows, rows_out.at[f], own_sem.at[0])
    own.start()
    passed = remote(rows, rows_out.at[f], pass_sem, 0, other)
    passed.start()

    def pass_on(p):
        rows_copy(p).wait_recv()
        rows_pass(p).start()

    loop(1, z_size, pass_on)
    own.wait()
    passed.wait()
    loop(1, z_size, lambda p: rows_pass(p).wait())
    loop(1, z_size, lambda p: rows_copy(p).wait_send())


def scatter_line(sizes, part, part_out, mine, theirs, part_sem, swap_sem, load_sem, own_sem):
    dp_size, z_size = sizes
    d, z, c = place()
    greet((1, z_size), along_fsdp=True)
    other = device(d, z, 1 - c)

    def swap_copy(p):
        to = (z + p) % z_size
        return remote(part.at[to, 1 - c], theirs.at[to], swap_sem, p, other)

    def load(p):
        to = (z + p) % z_size
        return pltpu.make_async_copy(part.at[to, c], mine.at[to], load_sem.at[p])

    def part_copy(p):
        to = (z + p) % z_size
        return remote(mine.at[to], part_out.at[z], part_sem, p, device(d, to, c))

    def begin(p):
        swap_copy(p).start()
        load(p).start()

    def add(p):
        to = (z + p) % z_size
        swap_copy(p).wait()
        load(p).wait()
        mine[to] = (mine[to].astype(F32) + theirs[to].astype(F32)).astype(BF)

    def send(p):
        add(p)
        part_copy(p).start()

    loop(1, z_size, begin)
    begin(0)
    loop(1, z_size, send)
    add(0)
    own = pltpu.make_async_copy(mine.at[z], part_out.at[z], own_sem.at[0])
    own.start()
    own.wait()
    loop(1, z_size, lambda p: part_copy(p).wait())


def end_kernel(sizes, rows, wide, out, gain, rows_out, wide_out, out_out, gain_out, *scratch):
    rows_own, wide_mine, wide_theirs, out_mine, out_theirs, gain_mine, gain_theirs = scratch[:7]
    rows_sem, wide_sem, out_sem, gain_sem, swap_sem, own_sem = scratch[7:]
    dp_size, z_size = sizes
    chips = dp_size * z_size
    d, z, c = place()
    greet(sizes, same_core=True, partner=True)
    other = device(d, z, 1 - c)
    swaps = [
        remote(out.at[:, 1 - c], out_theirs, swap_sem, 0, other),
        remote(wide.at[:, :, 1 - c], wide_theirs, swap_sem, 1, other),
        remote(gain.at[:, :, 1 - c], gain_theirs, swap_sem, 2, other),
    ]
    loads = [
        pltpu.make_async_copy(out.at[:, c], out_mine, own_sem.at[0]),
        pltpu.make_async_copy(wide.at[:, :, c], wide_mine, own_sem.at[1]),
        pltpu.make_async_copy(gain.at[:, :, c], gain_mine, own_sem.at[2]),
    ]
    for copy in swaps + loads:
        copy.start()

    def rows_copy(p):
        to = (d + p) % dp_size
        return remote(rows.at[to], rows_out.at[d], rows_sem, p, device(to, z, c))

    loop(1, dp_size, lambda p: rows_copy(p).start())
    rows_in = pltpu.make_async_copy(rows.at[d], rows_own, own_sem.at[3])
    rows_in.start()

    def out_copy(p):
        to = (z + p) % z_size
        return remote(out_mine.at[to], out_out.at[z], out_sem, p, device(d, to, c))

    def target(p):
        return (d + p // z_size) % dp_size, (z + p % z_size) % z_size

    def wide_copy(p):
        to_d, to_z = target(p)
        return remote(
            wide_mine.at[to_d, to_z], wide_out.at[d, z], wide_sem, p, device(to_d, to_z, c)
        )

    def gain_copy(p):
        to_d, to_z = target(p)
        return remote(
            gain_mine.at[to_d, to_z], gain_out.at[d, z], gain_sem, p, device(to_d, to_z, c)
        )

    def add_out(p):
        to = (z + p) % z_size
        out_mine[to] = (out_mine[to].astype(F32) + out_theirs[to].astype(F32)).astype(BF)

    def add_wide(p):
        to_d, to_z = target(p)
        total = wide_mine[to_d, to_z].astype(F32) + wide_theirs[to_d, to_z].astype(F32)
        wide_mine[to_d, to_z] = total.astype(BF)
        gain_mine[to_d, to_z] = gain_mine[to_d, to_z] + gain_theirs[to_d, to_z]

    swaps[0].wait()
    loads[0].wait()

    def send_out(p):
        add_out(p)
        out_copy(p).start()

    loop(1, z_size, send_out)
    add_out(0)
    for copy in swaps[1:] + loads[1:]:
        copy.wait()

    def send_wide(p):
        add_wide(p)
        wide_copy(p).start()
        gain_copy(p).start()

    loop(1, chips, send_wide)
    add_wide(0)
    rows_in.wait()
    own = [
        pltpu.make_async_copy(rows_own, rows_out.at[d], own_sem.at[4]),
        pltpu.make_async_copy(out_mine.at[z], out_out.at[z], own_sem.at[5]),
        pltpu.make_async_copy(wide_mine.at[d, z], wide_out.at[d, z], own_sem.at[6]),
        pltpu.make_async_copy(gain_mine.at[d, z], gain_out.at[d, z], own_sem.at[7]),
    ]
    for copy in own:
        copy.start()
    for copy in own:
        copy.wait()
    loop(1, dp_size, lambda p: rows_copy(p).wait())
    loop(1, z_size, lambda p: out_copy(p).wait())
    loop(1, chips, lambda p: wide_copy(p).wait())
    loop(1, chips, lambda p: gain_copy(p).wait())


def local(
    dp_size,
    fs_size,
    inputs,
    segment_ids,
    attn_gain,
    query_weight,
    key_weight,
    value_weight,
    output_weight,
    mlp_gain,
    gate_weight,
    up_weight,
    down_weight,
    cotangent,
):
    z_size = fs_size // 2
    sizes = (dp_size, z_size)
    row_count, width = inputs.shape
    weight_rows, ff_width = gate_weight.shape
    unit = down_weight.shape[0]
    share = dp_size * unit
    heads = HEADS // dp_size
    query_width = heads * HEAD_DIM
    wide_width = query_width + 2 * HEAD_DIM
    score_scale = HEAD_DIM ** (-0.5)
    vmem, hbm = pltpu.VMEM, pltpu.HBM

    def by_share(weight):
        weight = weight.reshape(weight_rows, dp_size, fs_size, unit).transpose(2, 0, 1, 3)
        return weight.reshape(fs_size, weight_rows, share)

    pair = jnp.concatenate([by_share(gate_weight), by_share(up_weight)], axis=2)
    down_full = gather(down_weight, "dp")
    cot_full = gather(cotangent, "fsdp")

    def by_head(weight):
        return weight.reshape(weight_rows, dp_size, -1).transpose(1, 0, 2)

    wide = jnp.concatenate(
        [by_head(query_weight), by_head(key_weight), by_head(value_weight)], axis=2
    )
    gain = jnp.concatenate([attn_gain, mlp_gain, jnp.zeros((128 - 2 * weight_rows,), BF)])
    gain = jnp.broadcast_to(gain[None, :], (16, 128))
    seg = jnp.broadcast_to(segment_ids[None, :], (8, row_count))
    chips = dp_size * z_size
    xs, segs, gains, wides, out_full = call(
        start_kernel,
        sizes,
        0,
        60,
        [
            ((dp_size, row_count, width), BF),
            ((dp_size, 8, row_count), jnp.int32),
            ((dp_size, fs_size, 16, 128), BF),
            ((dp_size, fs_size, weight_rows, wide_width), BF),
            ((fs_size, weight_rows, width), BF),
        ],
        [
            dma(2, dp_size),
            dma(2, dp_size),
            dma(2, chips),
            dma(2, chips),
            dma(2, z_size),
            dma(2, chips),
            dma(2, chips),
            dma(2, z_size),
            dma(5),
        ],
        [vmem] * 5,
        inputs,
        seg,
        gain,
        wide,
        output_weight,
    )
    gains = gains[:, :, 0, :].astype(F32)
    gain_one = gains[:, :, :weight_rows].reshape(width)
    gain_two = gains[:, :, weight_rows : 2 * weight_rows].reshape(width)
    wides = wides.reshape(width, wide_width)
    out_full = out_full.reshape(query_width, width)

    sources = xs.reshape(dp_size * row_count, width).astype(F32)
    inverse_one = lax.rsqrt(jnp.mean(sources * sources, axis=1, keepdims=True) + EPSILON)
    normed_all = sources * inverse_one
    act_one = (normed_all * gain_one).astype(BF)
    wide_rows = matmul(act_one, wides)
    query_rows = wide_rows[:, :query_width].reshape(dp_size, row_count, heads, HEAD_DIM)
    key_rows = wide_rows[:, query_width : query_width + HEAD_DIM]
    key_rows = key_rows.reshape(dp_size, row_count, 1, HEAD_DIM)
    value_low = wide_rows[:, query_width + HEAD_DIM :].astype(BF)
    value_low = value_low.reshape(dp_size, row_count, HEAD_DIM)
    segs = segs[:, 0, :]
    cosine_table, sine_table = jax.vmap(rotary_tables)(segs)
    query_rot = rotate(query_rows, cosine_table, sine_table).astype(BF)
    key_rot = rotate(key_rows, cosine_table, sine_table).astype(BF)[:, :, 0, :]
    row_index = jnp.arange(row_count, dtype=jnp.int32)
    allowed = (segs[:, :, None] == segs[:, None, :]) & (
        row_index[:, None] >= row_index[None, :]
    )
    raw = jnp.einsum("bqhd,bkd->bhqk", query_rot, key_rot, preferred_element_type=F32)
    scores = jnp.where(allowed[:, None], raw * score_scale, -1e30)
    row_max = jnp.max(scores, axis=-1, keepdims=True)
    log_total = row_max + jnp.log(jnp.sum(jnp.exp(scores - row_max), axis=-1, keepdims=True))
    attn_probs = jnp.exp(scores - log_total)
    probs_low = attn_probs.astype(BF)
    mixed_low = jnp.einsum("bhqk,bkd->bqhd", probs_low, value_low, preferred_element_type=F32)
    mixed_low = mixed_low.reshape(dp_size * row_count, query_width).astype(BF)
    mixed_out = matmul(mixed_low, out_full).astype(BF).reshape(dp_size, row_count, width)

    pair_shape = (fs_size, weight_rows, 2 * share)
    rows_shape = (dp_size, row_count, width)
    cross_scratch = [
        pltpu.VMEM((row_count, width), BF),
        pltpu.VMEM(pair_shape[1:], BF),
        dma(2, dp_size),
        dma(2, fs_size),
        dma(4),
    ]
    mixed_parts, pair_rows = call(
        scatter_cross,
        sizes,
        1,
        36,
        [(rows_shape, BF), (pair_shape, BF)],
        cross_scratch,
        [hbm, hbm],
        mixed_out,
        pair,
    )
    pair_full = gather(pair_rows.reshape(fs_size * weight_rows, 2 * share), "dp")
    source = inputs.astype(F32)
    residual = source + jnp.sum(mixed_parts.astype(F32), axis=0)
    inverse_two = lax.rsqrt(jnp.mean(residual * residual, axis=1, keepdims=True) + EPSILON)
    normed_two = residual * inverse_two
    act_two = (normed_two * gain_two).astype(BF)
    (act_full,) = call(
        gather_line,
        sizes,
        2,
        50,
        [((fs_size, row_count, width), BF)],
        [dma(2, z_size), dma(2, z_size), dma(1)],
        [vmem],
        act_two,
    )
    act_full = act_full.reshape(fs_size * row_count, width)

    both = matmul(act_full, pair_full)
    gate_value, up_value = both[:, :share], both[:, share:]
    sigmoid_gate = jax.nn.sigmoid(gate_value)
    hidden_low = (gate_value * sigmoid_gate * up_value).astype(BF)
    grad_hidden = times_trans(cot_full, down_full)
    grad_gate = (
        grad_hidden * up_value * sigmoid_gate * (1.0 + gate_value * (1.0 - sigmoid_gate))
    ).astype(BF)
    grad_up = (grad_hidden * gate_value * sigmoid_gate).astype(BF)
    grad_both = jnp.concatenate([grad_gate, grad_up], axis=1)
    grad_part = times_trans(grad_both, pair_full).astype(BF)
    (grad_parts,) = call(
        scatter_line,
        sizes,
        3,
        50,
        [((z_size, row_count, width), BF)],
        [
            pltpu.VMEM((z_size, row_count, width), BF),
            pltpu.VMEM((z_size, row_count, width), BF),
            dma(2, z_size),
            dma(2, z_size),
            dma(z_size),
            dma(1),
        ],
        [hbm],
        grad_part.reshape(z_size, 2, row_count, width),
    )
    mlp_out = scatter_sum(matmul(hidden_low, down_full).astype(BF), "fsdp")
    outputs = (residual + mlp_out.astype(F32)).astype(BF)
    pair_grad = scatter_sum(outer_sum(act_full, grad_both).astype(BF), "dp")
    down_grad = scatter_sum(outer_sum(hidden_low, cot_full).astype(BF), "dp").astype(F32)

    grad_act_two = jnp.sum(grad_parts.astype(F32), axis=0)
    mlp_gain_grad = jnp.sum(normed_two * grad_act_two, axis=0)
    grad_residual = cotangent.astype(F32) + norm_back(
        grad_act_two, normed_two, inverse_two, gain_two
    )
    grad_attn, pair_back = call(
        gather_cross,
        sizes,
        4,
        36,
        [(rows_shape, BF), (pair_shape, BF)],
        cross_scratch,
        [hbm, hbm],
        grad_residual.astype(BF),
        pair_grad.reshape(pair_shape),
    )
    pair_back = pair_back.reshape(fs_size, weight_rows, 2, dp_size, unit)
    pair_back = pair_back.transpose(2, 1, 3, 0, 4).reshape(2, weight_rows, ff_width)
    gate_grad = pair_back[0].astype(F32)
    up_grad = pair_back[1].astype(F32)

    grad_attn = grad_attn.reshape(dp_size * row_count, width)
    output_grad = outer_sum(mixed_low, grad_attn).astype(BF)
    grad_mixed = times_trans(grad_attn, out_full).astype(BF)
    grad_mixed = grad_mixed.reshape(dp_size, row_count, heads, HEAD_DIM)
    grad_probs = jnp.einsum("bqhd,bkd->bhqk", grad_mixed, value_low, preferred_element_type=F32)
    grad_value = jnp.einsum("bhqk,bqhd->bkd", probs_low, grad_mixed, preferred_element_type=F32)
    grad_value = grad_value.astype(BF).reshape(dp_size * row_count, HEAD_DIM)
    grad_raw = (
        score_scale
        * attn_probs
        * (grad_probs - jnp.sum(attn_probs * grad_probs, axis=-1, keepdims=True))
    )
    grad_raw = grad_raw.astype(BF)
    grad_qrot = jnp.einsum("bhqk,bkd->bqhd", grad_raw, key_rot, preferred_element_type=F32)
    grad_krot = jnp.einsum("bhqk,bqhd->bkd", grad_raw, query_rot, preferred_element_type=F32)
    grad_query = rotate_back(grad_qrot, cosine_table, sine_table).astype(BF)
    grad_key = rotate_back(grad_krot[:, :, None, :], cosine_table, sine_table).astype(BF)
    grad_wide = jnp.concatenate(
        [
            grad_query.reshape(dp_size * row_count, query_width),
            grad_key.reshape(dp_size * row_count, HEAD_DIM),
            grad_value,
        ],
        axis=1,
    )
    grad_act = times_trans(grad_wide, wides)
    gain_grad = jnp.sum(normed_all * grad_act, axis=0)
    by_owner = (dp_size, fs_size, weight_rows)
    gain_grads = jnp.concatenate(
        [
            gain_grad.reshape(by_owner),
            mlp_gain_grad.reshape(by_owner),
            jnp.zeros((dp_size, fs_size, 128 - 2 * weight_rows), F32),
        ],
        axis=2,
    )
    gain_grads = jnp.broadcast_to(gain_grads[:, :, None, :], (dp_size, fs_size, 8, 128))
    wide_grad = outer_sum(act_one, grad_wide).astype(BF)
    wide_half = (dp_size, z_size, weight_rows, wide_width)
    out_half = (z_size, weight_rows, width)
    gain_half = (dp_size, z_size, 8, 128)
    grad_act_parts, wide_parts, out_parts, gain_parts = call(
        end_kernel,
        sizes,
        5,
        60,
        [(rows_shape, BF), (wide_half, BF), (out_half, BF), (gain_half, F32)],
        [
            pltpu.VMEM((row_count, width), BF),
            pltpu.VMEM(wide_half, BF),
            pltpu.VMEM(wide_half, BF),
            pltpu.VMEM(out_half, BF),
            pltpu.VMEM(out_half, BF),
            pltpu.VMEM(gain_half, F32),
            pltpu.VMEM(gain_half, F32),
            dma(2, dp_size),
            dma(2, chips),
            dma(2, z_size),
            dma(2, chips),
            dma(2, 3),
            dma(8),
        ],
        [hbm] * 4,
        grad_act.astype(BF).reshape(rows_shape),
        wide_grad.reshape(dp_size, z_size, 2, weight_rows, wide_width),
        output_grad.reshape(z_size, 2, weight_rows, width),
        gain_grads.reshape(dp_size, z_size, 2, 8, 128),
    )
    grad_act_one = jnp.sum(grad_act_parts.astype(F32), axis=0)
    own_inverse = lax.rsqrt(jnp.mean(source * source, axis=1, keepdims=True) + EPSILON)
    input_grad = (
        grad_residual + norm_back(grad_act_one, source * own_inverse, own_inverse, gain_one)
    ).astype(BF)
    gain_total = jnp.sum(gain_parts[:, :, 0, :], axis=(0, 1))
    wide_total = jnp.sum(wide_parts.astype(F32), axis=1)

    def from_heads(value):
        return value.transpose(1, 0, 2).reshape(weight_rows, -1)

    return (
        outputs,
        input_grad,
        gain_total[:weight_rows],
        from_heads(wide_total[:, :, :query_width]),
        from_heads(wide_total[:, :, query_width : query_width + HEAD_DIM]),
        from_heads(wide_total[:, :, query_width + HEAD_DIM :]),
        jnp.sum(out_parts.astype(F32), axis=0),
        gain_total[weight_rows : 2 * weight_rows],
        gate_grad,
        up_grad,
        down_grad,
    )


def solution(mesh):
    dp_size, fs_size = mesh.shape["dp"], mesh.shape["fsdp"]
    row = P(ALL, None)
    flat = P(ALL)

    def step(*args):
        return local(dp_size, fs_size, *args)

    return jax.shard_map(
        step,
        mesh=mesh,
        in_specs=(row, flat, flat, row, row, row, row, flat, row, row, row, row),
        out_specs=(row, row, flat, row, row, row, row, flat, row, row, row),
        check_vma=False,
    )
```

```python
import functools

import jax
import jax.numpy as jnp
from jax import lax
from jax.experimental import pallas as pl
from jax.experimental.pallas import tpu as pltpu
from jax.sharding import PartitionSpec as P

HEADS = 32
HEAD_DIM = 64
KV_HEADS = 4
EPSILON = 1e-05
ALL = ("dp", "fsdp")
BF = jnp.bfloat16
F32 = jnp.float32
MESH = pl.DeviceIdType.MESH


def matmul(left_side, right_side):
    return jnp.dot(left_side, right_side, preferred_element_type=F32)


def outer_sum(left_side, right_side):
    return lax.dot_general(
        left_side, right_side, (((0,), (0,)), ((), ())), preferred_element_type=F32
    )


def times_trans(left_side, right_side):
    return lax.dot_general(
        left_side, right_side, (((1,), (1,)), ((), ())), preferred_element_type=F32
    )


def rotary_tables(segments):
    row_count = segments.shape[0]
    row_index = jnp.arange(row_count, dtype=jnp.int32)
    earlier = jnp.sum((segments[None, :] < segments[:, None]).astype(jnp.int32), axis=1)
    places = (row_index - earlier).astype(F32)
    halfway = HEAD_DIM // 2
    frequency = 10000.0 ** (jnp.arange(halfway, dtype=F32) * (-2.0 / HEAD_DIM))
    angles = places[:, None] * frequency[None, :]
    cosine_table = jnp.concatenate([jnp.cos(angles), jnp.cos(angles)], axis=1)
    sine_table = jnp.concatenate([jnp.sin(angles), jnp.sin(angles)], axis=1)
    return (cosine_table[:, None, :], sine_table[:, None, :])


def rotate(values, cosine_table, sine_table):
    halfway = values.shape[-1] // 2
    turned = jnp.concatenate([-values[..., halfway:], values[..., :halfway]], axis=-1)
    return values * cosine_table + turned * sine_table


def rotate_back(upstream, cosine_table, sine_table):
    halfway = upstream.shape[-1] // 2
    scaled = upstream * sine_table
    turned = jnp.concatenate([scaled[..., halfway:], -scaled[..., :halfway]], axis=-1)
    return upstream * cosine_table + turned


def norm_back(upstream, normed, inverse, gain_vec):
    scaled = upstream * gain_vec
    return inverse * (scaled - normed * jnp.mean(scaled * normed, axis=1, keepdims=True))


def gather(value, axes):
    return lax.all_gather(value, axes, axis=0, tiled=True)


def scatter_sum(value, axes):
    return lax.psum_scatter(value, axes, scatter_dimension=0, tiled=True)


def place():
    d, f = lax.axis_index("dp"), lax.axis_index("fsdp")
    return d, f // 2, f % 2


def device(d, z, c):
    return {"dp": d, "fsdp": 2 * z + c}


def remote(src, dst, sems, index, target):
    return pltpu.make_async_remote_copy(
        src_ref=src,
        dst_ref=dst,
        send_sem=sems.at[0, index],
        recv_sem=sems.at[1, index],
        device_id=target,
        device_id_type=MESH,
    )


def hop(src, dst, sems, send, recv, target):
    return pltpu.make_async_remote_copy(
        src_ref=src,
        dst_ref=dst,
        send_sem=sems.at[0, send],
        recv_sem=sems.at[1, recv],
        device_id=target,
        device_id_type=MESH,
    )


def chain(z_size, shard, sems, first):
    d, z, c = place()

    def copy(s, to, send=None, src=None):
        src = shard(s) if src is None else src
        return hop(src, shard(s), sems, s if send is None else send, s, device(d, to, c))

    up, down = z < z_size - 1, z > 0

    def start():
        @pl.when(up)
        def _():
            copy(z, z + 1, src=first).start()

        @pl.when(down)
        def _():
            copy(z, z - 1, z_size, first).start()

    def go(arrived):
        def step(k):
            @pl.when(z - k >= 0)
            def _():
                copy(z - k, z).wait_recv()

                @pl.when(up)
                def _():
                    copy(z - k, z + 1).start()

                arrived(z - k)

            @pl.when(z + k < z_size)
            def _():
                copy(z + k, z).wait_recv()

                @pl.when(down)
                def _():
                    copy(z + k, z - 1).start()

                arrived(z + k)

        loop(1, z_size, step)

    def finish():
        @pl.when(up)
        def _():
            copy(z, z + 1, src=first).wait_send()

        @pl.when(down)
        def _():
            copy(z, z - 1, z_size, first).wait_send()

        def step(k):
            @pl.when((z - k >= 0) & up)
            def _():
                copy(z - k, z + 1).wait_send()

            @pl.when((z + k < z_size) & down)
            def _():
                copy(z + k, z - 1).wait_send()

        loop(1, z_size, step)

    return start, go, finish


def ring_place(q, size):
    q = (q + size) % size
    return q + (q // 2) * (1 - 2 * (q % 2)) if size == 4 else q


def loop(low, high, body):
    def step(index, carry):
        body(index)
        return carry

    lax.fori_loop(low, high, step, 0)


def greet(sizes, same_core=False, along_dp=False, along_fsdp=False, partner=False):
    dp_size, z_size = sizes
    d, z, c = place()
    barrier = pltpu.get_barrier_semaphore()

    def signal(target):
        pl.semaphore_signal(barrier, inc=1, device_id=target, device_id_type=MESH)

    count = 0
    if same_core:

        def to_chip(p):
            signal(device((d + p // z_size) % dp_size, (z + p % z_size) % z_size, c))

        loop(1, dp_size * z_size, to_chip)
        count += dp_size * z_size - 1
    if along_dp:
        loop(1, dp_size, lambda p: signal(device((d + p) % dp_size, z, c)))
        count += dp_size - 1
    if along_fsdp:
        f_size = 2 * z_size

        def to_line(p):
            signal({"dp": d, "fsdp": (2 * z + c + p) % f_size})

        loop(1, f_size, to_line)
        count += f_size - 1
    if partner:
        signal(device(d, z, 1 - c))
        count += 1
    pl.semaphore_wait(barrier, count)


def call(kernel, sizes, number, micros, outs, scratch, spaces, *args):
    return pl.pallas_call(
        functools.partial(kernel, sizes),
        out_shape=tuple(jax.ShapeDtypeStruct(shape, dtype) for shape, dtype in outs),
        in_specs=[pl.BlockSpec(memory_space=space) for space in spaces],
        out_specs=tuple(pl.BlockSpec(memory_space=pltpu.HBM) for _ in outs),
        scratch_shapes=scratch,
        compiler_params=pltpu.CompilerParams(collective_id=number, has_side_effects=True),
        cost_estimate=pl.CostEstimate(
            flops=int(micros * 1e9), bytes_accessed=0, transcendentals=0
        ),
        name=kernel.__name__,
    )(*args)


def dma(*shape):
    return pltpu.SemaphoreType.DMA(shape)


def start_kernel(sizes, x, seg, gain, wide, out, xs, segs, gains, wides, outs, *sems):
    x_sem, seg_sem, gain_sem, piece_sem, wide_sem, out_sem = sems[:6]
    gain_fwd, wide_fwd, out_fwd, own_sem = sems[6:]
    dp_size, z_size = sizes
    chips = dp_size * z_size
    d, z, c = place()
    f = 2 * z + c
    greet(sizes, same_core=True, partner=True)
    other = device(d, z, 1 - c)

    def piece_copy(p):
        to = (d + p) % dp_size
        return remote(wide.at[to], wides.at[d, f], piece_sem, p, device(to, z, c))

    def gain_copy(p):
        to_d, to_z = (d + p // z_size) % dp_size, (z + p % z_size) % z_size
        return remote(gain, gains.at[d, f], gain_sem, p, device(to_d, to_z, c))

    def x_copy(p):
        return remote(x, xs.at[d], x_sem, p, device((d + p) % dp_size, z, c))

    def seg_copy(p):
        return remote(seg, segs.at[d], seg_sem, p, device((d + p) % dp_size, z, c))

    def out_pass(s):
        slot = outs.at[2 * s + c]
        return remote(slot, slot, out_fwd, s, other)

    def wide_pass(s):
        slot = wides.at[:, 2 * s + c]
        return remote(slot, slot, wide_fwd, s, other)

    def gain_pass(p):
        from_d = (d - p // z_size + dp_size) % dp_size
        slot = gains.at[from_d, 2 * ((z - p % z_size + z_size) % z_size) + c]
        return remote(slot, slot, gain_fwd, p, other)

    out_start, out_go, out_finish = chain(z_size, lambda s: outs.at[2 * s + c], out_sem, out)
    wide_start, wide_go, wide_finish = chain(
        z_size, lambda s: wides.at[:, 2 * s + c], wide_sem, wides.at[:, f]
    )
    own = [
        pltpu.make_async_copy(wide.at[d], wides.at[d, f], own_sem.at[0]),
        pltpu.make_async_copy(x, xs.at[d], own_sem.at[1]),
        pltpu.make_async_copy(seg, segs.at[d], own_sem.at[2]),
        pltpu.make_async_copy(gain, gains.at[d, f], own_sem.at[3]),
        pltpu.make_async_copy(out, outs.at[f], own_sem.at[4]),
    ]
    loop(1, dp_size, lambda p: piece_copy(p).start())
    for copy in own:
        copy.start()
    out_start()
    loop(1, chips, lambda p: gain_copy(p).start())
    loop(1, dp_size, lambda p: seg_copy(p).start())
    loop(1, dp_size, lambda p: x_copy(p).start())
    passed = [
        remote(gain, gains.at[d, f], gain_fwd, 0, other),
        remote(out, outs.at[f], out_fwd, z, other),
    ]
    for copy in passed:
        copy.start()
    own[0].wait()
    loop(1, dp_size, lambda p: piece_copy(p).wait())
    wide_start()
    wide_pass(z).start()
    out_go(lambda s: out_pass(s).start())
    wide_go(lambda s: wide_pass(s).start())

    def pass_gain(p):
        gain_copy(p).wait_recv()
        gain_pass(p).start()

    loop(1, chips, pass_gain)
    loop(1, dp_size, lambda p: seg_copy(p).wait())
    loop(1, dp_size, lambda p: x_copy(p).wait())
    for copy in own[1:]:
        copy.wait()
    for copy in passed:
        copy.wait()
    wide_pass(z).wait()

    def end_pass(k):
        s = (z + k) % z_size
        out_pass(s).wait()
        wide_pass(s).wait()

    loop(1, z_size, end_pass)
    loop(1, chips, lambda p: gain_pass(p).wait())
    loop(1, chips, lambda p: gain_copy(p).wait_send())
    out_finish()
    wide_finish()


def cross_kernel(spread, sizes, rows, pair, rows_out, pair_out, *scratch):
    rows_own, pair_own, rows_sem, pair_sem, own_sem = scratch
    dp_size, z_size = sizes
    f_size = 2 * z_size
    d, z, c = place()
    f = 2 * z + c
    greet(sizes, along_dp=True, along_fsdp=True)

    def rows_copy(p):
        to = (d + p) % dp_size
        piece = rows if spread else rows.at[to]
        return remote(piece, rows_out.at[d], rows_sem, p, device(to, z, c))

    def pair_copy(p):
        to = (f + p) % f_size
        return remote(
            pair.at[to], pair_out.at[f], pair_sem, p, {"dp": d, "fsdp": to}
        )

    loop(1, dp_size, lambda p: rows_copy(p).start())
    loop(1, f_size, lambda p: pair_copy(p).start())
    first = pltpu.make_async_copy(rows if spread else rows.at[d], rows_own, own_sem.at[0])
    second = pltpu.make_async_copy(pair.at[f], pair_own, own_sem.at[1])
    first.start()
    second.start()
    first.wait()
    second.wait()
    third = pltpu.make_async_copy(rows_own, rows_out.at[d], own_sem.at[2])
    fourth = pltpu.make_async_copy(pair_own, pair_out.at[f], own_sem.at[3])
    third.start()
    fourth.start()
    third.wait()
    fourth.wait()
    loop(1, dp_size, lambda p: rows_copy(p).wait())
    loop(1, f_size, lambda p: pair_copy(p).wait())


def scatter_cross(sizes, *refs):
    cross_kernel(False, sizes, *refs)


def gather_cross(sizes, *refs):
    cross_kernel(True, sizes, *refs)


def gather_line(sizes, rows, pair, rows_out, pair_out, bounce, *sems):
    rows_sem, pass_sem, pair_sem, own_sem = sems
    dp_size, z_size = sizes
    d, z, c = place()
    f = 2 * z + c
    greet(sizes, along_dp=True, along_fsdp=True)
    q = ring_place(d, dp_size)
    right, left = ring_place(q + 1, dp_size), ring_place(q - 1, dp_size)
    other = device(d, z, 1 - c)
    half = pair.shape[0] // 2

    def rows_pass(s):
        slot = rows_out.at[2 * s + c]
        return remote(slot, slot, pass_sem, s, other)

    def whole_copy(to, index):
        return remote(pair, pair_out.at[d], pair_sem, index, device(to, z, c))

    def half_copy(source, to, low, index):
        slot = pair_out.at[source, pl.ds(low, half)]
        return remote(slot, slot, pair_sem, index, device(to, z, c))

    start, go, finish = chain(z_size, lambda s: rows_out.at[2 * s + c], rows_sem, rows)
    start()
    to_right, to_left = whole_copy(right, 0), whole_copy(left, 1)
    to_right.start()
    to_left.start()
    own = pltpu.make_async_copy(rows, rows_out.at[f], own_sem.at[0])
    own.start()
    passed = remote(rows, rows_out.at[f], pass_sem, z, other)
    passed.start()
    take = pltpu.make_async_copy(pair, bounce, own_sem.at[1])
    take.start()
    take.wait()
    give = pltpu.make_async_copy(bounce, pair_out.at[d], own_sem.at[2])
    give.start()
    go(lambda s: rows_pass(s).start())
    to_right.wait_recv()
    on_right = half_copy(left, right, 0, 2)
    on_right.start()
    to_left.wait_recv()
    on_left = half_copy(right, left, half, 3)
    on_left.start()
    give.wait()
    own.wait()
    passed.wait()
    loop(1, z_size, lambda k: rows_pass((z + k) % z_size).wait())
    finish()
    to_right.wait_send()
    to_left.wait_send()
    on_right.wait()
    on_left.wait()


def scatter_line(sizes, part, part_out, mine, theirs, part_sem, swap_sem, load_sem, own_sem):
    dp_size, z_size = sizes
    d, z, c = place()
    greet((1, z_size), along_fsdp=True)
    other = device(d, z, 1 - c)

    def swap_copy(p):
        to = (z + p) % z_size
        return remote(part.at[to, 1 - c], theirs.at[to], swap_sem, p, other)

    def load(p):
        to = (z + p) % z_size
        return pltpu.make_async_copy(part.at[to, c], mine.at[to], load_sem.at[p])

    def part_copy(p):
        to = (z + p) % z_size
        return remote(mine.at[to], part_out.at[z], part_sem, p, device(d, to, c))

    def begin(p):
        swap_copy(p).start()
        load(p).start()

    def add(p):
        to = (z + p) % z_size
        swap_copy(p).wait()
        load(p).wait()
        mine[to] = (mine[to].astype(F32) + theirs[to].astype(F32)).astype(BF)

    def send(p):
        add(p)
        part_copy(p).start()

    loop(1, z_size, begin)
    begin(0)
    loop(1, z_size, send)
    add(0)
    own = pltpu.make_async_copy(mine.at[z], part_out.at[z], own_sem.at[0])
    own.start()
    own.wait()
    loop(1, z_size, lambda p: part_copy(p).wait())


def end_kernel(sizes, rows, wide, out, gain, rows_out, wide_out, out_out, gain_out, *scratch):
    rows_own, wide_mine, wide_theirs, out_mine, out_theirs, gain_mine, gain_theirs = scratch[:7]
    rows_sem, wide_sem, out_sem, gain_sem, swap_sem, own_sem = scratch[7:]
    dp_size, z_size = sizes
    chips = dp_size * z_size
    d, z, c = place()
    greet(sizes, same_core=True, partner=True)
    other = device(d, z, 1 - c)
    swaps = [
        remote(out.at[:, 1 - c], out_theirs, swap_sem, 0, other),
        remote(wide.at[:, :, 1 - c], wide_theirs, swap_sem, 1, other),
        remote(gain.at[:, :, 1 - c], gain_theirs, swap_sem, 2, other),
    ]
    loads = [
        pltpu.make_async_copy(out.at[:, c], out_mine, own_sem.at[0]),
        pltpu.make_async_copy(wide.at[:, :, c], wide_mine, own_sem.at[1]),
        pltpu.make_async_copy(gain.at[:, :, c], gain_mine, own_sem.at[2]),
    ]
    for copy in swaps + loads:
        copy.start()

    def rows_copy(p):
        to = (d + p) % dp_size
        return remote(rows.at[to], rows_out.at[d], rows_sem, p, device(to, z, c))

    loop(1, dp_size, lambda p: rows_copy(p).start())
    rows_in = pltpu.make_async_copy(rows.at[d], rows_own, own_sem.at[3])
    rows_in.start()

    def out_copy(p):
        to = (z + p) % z_size
        return remote(out_mine.at[to], out_out.at[z], out_sem, p, device(d, to, c))

    def target(p):
        return (d + p // z_size) % dp_size, (z + p % z_size) % z_size

    def wide_copy(p):
        to_d, to_z = target(p)
        return remote(
            wide_mine.at[to_d, to_z], wide_out.at[d, z], wide_sem, p, device(to_d, to_z, c)
        )

    def gain_copy(p):
        to_d, to_z = target(p)
        return remote(
            gain_mine.at[to_d, to_z], gain_out.at[d, z], gain_sem, p, device(to_d, to_z, c)
        )

    def add_out(p):
        to = (z + p) % z_size
        out_mine[to] = (out_mine[to].astype(F32) + out_theirs[to].astype(F32)).astype(BF)

    def add_wide(p):
        to_d, to_z = target(p)
        total = wide_mine[to_d, to_z].astype(F32) + wide_theirs[to_d, to_z].astype(F32)
        wide_mine[to_d, to_z] = total.astype(BF)
        gain_mine[to_d, to_z] = gain_mine[to_d, to_z] + gain_theirs[to_d, to_z]

    swaps[0].wait()
    loads[0].wait()

    def send_out(p):
        add_out(p)
        out_copy(p).start()

    loop(1, z_size, send_out)
    add_out(0)
    for copy in swaps[1:] + loads[1:]:
        copy.wait()

    def send_wide(p):
        add_wide(p)
        wide_copy(p).start()
        gain_copy(p).start()

    loop(1, chips, send_wide)
    add_wide(0)
    rows_in.wait()
    own = [
        pltpu.make_async_copy(rows_own, rows_out.at[d], own_sem.at[4]),
        pltpu.make_async_copy(out_mine.at[z], out_out.at[z], own_sem.at[5]),
        pltpu.make_async_copy(wide_mine.at[d, z], wide_out.at[d, z], own_sem.at[6]),
        pltpu.make_async_copy(gain_mine.at[d, z], gain_out.at[d, z], own_sem.at[7]),
    ]
    for copy in own:
        copy.start()
    for copy in own:
        copy.wait()
    loop(1, dp_size, lambda p: rows_copy(p).wait())
    loop(1, z_size, lambda p: out_copy(p).wait())
    loop(1, chips, lambda p: wide_copy(p).wait())
    loop(1, chips, lambda p: gain_copy(p).wait())


def local(
    dp_size,
    fs_size,
    inputs,
    segment_ids,
    attn_gain,
    query_weight,
    key_weight,
    value_weight,
    output_weight,
    mlp_gain,
    gate_weight,
    up_weight,
    down_weight,
    cotangent,
):
    z_size = fs_size // 2
    sizes = (dp_size, z_size)
    row_count, width = inputs.shape
    weight_rows, ff_width = gate_weight.shape
    unit = down_weight.shape[0]
    share = dp_size * unit
    heads = HEADS // dp_size
    query_width = heads * HEAD_DIM
    wide_width = query_width + 2 * HEAD_DIM
    score_scale = HEAD_DIM ** (-0.5)
    vmem, hbm = pltpu.VMEM, pltpu.HBM

    def by_share(weight):
        weight = weight.reshape(weight_rows, dp_size, fs_size, unit).transpose(2, 0, 1, 3)
        return weight.reshape(fs_size, weight_rows, share)

    pair = jnp.concatenate([by_share(gate_weight), by_share(up_weight)], axis=2)
    down_full = gather(down_weight, "dp")
    def by_head(weight):
        return weight.reshape(weight_rows, dp_size, -1).transpose(1, 0, 2)

    wide = jnp.concatenate(
        [by_head(query_weight), by_head(key_weight), by_head(value_weight)], axis=2
    )
    gain = jnp.concatenate([attn_gain, mlp_gain, jnp.zeros((128 - 2 * weight_rows,), BF)])
    gain = jnp.broadcast_to(gain[None, :], (16, 128))
    seg = jnp.broadcast_to(segment_ids[None, :], (8, row_count))
    chips = dp_size * z_size
    xs, segs, gains, wides, out_full = call(
        start_kernel,
        sizes,
        0,
        60,
        [
            ((dp_size, row_count, width), BF),
            ((dp_size, 8, row_count), jnp.int32),
            ((dp_size, fs_size, 16, 128), BF),
            ((dp_size, fs_size, weight_rows, wide_width), BF),
            ((fs_size, weight_rows, width), BF),
        ],
        [
            dma(2, dp_size),
            dma(2, dp_size),
            dma(2, chips),
            dma(2, dp_size),
            dma(2, z_size + 1),
            dma(2, z_size + 1),
            dma(2, chips),
            dma(2, z_size),
            dma(2, z_size),
            dma(5),
        ],
        [vmem] * 5,
        inputs,
        seg,
        gain,
        wide,
        output_weight,
    )
    down_full, cot_late, xs = lax.optimization_barrier((down_full, cotangent, xs))
    cot_full = gather(cot_late, "fsdp")
    gains = gains[:, :, 0, :].astype(F32)
    gain_one = gains[:, :, :weight_rows].reshape(width)
    gain_two = gains[:, :, weight_rows : 2 * weight_rows].reshape(width)
    wides = wides.reshape(width, wide_width)
    out_full = out_full.reshape(query_width, width)

    sources = xs.reshape(dp_size * row_count, width).astype(F32)
    inverse_one = lax.rsqrt(jnp.mean(sources * sources, axis=1, keepdims=True) + EPSILON)
    normed_all = sources * inverse_one
    act_one = (normed_all * gain_one).astype(BF)
    wide_rows = matmul(act_one, wides)
    query_rows = wide_rows[:, :query_width].reshape(dp_size, row_count, heads, HEAD_DIM)
    key_rows = wide_rows[:, query_width : query_width + HEAD_DIM]
    key_rows = key_rows.reshape(dp_size, row_count, 1, HEAD_DIM)
    value_low = wide_rows[:, query_width + HEAD_DIM :].astype(BF)
    value_low = value_low.reshape(dp_size, row_count, HEAD_DIM)
    segs = segs[:, 0, :]
    cosine_table, sine_table = jax.vmap(rotary_tables)(segs)
    query_rot = rotate(query_rows, cosine_table, sine_table).astype(BF)
    key_rot = rotate(key_rows, cosine_table, sine_table).astype(BF)[:, :, 0, :]
    row_index = jnp.arange(row_count, dtype=jnp.int32)
    allowed = (segs[:, :, None] == segs[:, None, :]) & (
        row_index[:, None] >= row_index[None, :]
    )
    raw = jnp.einsum("bqhd,bkd->bhqk", query_rot, key_rot, preferred_element_type=F32)
    scores = jnp.where(allowed[:, None], raw * score_scale, -1e30)
    row_max = jnp.max(scores, axis=-1, keepdims=True)
    log_total = row_max + jnp.log(jnp.sum(jnp.exp(scores - row_max), axis=-1, keepdims=True))
    attn_probs = jnp.exp(scores - log_total)
    probs_low = attn_probs.astype(BF)
    mixed_low = jnp.einsum("bhqk,bkd->bqhd", probs_low, value_low, preferred_element_type=F32)
    mixed_low = mixed_low.reshape(dp_size * row_count, query_width).astype(BF)
    mixed_out = matmul(mixed_low, out_full).astype(BF).reshape(dp_size, row_count, width)

    pair_shape = (fs_size, weight_rows, 2 * share)
    rows_shape = (dp_size, row_count, width)
    cross_scratch = [
        pltpu.VMEM((row_count, width), BF),
        pltpu.VMEM(pair_shape[1:], BF),
        dma(2, dp_size),
        dma(2, fs_size),
        dma(4),
    ]
    mixed_parts, pair_rows = call(
        scatter_cross,
        sizes,
        1,
        36,
        [(rows_shape, BF), (pair_shape, BF)],
        cross_scratch,
        [hbm, hbm],
        mixed_out,
        pair,
    )
    source = inputs.astype(F32)
    residual = source + jnp.sum(mixed_parts.astype(F32), axis=0)
    inverse_two = lax.rsqrt(jnp.mean(residual * residual, axis=1, keepdims=True) + EPSILON)
    normed_two = residual * inverse_two
    act_two = (normed_two * gain_two).astype(BF)
    grad_hidden = times_trans(cot_full, down_full)
    act_two, grad_hidden = lax.optimization_barrier((act_two, grad_hidden))
    pair_rows = pair_rows.reshape(fs_size * weight_rows, 2 * share)
    act_full, pair_full = call(
        gather_line,
        sizes,
        2,
        55,
        [((fs_size, row_count, width), BF), ((dp_size,) + pair_rows.shape, BF)],
        [
            pltpu.VMEM(pair_rows.shape, BF),
            dma(2, z_size + 1),
            dma(2, z_size),
            dma(2, 4),
            dma(3),
        ],
        [vmem, hbm],
        act_two,
        pair_rows,
    )
    pair_full = pair_full.reshape(width, 2 * share)
    act_full = act_full.reshape(fs_size * row_count, width)

    both = matmul(act_full, pair_full)
    gate_value, up_value = both[:, :share], both[:, share:]
    sigmoid_gate = jax.nn.sigmoid(gate_value)
    hidden_low = (gate_value * sigmoid_gate * up_value).astype(BF)
    grad_gate = (
        grad_hidden * up_value * sigmoid_gate * (1.0 + gate_value * (1.0 - sigmoid_gate))
    ).astype(BF)
    grad_up = (grad_hidden * gate_value * sigmoid_gate).astype(BF)
    grad_both = jnp.concatenate([grad_gate, grad_up], axis=1)
    grad_part = times_trans(grad_both, pair_full).astype(BF)
    pair_grad = outer_sum(act_full, grad_both).astype(BF)
    grad_part, pair_grad = lax.optimization_barrier((grad_part, pair_grad))
    pair_grad = scatter_sum(pair_grad, "dp")
    (grad_parts,) = call(
        scatter_line,
        sizes,
        3,
        50,
        [((z_size, row_count, width), BF)],
        [
            pltpu.VMEM((z_size, row_count, width), BF),
            pltpu.VMEM((z_size, row_count, width), BF),
            dma(2, z_size),
            dma(2, z_size),
            dma(z_size),
            dma(1),
        ],
        [hbm],
        grad_part.reshape(z_size, 2, row_count, width),
    )
    hidden_low, grad_parts, pair_grad = lax.optimization_barrier(
        (hidden_low, grad_parts, pair_grad)
    )
    down_grad = scatter_sum(outer_sum(hidden_low, cot_full).astype(BF), "dp").astype(F32)

    grad_act_two = jnp.sum(grad_parts.astype(F32), axis=0)
    mlp_gain_grad = jnp.sum(normed_two * grad_act_two, axis=0)
    grad_residual = cotangent.astype(F32) + norm_back(
        grad_act_two, normed_two, inverse_two, gain_two
    )
    grad_attn, pair_back = call(
        gather_cross,
        sizes,
        4,
        36,
        [(rows_shape, BF), (pair_shape, BF)],
        cross_scratch,
        [hbm, hbm],
        grad_residual.astype(BF),
        pair_grad.reshape(pair_shape),
    )
    hidden_low, grad_attn = lax.optimization_barrier((hidden_low, grad_attn))
    mlp_out = scatter_sum(matmul(hidden_low, down_full).astype(BF), "fsdp")
    outputs = (residual + mlp_out.astype(F32)).astype(BF)
    pair_back = pair_back.reshape(fs_size, weight_rows, 2, dp_size, unit)
    pair_back = pair_back.transpose(2, 1, 3, 0, 4).reshape(2, weight_rows, ff_width)
    gate_grad = pair_back[0].astype(F32)
    up_grad = pair_back[1].astype(F32)

    grad_attn = grad_attn.reshape(dp_size * row_count, width)
    output_grad = outer_sum(mixed_low, grad_attn).astype(BF)
    grad_mixed = times_trans(grad_attn, out_full).astype(BF)
    grad_mixed = grad_mixed.reshape(dp_size, row_count, heads, HEAD_DIM)
    grad_probs = jnp.einsum("bqhd,bkd->bhqk", grad_mixed, value_low, preferred_element_type=F32)
    grad_value = jnp.einsum("bhqk,bqhd->bkd", probs_low, grad_mixed, preferred_element_type=F32)
    grad_value = grad_value.astype(BF).reshape(dp_size * row_count, HEAD_DIM)
    grad_raw = (
        score_scale
        * attn_probs
        * (grad_probs - jnp.sum(attn_probs * grad_probs, axis=-1, keepdims=True))
    )
    grad_raw = grad_raw.astype(BF)
    grad_qrot = jnp.einsum("bhqk,bkd->bqhd", grad_raw, key_rot, preferred_element_type=F32)
    grad_krot = jnp.einsum("bhqk,bqhd->bkd", grad_raw, query_rot, preferred_element_type=F32)
    grad_query = rotate_back(grad_qrot, cosine_table, sine_table).astype(BF)
    grad_key = rotate_back(grad_krot[:, :, None, :], cosine_table, sine_table).astype(BF)
    grad_wide = jnp.concatenate(
        [
            grad_query.reshape(dp_size * row_count, query_width),
            grad_key.reshape(dp_size * row_count, HEAD_DIM),
            grad_value,
        ],
        axis=1,
    )
    grad_act = times_trans(grad_wide, wides)
    gain_grad = jnp.sum(normed_all * grad_act, axis=0)
    by_owner = (dp_size, fs_size, weight_rows)
    gain_grads = jnp.concatenate(
        [
            gain_grad.reshape(by_owner),
            mlp_gain_grad.reshape(by_owner),
            jnp.zeros((dp_size, fs_size, 128 - 2 * weight_rows), F32),
        ],
        axis=2,
    )
    gain_grads = jnp.broadcast_to(gain_grads[:, :, None, :], (dp_size, fs_size, 8, 128))
    wide_grad = outer_sum(act_one, grad_wide).astype(BF)
    wide_half = (dp_size, z_size, weight_rows, wide_width)
    out_half = (z_size, weight_rows, width)
    gain_half = (dp_size, z_size, 8, 128)
    grad_act_parts, wide_parts, out_parts, gain_parts = call(
        end_kernel,
        sizes,
        5,
        60,
        [(rows_shape, BF), (wide_half, BF), (out_half, BF), (gain_half, F32)],
        [
            pltpu.VMEM((row_count, width), BF),
            pltpu.VMEM(wide_half, BF),
            pltpu.VMEM(wide_half, BF),
            pltpu.VMEM(out_half, BF),
            pltpu.VMEM(out_half, BF),
            pltpu.VMEM(gain_half, F32),
            pltpu.VMEM(gain_half, F32),
            dma(2, dp_size),
            dma(2, chips),
            dma(2, z_size),
            dma(2, chips),
            dma(2, 3),
            dma(8),
        ],
        [hbm] * 4,
        grad_act.astype(BF).reshape(rows_shape),
        wide_grad.reshape(dp_size, z_size, 2, weight_rows, wide_width),
        output_grad.reshape(z_size, 2, weight_rows, width),
        gain_grads.reshape(dp_size, z_size, 2, 8, 128),
    )
    grad_act_one = jnp.sum(grad_act_parts.astype(F32), axis=0)
    own_inverse = lax.rsqrt(jnp.mean(source * source, axis=1, keepdims=True) + EPSILON)
    input_grad = (
        grad_residual + norm_back(grad_act_one, source * own_inverse, own_inverse, gain_one)
    ).astype(BF)
    gain_total = jnp.sum(gain_parts[:, :, 0, :], axis=(0, 1))
    wide_total = jnp.sum(wide_parts.astype(F32), axis=1)

    def from_heads(value):
        return value.transpose(1, 0, 2).reshape(weight_rows, -1)

    return (
        outputs,
        input_grad,
        gain_total[:weight_rows],
        from_heads(wide_total[:, :, :query_width]),
        from_heads(wide_total[:, :, query_width : query_width + HEAD_DIM]),
        from_heads(wide_total[:, :, query_width + HEAD_DIM :]),
        jnp.sum(out_parts.astype(F32), axis=0),
        gain_total[weight_rows : 2 * weight_rows],
        gate_grad,
        up_grad,
        down_grad,
    )


def solution(mesh):
    dp_size, fs_size = mesh.shape["dp"], mesh.shape["fsdp"]
    row = P(ALL, None)
    flat = P(ALL)

    def step(*args):
        return local(dp_size, fs_size, *args)

    return jax.shard_map(
        step,
        mesh=mesh,
        in_specs=(row, flat, flat, row, row, row, row, flat, row, row, row, row),
        out_specs=(row, row, flat, row, row, row, row, flat, row, row, row),
        check_vma=False,
    )
```

```python
import functools

import jax
import jax.numpy as jnp
from jax import lax
from jax.experimental import pallas as pl
from jax.experimental.pallas import tpu as pltpu
from jax.sharding import PartitionSpec as P

HEADS = 32
HEAD_DIM = 64
KV_HEADS = 4
EPSILON = 1e-05
ALL = ("dp", "fsdp")
BF = jnp.bfloat16
F32 = jnp.float32
MESH = pl.DeviceIdType.MESH


def matmul(left_side, right_side):
    return jnp.dot(left_side, right_side, preferred_element_type=F32)


def outer_sum(left_side, right_side):
    return lax.dot_general(
        left_side, right_side, (((0,), (0,)), ((), ())), preferred_element_type=F32
    )


def times_trans(left_side, right_side):
    return lax.dot_general(
        left_side, right_side, (((1,), (1,)), ((), ())), preferred_element_type=F32
    )


def rotary_tables(segments):
    row_count = segments.shape[0]
    row_index = jnp.arange(row_count, dtype=jnp.int32)
    earlier = jnp.sum((segments[None, :] < segments[:, None]).astype(jnp.int32), axis=1)
    places = (row_index - earlier).astype(F32)
    halfway = HEAD_DIM // 2
    frequency = 10000.0 ** (jnp.arange(halfway, dtype=F32) * (-2.0 / HEAD_DIM))
    angles = places[:, None] * frequency[None, :]
    cosine_table, sine_table = jnp.cos(angles), jnp.sin(angles)
    pairs = 128 // HEAD_DIM
    return (
        jnp.concatenate([cosine_table, cosine_table] * pairs, axis=1),
        jnp.concatenate([-sine_table, sine_table] * pairs, axis=1),
    )


def norm_back(upstream, normed, inverse, gain_vec):
    scaled = upstream * gain_vec
    return inverse * (scaled - normed * jnp.mean(scaled * normed, axis=1, keepdims=True))


def gather(value, axes):
    return lax.all_gather(value, axes, axis=0, tiled=True)


def scatter_sum(value, axes):
    return lax.psum_scatter(value, axes, scatter_dimension=0, tiled=True)


def place():
    d, f = lax.axis_index("dp"), lax.axis_index("fsdp")
    return d, f // 2, f % 2


def device(d, z, c):
    return {"dp": d, "fsdp": 2 * z + c}


def remote(src, dst, sems, index, target):
    return pltpu.make_async_remote_copy(
        src_ref=src,
        dst_ref=dst,
        send_sem=sems.at[0, index],
        recv_sem=sems.at[1, index],
        device_id=target,
        device_id_type=MESH,
    )


def hop(src, dst, sems, send, recv, target):
    return pltpu.make_async_remote_copy(
        src_ref=src,
        dst_ref=dst,
        send_sem=sems.at[0, send],
        recv_sem=sems.at[1, recv],
        device_id=target,
        device_id_type=MESH,
    )


def chain(z_size, shard, sems, first):
    d, z, c = place()

    def copy(s, to, send=None, src=None):
        src = shard(s) if src is None else src
        return hop(src, shard(s), sems, s if send is None else send, s, device(d, to, c))

    up, down = z < z_size - 1, z > 0

    def start():
        @pl.when(up)
        def _():
            copy(z, z + 1, src=first).start()

        @pl.when(down)
        def _():
            copy(z, z - 1, z_size, first).start()

    def go(arrived, low=1, high=z_size):
        def step(k):
            @pl.when(z - k >= 0)
            def _():
                copy(z - k, z).wait_recv()

                @pl.when(up)
                def _():
                    copy(z - k, z + 1).start()

                arrived(z - k)

            @pl.when(z + k < z_size)
            def _():
                copy(z + k, z).wait_recv()

                @pl.when(down)
                def _():
                    copy(z + k, z - 1).start()

                arrived(z + k)

        loop(low, high, step)

    def finish():
        @pl.when(up)
        def _():
            copy(z, z + 1, src=first).wait_send()

        @pl.when(down)
        def _():
            copy(z, z - 1, z_size, first).wait_send()

        def step(k):
            @pl.when((z - k >= 0) & up)
            def _():
                copy(z - k, z + 1).wait_send()

            @pl.when((z + k < z_size) & down)
            def _():
                copy(z + k, z - 1).wait_send()

        loop(1, z_size, step)

    return start, go, finish


def ring_place(q, size):
    q = (q + size) % size
    return q + (q // 2) * (1 - 2 * (q % 2)) if size == 4 else q


def loop(low, high, body):
    def step(index, carry):
        body(index)
        return carry

    lax.fori_loop(low, high, step, 0)


def greet(sizes, same_core=False, along_dp=False, along_fsdp=False, partner=False):
    dp_size, z_size = sizes
    d, z, c = place()
    barrier = pltpu.get_barrier_semaphore()

    def signal(target):
        pl.semaphore_signal(barrier, inc=1, device_id=target, device_id_type=MESH)

    count = 0
    if same_core:

        def to_chip(p):
            signal(device((d + p // z_size) % dp_size, (z + p % z_size) % z_size, c))

        loop(1, dp_size * z_size, to_chip)
        count += dp_size * z_size - 1
    if along_dp:
        loop(1, dp_size, lambda p: signal(device((d + p) % dp_size, z, c)))
        count += dp_size - 1
    if along_fsdp:
        f_size = 2 * z_size

        def to_line(p):
            signal({"dp": d, "fsdp": (2 * z + c + p) % f_size})

        loop(1, f_size, to_line)
        count += f_size - 1
    if partner:
        signal(device(d, z, 1 - c))
        count += 1
    pl.semaphore_wait(barrier, count)


def call(kernel, sizes, number, micros, outs, scratch, spaces, *args):
    return pl.pallas_call(
        functools.partial(kernel, sizes),
        out_shape=tuple(jax.ShapeDtypeStruct(shape, dtype) for shape, dtype in outs),
        in_specs=[pl.BlockSpec(memory_space=space) for space in spaces],
        out_specs=tuple(pl.BlockSpec(memory_space=pltpu.HBM) for _ in outs),
        scratch_shapes=scratch,
        compiler_params=pltpu.CompilerParams(collective_id=number, has_side_effects=True),
        cost_estimate=pl.CostEstimate(
            flops=int(micros * 1e9), bytes_accessed=0, transcendentals=0
        ),
        name=kernel.__name__,
    )(*args)


def dma(*shape):
    return pltpu.SemaphoreType.DMA(shape)


def start_kernel(sizes, x, seg, gain, wide, out, xs, segs, gains, wides, outs, *sems):
    x_sem, seg_sem, gain_sem, piece_sem, wide_sem, out_sem = sems[:6]
    gain_fwd, wide_fwd, out_fwd, own_sem = sems[6:]
    dp_size, z_size = sizes
    chips = dp_size * z_size
    d, z, c = place()
    f = 2 * z + c
    greet(sizes, same_core=True, partner=True)
    other = device(d, z, 1 - c)

    def piece_copy(p):
        to = (d + p) % dp_size
        return remote(wide.at[to], wides.at[d, f], piece_sem, p, device(to, z, c))

    def gain_copy(p):
        to_d, to_z = (d + p // z_size) % dp_size, (z + p % z_size) % z_size
        return remote(gain, gains.at[d, f], gain_sem, p, device(to_d, to_z, c))

    def x_copy(p):
        return remote(x, xs.at[d], x_sem, p, device((d + p) % dp_size, z, c))

    def seg_copy(p):
        return remote(seg, segs.at[d], seg_sem, p, device((d + p) % dp_size, z, c))

    def out_pass(s):
        slot = outs.at[2 * s + c]
        return remote(slot, slot, out_fwd, s, other)

    def wide_pass(s):
        slot = wides.at[:, 2 * s + c]
        return remote(slot, slot, wide_fwd, s, other)

    def gain_pass(p):
        from_d = (d - p // z_size + dp_size) % dp_size
        slot = gains.at[from_d, 2 * ((z - p % z_size + z_size) % z_size) + c]
        return remote(slot, slot, gain_fwd, p, other)

    out_start, out_go, out_finish = chain(z_size, lambda s: outs.at[2 * s + c], out_sem, out)
    wide_start, wide_go, wide_finish = chain(
        z_size, lambda s: wides.at[:, 2 * s + c], wide_sem, wides.at[:, f]
    )
    own = [
        pltpu.make_async_copy(wide.at[d], wides.at[d, f], own_sem.at[0]),
        pltpu.make_async_copy(x, xs.at[d], own_sem.at[1]),
        pltpu.make_async_copy(seg, segs.at[d], own_sem.at[2]),
        pltpu.make_async_copy(gain, gains.at[d, f], own_sem.at[3]),
        pltpu.make_async_copy(out, outs.at[f], own_sem.at[4]),
    ]
    loop(1, dp_size, lambda p: piece_copy(p).start())
    for copy in own:
        copy.start()
    out_start()
    loop(1, chips, lambda p: gain_copy(p).start())
    loop(1, dp_size, lambda p: seg_copy(p).start())
    loop(1, dp_size, lambda p: x_copy(p).start())
    passed = [
        remote(gain, gains.at[d, f], gain_fwd, 0, other),
        remote(out, outs.at[f], out_fwd, z, other),
    ]
    for copy in passed:
        copy.start()
    own[0].wait()
    loop(1, dp_size, lambda p: piece_copy(p).wait())
    wide_start()
    wide_pass(z).start()
    out_go(lambda s: out_pass(s).start())
    wide_go(lambda s: wide_pass(s).start())

    def pass_gain(p):
        gain_copy(p).wait_recv()
        gain_pass(p).start()

    loop(1, chips, pass_gain)
    loop(1, dp_size, lambda p: seg_copy(p).wait())
    loop(1, dp_size, lambda p: x_copy(p).wait())
    for copy in own[1:]:
        copy.wait()
    for copy in passed:
        copy.wait()
    wide_pass(z).wait()

    def end_pass(k):
        s = (z + k) % z_size
        out_pass(s).wait()
        wide_pass(s).wait()

    loop(1, z_size, end_pass)
    loop(1, chips, lambda p: gain_pass(p).wait())
    loop(1, chips, lambda p: gain_copy(p).wait_send())
    out_finish()
    wide_finish()


def cross_kernel(spread, sizes, rows, pair, rows_out, pair_out, *scratch):
    rows_own, pair_own, rows_sem, pair_sem, own_sem = scratch
    dp_size, z_size = sizes
    f_size = 2 * z_size
    d, z, c = place()
    f = 2 * z + c
    greet(sizes, along_dp=True, along_fsdp=True)

    def rows_copy(p):
        to = (d + p) % dp_size
        piece = rows if spread else rows.at[to]
        return remote(piece, rows_out.at[d], rows_sem, p, device(to, z, c))

    def pair_copy(p):
        to = (f + p) % f_size
        return remote(
            pair.at[to], pair_out.at[f], pair_sem, p, {"dp": d, "fsdp": to}
        )

    loop(1, dp_size, lambda p: rows_copy(p).start())
    loop(1, f_size, lambda p: pair_copy(p).start())
    first = pltpu.make_async_copy(rows if spread else rows.at[d], rows_own, own_sem.at[0])
    second = pltpu.make_async_copy(pair.at[f], pair_own, own_sem.at[1])
    first.start()
    second.start()
    first.wait()
    second.wait()
    third = pltpu.make_async_copy(rows_own, rows_out.at[d], own_sem.at[2])
    fourth = pltpu.make_async_copy(pair_own, pair_out.at[f], own_sem.at[3])
    third.start()
    fourth.start()
    third.wait()
    fourth.wait()
    loop(1, dp_size, lambda p: rows_copy(p).wait())
    loop(1, f_size, lambda p: pair_copy(p).wait())


def scatter_cross(sizes, *refs):
    cross_kernel(False, sizes, *refs)


def gather_cross(sizes, *refs):
    cross_kernel(True, sizes, *refs)


def gather_line(sizes, rows, pair, rows_out, pair_out, bounce, *sems):
    rows_sem, pass_sem, pair_sem, own_sem = sems
    dp_size, z_size = sizes
    d, z, c = place()
    f = 2 * z + c
    greet(sizes, along_dp=True, along_fsdp=True)
    q = ring_place(d, dp_size)
    right, left = ring_place(q + 1, dp_size), ring_place(q - 1, dp_size)
    other = device(d, z, 1 - c)
    half = pair.shape[0] // 2

    def rows_pass(s):
        slot = rows_out.at[2 * s + c]
        return remote(slot, slot, pass_sem, s, other)

    def whole_copy(to, index):
        return remote(pair, pair_out.at[d], pair_sem, index, device(to, z, c))

    def half_copy(source, to, low, index):
        slot = pair_out.at[source, pl.ds(low, half)]
        return remote(slot, slot, pair_sem, index, device(to, z, c))

    start, go, finish = chain(z_size, lambda s: rows_out.at[2 * s + c], rows_sem, rows)
    start()
    to_right, to_left = whole_copy(right, 0), whole_copy(left, 1)
    to_right.start()
    to_left.start()
    own = pltpu.make_async_copy(rows, rows_out.at[f], own_sem.at[0])
    own.start()
    passed = remote(rows, rows_out.at[f], pass_sem, z, other)
    passed.start()
    take = pltpu.make_async_copy(pair, bounce, own_sem.at[1])
    take.start()
    take.wait()
    give = pltpu.make_async_copy(bounce, pair_out.at[d], own_sem.at[2])
    give.start()
    go(lambda s: rows_pass(s).start(), 1, z_size - 1)
    to_right.wait_recv()
    on_right = half_copy(left, right, 0, 2)
    on_right.start()
    to_left.wait_recv()
    on_left = half_copy(right, left, half, 3)
    on_left.start()
    go(lambda s: rows_pass(s).start(), z_size - 1)
    give.wait()
    own.wait()
    passed.wait()
    loop(1, z_size, lambda k: rows_pass((z + k) % z_size).wait())
    finish()
    to_right.wait_send()
    to_left.wait_send()
    on_right.wait()
    on_left.wait()


def scatter_line(sizes, part, part_out, mine, theirs, part_sem, swap_sem, load_sem, own_sem):
    dp_size, z_size = sizes
    d, z, c = place()
    greet((1, z_size), along_fsdp=True)
    other = device(d, z, 1 - c)

    def swap_copy(p):
        to = (z + p) % z_size
        return remote(part.at[to, 1 - c], theirs.at[to], swap_sem, p, other)

    def load(p):
        to = (z + p) % z_size
        return pltpu.make_async_copy(part.at[to, c], mine.at[to], load_sem.at[p])

    def part_copy(p):
        to = (z + p) % z_size
        return remote(mine.at[to], part_out.at[z], part_sem, p, device(d, to, c))

    def begin(p):
        swap_copy(p).start()
        load(p).start()

    def add(p):
        to = (z + p) % z_size
        swap_copy(p).wait()
        load(p).wait()
        mine[to] = (mine[to].astype(F32) + theirs[to].astype(F32)).astype(BF)

    def send(p):
        add(p)
        part_copy(p).start()

    loop(1, z_size, begin)
    begin(0)
    loop(1, z_size, send)
    add(0)
    own = pltpu.make_async_copy(mine.at[z], part_out.at[z], own_sem.at[0])
    own.start()
    own.wait()
    loop(1, z_size, lambda p: part_copy(p).wait())


def end_kernel(sizes, rows, wide, out, gain, rows_out, wide_out, out_out, gain_out, *scratch):
    rows_own, wide_mine, wide_theirs, out_mine, out_theirs, gain_mine, gain_theirs = scratch[:7]
    rows_sem, wide_sem, out_sem, gain_sem, swap_sem, own_sem = scratch[7:]
    dp_size, z_size = sizes
    chips = dp_size * z_size
    d, z, c = place()
    greet(sizes, same_core=True, partner=True)
    other = device(d, z, 1 - c)
    swaps = [
        remote(out.at[:, 1 - c], out_theirs, swap_sem, 0, other),
        remote(wide.at[:, :, 1 - c], wide_theirs, swap_sem, 1, other),
        remote(gain.at[:, :, 1 - c], gain_theirs, swap_sem, 2, other),
    ]
    loads = [
        pltpu.make_async_copy(out.at[:, c], out_mine, own_sem.at[0]),
        pltpu.make_async_copy(wide.at[:, :, c], wide_mine, own_sem.at[1]),
        pltpu.make_async_copy(gain.at[:, :, c], gain_mine, own_sem.at[2]),
    ]
    for copy in swaps + loads:
        copy.start()

    def rows_copy(p):
        to = (d + p) % dp_size
        return remote(rows.at[to], rows_out.at[d], rows_sem, p, device(to, z, c))

    loop(1, dp_size, lambda p: rows_copy(p).start())
    rows_in = pltpu.make_async_copy(rows.at[d], rows_own, own_sem.at[3])
    rows_in.start()

    def out_copy(p):
        to = (z + p) % z_size
        return remote(out_mine.at[to], out_out.at[z], out_sem, p, device(d, to, c))

    def target(p):
        return (d + p // z_size) % dp_size, (z + p % z_size) % z_size

    def wide_copy(p):
        to_d, to_z = target(p)
        return remote(
            wide_mine.at[to_d, to_z], wide_out.at[d, z], wide_sem, p, device(to_d, to_z, c)
        )

    def gain_copy(p):
        to_d, to_z = target(p)
        return remote(
            gain_mine.at[to_d, to_z], gain_out.at[d, z], gain_sem, p, device(to_d, to_z, c)
        )

    def add_out(p):
        to = (z + p) % z_size
        out_mine[to] = (out_mine[to].astype(F32) + out_theirs[to].astype(F32)).astype(BF)

    def add_wide(p):
        to_d, to_z = target(p)
        total = wide_mine[to_d, to_z].astype(F32) + wide_theirs[to_d, to_z].astype(F32)
        wide_mine[to_d, to_z] = total.astype(BF)
        gain_mine[to_d, to_z] = gain_mine[to_d, to_z] + gain_theirs[to_d, to_z]

    swaps[0].wait()
    loads[0].wait()

    def send_out(p):
        add_out(p)
        out_copy(p).start()

    loop(1, z_size, send_out)
    add_out(0)
    for copy in swaps[1:] + loads[1:]:
        copy.wait()

    def send_wide(p):
        add_wide(p)
        wide_copy(p).start()
        gain_copy(p).start()

    loop(1, chips, send_wide)
    add_wide(0)
    rows_in.wait()
    own = [
        pltpu.make_async_copy(rows_own, rows_out.at[d], own_sem.at[4]),
        pltpu.make_async_copy(out_mine.at[z], out_out.at[z], own_sem.at[5]),
        pltpu.make_async_copy(wide_mine.at[d, z], wide_out.at[d, z], own_sem.at[6]),
        pltpu.make_async_copy(gain_mine.at[d, z], gain_out.at[d, z], own_sem.at[7]),
    ]
    for copy in own:
        copy.start()
    for copy in own:
        copy.wait()
    loop(1, dp_size, lambda p: rows_copy(p).wait())
    loop(1, z_size, lambda p: out_copy(p).wait())
    loop(1, chips, lambda p: wide_copy(p).wait())
    loop(1, chips, lambda p: gain_copy(p).wait())


def turned(value):
    lane = lax.broadcasted_iota(jnp.int32, value.shape, 1)
    ahead, behind = pltpu.roll(value, 128 - HEAD_DIM // 2, 1), pltpu.roll(value, HEAD_DIM // 2, 1)
    return jnp.where(lane % HEAD_DIM < HEAD_DIM // 2, ahead, behind)


def low_lanes(value):
    lane = lax.broadcasted_iota(jnp.int32, value.shape, 1)
    return jnp.where(lane < HEAD_DIM, value, jnp.zeros_like(value))


def high_lanes(value):
    lane = lax.broadcasted_iota(jnp.int32, value.shape, 1)
    return jnp.where(lane < HEAD_DIM, jnp.zeros_like(value), value)


def both_sides(value):
    low = low_lanes(value)
    return low, pltpu.roll(low, HEAD_DIM, 1)


def head_forward(pairs, x, gain, mask, cosine, sine, wides, out, *outs):
    part, probs, query_out, keyval_out, mixed_out, act_out = outs
    source = x[0].astype(F32)
    inverse = lax.rsqrt(jnp.mean(source * source, axis=1, keepdims=True) + EPSILON)
    act = (source * inverse * gain[...]).astype(BF)
    act_out[0] = act
    rows = matmul(act, wides[...])
    cosine_table, sine_table = cosine[0], sine[0]
    keyval = rows[:, pairs * 128 :]
    key = (keyval * cosine_table + turned(keyval) * sine_table).astype(BF).astype(F32)
    value = keyval.astype(BF).astype(F32)
    keyval_out[0] = jnp.where(
        lax.broadcasted_iota(jnp.int32, key.shape, 1) < HEAD_DIM, key, value
    ).astype(BF)
    keys = [side.astype(BF) for side in both_sides(key)]
    values = [
        side.astype(BF) for side in both_sides(pltpu.roll(value, HEAD_DIM, 1))
    ]
    allowed = mask[0] > 0
    for pair in range(pairs):
        lanes = pl.ds(pair * 128, 128)
        query = rows[:, pair * 128 : pair * 128 + 128]
        query = (query * cosine_table + turned(query) * sine_table).astype(BF)
        query_out[0, :, lanes] = query
        mixed = jnp.zeros(query.shape, F32)
        for side in range(2):
            raw = times_trans(query, keys[side])
            scores = jnp.where(allowed, raw * HEAD_DIM ** (-0.5), -1e30)
            powers = jnp.exp(scores - jnp.max(scores, axis=1, keepdims=True))
            weights = powers / jnp.sum(powers, axis=1, keepdims=True)
            probs[0, 2 * pair + side] = weights
            mixed += matmul(weights.astype(BF), values[side])
        mixed_out[0, :, lanes] = mixed.astype(BF)
    part[0] = matmul(mixed_out[0], out[...]).astype(BF)


def head_backward(pairs, upstream, x, cosine, sine, wides, out, *refs):
    probs, query_in, keyval_in, grad_wide, grad_act, gain_grad = refs
    grad_mixed = times_trans(upstream[0], out[...]).astype(BF)
    cosine_table, sine_table = cosine[0], sine[0]
    keyval = keyval_in[0].astype(F32)
    keys = [side.astype(BF) for side in both_sides(keyval)]
    values = [side.astype(BF) for side in both_sides(pltpu.roll(keyval, HEAD_DIM, 1))]
    key_sums = [jnp.zeros(keyval.shape, F32), jnp.zeros(keyval.shape, F32)]
    value_sums = [jnp.zeros(keyval.shape, F32), jnp.zeros(keyval.shape, F32)]
    for pair in range(pairs):
        lanes = pl.ds(pair * 128, 128)
        up = grad_mixed[:, pair * 128 : pair * 128 + 128]
        query = query_in[0, :, lanes]
        grad_query = jnp.zeros(query.shape, F32)
        for side in range(2):
            weights = probs[0, 2 * pair + side]
            grad_probs = times_trans(up, values[side])
            value_sums[side] += outer_sum(weights.astype(BF), up)
            inner = jnp.sum(weights * grad_probs, axis=1, keepdims=True)
            grad_raw = (HEAD_DIM ** (-0.5) * weights * (grad_probs - inner)).astype(BF)
            grad_query += matmul(grad_raw, keys[side])
            key_sums[side] += outer_sum(grad_raw, query)
        grad_query = grad_query * cosine_table - turned(grad_query) * sine_table
        grad_wide[0, :, lanes] = grad_query.astype(BF)
    grad_key = key_sums[0] + pltpu.roll(key_sums[1], HEAD_DIM, 1)
    grad_key = grad_key * cosine_table - turned(grad_key) * sine_table
    grad_value = value_sums[1] + pltpu.roll(value_sums[0], HEAD_DIM, 1)
    lane = lax.broadcasted_iota(jnp.int32, grad_key.shape, 1)
    grad_wide[0, :, pl.ds(pairs * 128, 128)] = jnp.where(
        lane < HEAD_DIM, grad_key, grad_value
    ).astype(BF)
    grad = times_trans(grad_wide[0], wides[...])
    grad_act[0] = grad.astype(BF)
    source = x[0].astype(F32)
    inverse = lax.rsqrt(jnp.mean(source * source, axis=1, keepdims=True) + EPSILON)
    total = jnp.sum(source * inverse * grad, axis=0, keepdims=True)

    @pl.when(pl.program_id(0) == 0)
    def _():
        gain_grad[...] = jnp.zeros_like(gain_grad)

    gain_grad[...] += total


def blocked(kernel, steps, micros, outs, args, whole):
    def spec(shape, keep):
        rank = len(shape)
        if keep:
            return pl.BlockSpec(shape, lambda i: (0,) * rank)
        return pl.BlockSpec((1,) + shape[1:], lambda i: (i,) + (0,) * (rank - 1))

    return pl.pallas_call(
        kernel,
        grid=(steps,),
        out_shape=tuple(jax.ShapeDtypeStruct(shape, dtype) for shape, dtype in outs),
        in_specs=[spec(arg.shape, k in whole) for k, arg in enumerate(args)],
        out_specs=tuple(spec(shape, len(shape) == 2) for shape, _ in outs),
        cost_estimate=pl.CostEstimate(
            flops=int(micros * 1e9), bytes_accessed=0, transcendentals=0
        ),
    )(*args)


def pack_kernel(counts, gate, up, packed):
    dp_size, fs_size, unit = counts
    for f in range(fs_size):
        pieces = []
        for weight in (gate, up):
            for g in range(dp_size):
                low = (g * fs_size + f) * unit
                pieces.append(weight[:, low : low + unit].astype(F32))
        packed[f] = jnp.concatenate(pieces, axis=1).astype(BF)


def unpack_kernel(counts, packed, gate, up):
    dp_size, fs_size, unit = counts
    for half, grad in enumerate((gate, up)):
        for g in range(dp_size):
            low = (half * dp_size + g) * unit
            pieces = [packed[f, :, low : low + unit].astype(F32) for f in range(fs_size)]
            grad[:, g * fs_size * unit : (g + 1) * fs_size * unit] = jnp.concatenate(
                pieces, axis=1
            )


def small_call(kernel, outs, *args):
    return pl.pallas_call(
        kernel,
        out_shape=tuple(jax.ShapeDtypeStruct(shape, dtype) for shape, dtype in outs),
        cost_estimate=pl.CostEstimate(flops=int(3e9), bytes_accessed=0, transcendentals=0),
    )(*args)


def local(
    dp_size,
    fs_size,
    inputs,
    segment_ids,
    attn_gain,
    query_weight,
    key_weight,
    value_weight,
    output_weight,
    mlp_gain,
    gate_weight,
    up_weight,
    down_weight,
    cotangent,
):
    z_size = fs_size // 2
    sizes = (dp_size, z_size)
    row_count, width = inputs.shape
    weight_rows, ff_width = gate_weight.shape
    unit = down_weight.shape[0]
    share = dp_size * unit
    heads = HEADS // dp_size
    query_width = heads * HEAD_DIM
    wide_width = query_width + 2 * HEAD_DIM
    vmem, hbm = pltpu.VMEM, pltpu.HBM

    counts = (dp_size, fs_size, unit)
    pair_shape = (fs_size, weight_rows, 2 * share)
    (pair,) = small_call(
        functools.partial(pack_kernel, counts), [(pair_shape, BF)], gate_weight, up_weight
    )
    down_full = gather(down_weight, "dp")
    def by_head(weight):
        return weight.reshape(weight_rows, dp_size, -1).transpose(1, 0, 2)

    wide = jnp.concatenate(
        [by_head(query_weight), by_head(key_weight), by_head(value_weight)], axis=2
    )
    gain = jnp.concatenate([attn_gain, mlp_gain, jnp.zeros((128 - 2 * weight_rows,), BF)])
    gain = jnp.broadcast_to(gain[None, :], (16, 128))
    seg = jnp.broadcast_to(segment_ids[None, :], (8, row_count))
    chips = dp_size * z_size
    xs, segs, gains, wides, out_full = call(
        start_kernel,
        sizes,
        0,
        60,
        [
            ((dp_size, row_count, width), BF),
            ((dp_size, 8, row_count), jnp.int32),
            ((dp_size, fs_size, 16, 128), BF),
            ((dp_size, fs_size, weight_rows, wide_width), BF),
            ((fs_size, weight_rows, width), BF),
        ],
        [
            dma(2, dp_size),
            dma(2, dp_size),
            dma(2, chips),
            dma(2, dp_size),
            dma(2, z_size + 1),
            dma(2, z_size + 1),
            dma(2, chips),
            dma(2, z_size),
            dma(2, z_size),
            dma(5),
        ],
        [vmem] * 5,
        inputs,
        seg,
        gain,
        wide,
        output_weight,
    )
    down_full, cot_late, xs = lax.optimization_barrier((down_full, cotangent, xs))
    cot_full = gather(cot_late, "fsdp")
    gains = gains[:, :, 0, :].astype(F32)
    gain_one = gains[:, :, :weight_rows].reshape(width)
    gain_two = gains[:, :, weight_rows : 2 * weight_rows].reshape(width)
    wides = wides.reshape(width, wide_width)
    out_full = out_full.reshape(query_width, width)

    segs = segs[:, 0, :]
    cosine_table, sine_table = jax.vmap(rotary_tables)(segs)
    row_index = jnp.arange(row_count, dtype=jnp.int32)
    allowed = (segs[:, :, None] == segs[:, None, :]) & (
        row_index[:, None] >= row_index[None, :]
    )
    mask = allowed.astype(F32)
    pairs = heads // 2
    by_row = (dp_size, row_count)
    mixed_out, probs, query_rot, keyval, mixed_low, act_one = blocked(
        functools.partial(head_forward, pairs),
        dp_size,
        12,
        [
            (by_row + (width,), BF),
            ((dp_size, heads, row_count, row_count), F32),
            (by_row + (query_width,), BF),
            (by_row + (128,), BF),
            (by_row + (query_width,), BF),
            (by_row + (width,), BF),
        ],
        [xs, gain_one[None, :], mask, cosine_table, sine_table, wides, out_full],
        (1, 5, 6),
    )
    mixed_low = mixed_low.reshape(dp_size * row_count, query_width)
    act_one = act_one.reshape(dp_size * row_count, width)

    rows_shape = (dp_size, row_count, width)
    cross_scratch = [
        pltpu.VMEM((row_count, width), BF),
        pltpu.VMEM(pair_shape[1:], BF),
        dma(2, dp_size),
        dma(2, fs_size),
        dma(4),
    ]
    mixed_parts, pair_rows = call(
        scatter_cross,
        sizes,
        1,
        36,
        [(rows_shape, BF), (pair_shape, BF)],
        cross_scratch,
        [hbm, hbm],
        mixed_out,
        pair,
    )
    source = inputs.astype(F32)
    residual = source + jnp.sum(mixed_parts.astype(F32), axis=0)
    inverse_two = lax.rsqrt(jnp.mean(residual * residual, axis=1, keepdims=True) + EPSILON)
    normed_two = residual * inverse_two
    act_two = (normed_two * gain_two).astype(BF)
    grad_hidden = times_trans(cot_full, down_full)
    act_two, grad_hidden = lax.optimization_barrier((act_two, grad_hidden))
    pair_rows = pair_rows.reshape(fs_size * weight_rows, 2 * share)
    act_full, pair_full = call(
        gather_line,
        sizes,
        2,
        55,
        [((fs_size, row_count, width), BF), ((dp_size,) + pair_rows.shape, BF)],
        [
            pltpu.VMEM(pair_rows.shape, BF),
            dma(2, z_size + 1),
            dma(2, z_size),
            dma(2, 4),
            dma(3),
        ],
        [vmem, hbm],
        act_two,
        pair_rows,
    )
    pair_full = pair_full.reshape(width, 2 * share)
    act_full = act_full.reshape(fs_size * row_count, width)

    both = matmul(act_full, pair_full)
    gate_value, up_value = both[:, :share], both[:, share:]
    sigmoid_gate = jax.nn.sigmoid(gate_value)
    hidden_low = (gate_value * sigmoid_gate * up_value).astype(BF)
    grad_gate = (
        grad_hidden * up_value * sigmoid_gate * (1.0 + gate_value * (1.0 - sigmoid_gate))
    ).astype(BF)
    grad_up = (grad_hidden * gate_value * sigmoid_gate).astype(BF)
    grad_both = jnp.concatenate([grad_gate, grad_up], axis=1)
    grad_part = times_trans(grad_both, pair_full).astype(BF)
    pair_grad = outer_sum(act_full, grad_both).astype(BF)
    grad_part, pair_grad = lax.optimization_barrier((grad_part, pair_grad))
    pair_grad = scatter_sum(pair_grad, "dp")
    (grad_parts,) = call(
        scatter_line,
        sizes,
        3,
        50,
        [((z_size, row_count, width), BF)],
        [
            pltpu.VMEM((z_size, row_count, width), BF),
            pltpu.VMEM((z_size, row_count, width), BF),
            dma(2, z_size),
            dma(2, z_size),
            dma(z_size),
            dma(1),
        ],
        [hbm],
        grad_part.reshape(z_size, 2, row_count, width),
    )
    hidden_low, grad_parts, pair_grad = lax.optimization_barrier(
        (hidden_low, grad_parts, pair_grad)
    )
    down_grad = scatter_sum(outer_sum(hidden_low, cot_full).astype(BF), "dp").astype(F32)

    grad_act_two = jnp.sum(grad_parts.astype(F32), axis=0)
    mlp_gain_grad = jnp.sum(normed_two * grad_act_two, axis=0)
    grad_residual = cotangent.astype(F32) + norm_back(
        grad_act_two, normed_two, inverse_two, gain_two
    )
    grad_attn, pair_back = call(
        gather_cross,
        sizes,
        4,
        36,
        [(rows_shape, BF), (pair_shape, BF)],
        cross_scratch,
        [hbm, hbm],
        grad_residual.astype(BF),
        pair_grad.reshape(pair_shape),
    )
    hidden_low, grad_attn = lax.optimization_barrier((hidden_low, grad_attn))
    mlp_out = scatter_sum(matmul(hidden_low, down_full).astype(BF), "fsdp")
    outputs = (residual + mlp_out.astype(F32)).astype(BF)
    gate_grad, up_grad = small_call(
        functools.partial(unpack_kernel, counts), [(gate_weight.shape, F32)] * 2, pair_back
    )
    grad_wide, grad_act, gain_grad = blocked(
        functools.partial(head_backward, pairs),
        dp_size,
        12,
        [
            (by_row + (wide_width,), BF),
            (by_row + (width,), BF),
            ((1, width), F32),
        ],
        [grad_attn, xs, cosine_table, sine_table, wides, out_full, probs, query_rot, keyval],
        (4, 5),
    )
    grad_attn = grad_attn.reshape(dp_size * row_count, width)
    output_grad = outer_sum(mixed_low, grad_attn).astype(BF)
    grad_wide = grad_wide.reshape(dp_size * row_count, wide_width)
    wide_grad = outer_sum(act_one, grad_wide).astype(BF)
    by_owner = (dp_size, fs_size, weight_rows)
    gain_grads = jnp.concatenate(
        [
            gain_grad.reshape(by_owner),
            mlp_gain_grad.reshape(by_owner),
            jnp.zeros((dp_size, fs_size, 128 - 2 * weight_rows), F32),
        ],
        axis=2,
    )
    gain_grads = jnp.broadcast_to(gain_grads[:, :, None, :], (dp_size, fs_size, 8, 128))
    wide_half = (dp_size, z_size, weight_rows, wide_width)
    out_half = (z_size, weight_rows, width)
    gain_half = (dp_size, z_size, 8, 128)
    grad_act_parts, wide_parts, out_parts, gain_parts = call(
        end_kernel,
        sizes,
        5,
        60,
        [(rows_shape, BF), (wide_half, BF), (out_half, BF), (gain_half, F32)],
        [
            pltpu.VMEM((row_count, width), BF),
            pltpu.VMEM(wide_half, BF),
            pltpu.VMEM(wide_half, BF),
            pltpu.VMEM(out_half, BF),
            pltpu.VMEM(out_half, BF),
            pltpu.VMEM(gain_half, F32),
            pltpu.VMEM(gain_half, F32),
            dma(2, dp_size),
            dma(2, chips),
            dma(2, z_size),
            dma(2, chips),
            dma(2, 3),
            dma(8),
        ],
        [hbm] * 4,
        grad_act,
        wide_grad.reshape(dp_size, z_size, 2, weight_rows, wide_width),
        output_grad.reshape(z_size, 2, weight_rows, width),
        gain_grads.reshape(dp_size, z_size, 2, 8, 128),
    )
    grad_act_one = jnp.sum(grad_act_parts.astype(F32), axis=0)
    own_inverse = lax.rsqrt(jnp.mean(source * source, axis=1, keepdims=True) + EPSILON)
    input_grad = (
        grad_residual + norm_back(grad_act_one, source * own_inverse, own_inverse, gain_one)
    ).astype(BF)
    gain_total = jnp.sum(gain_parts[:, :, 0, :], axis=(0, 1))
    wide_total = jnp.sum(wide_parts.astype(F32), axis=1)

    def from_heads(value):
        return value.transpose(1, 0, 2).reshape(weight_rows, -1)

    return (
        outputs,
        input_grad,
        gain_total[:weight_rows],
        from_heads(wide_total[:, :, :query_width]),
        from_heads(wide_total[:, :, query_width : query_width + HEAD_DIM]),
        from_heads(wide_total[:, :, query_width + HEAD_DIM :]),
        jnp.sum(out_parts.astype(F32), axis=0),
        gain_total[weight_rows : 2 * weight_rows],
        gate_grad,
        up_grad,
        down_grad,
    )


def solution(mesh):
    dp_size, fs_size = mesh.shape["dp"], mesh.shape["fsdp"]
    row = P(ALL, None)
    flat = P(ALL)

    def step(*args):
        return local(dp_size, fs_size, *args)

    return jax.shard_map(
        step,
        mesh=mesh,
        in_specs=(row, flat, flat, row, row, row, row, flat, row, row, row, row),
        out_specs=(row, row, flat, row, row, row, row, flat, row, row, row),
        check_vma=False,
    )
```

```python
import functools

import jax
import jax.numpy as jnp
from jax import lax
from jax.experimental import pallas as pl
from jax.experimental.pallas import tpu as pltpu
from jax.sharding import PartitionSpec as P

HEADS = 32
HEAD_DIM = 64
KV_HEADS = 4
EPSILON = 1e-05
ALL = ("dp", "fsdp")
BF = jnp.bfloat16
F32 = jnp.float32
MESH = pl.DeviceIdType.MESH


def matmul(left_side, right_side):
    return jnp.dot(left_side, right_side, preferred_element_type=F32)


def outer_sum(left_side, right_side):
    return lax.dot_general(
        left_side, right_side, (((0,), (0,)), ((), ())), preferred_element_type=F32
    )


def times_trans(left_side, right_side):
    return lax.dot_general(
        left_side, right_side, (((1,), (1,)), ((), ())), preferred_element_type=F32
    )


def rotary_tables(segments):
    row_count = segments.shape[0]
    row_index = jnp.arange(row_count, dtype=jnp.int32)
    earlier = jnp.sum((segments[None, :] < segments[:, None]).astype(jnp.int32), axis=1)
    places = (row_index - earlier).astype(F32)
    halfway = HEAD_DIM // 2
    frequency = 10000.0 ** (jnp.arange(halfway, dtype=F32) * (-2.0 / HEAD_DIM))
    angles = places[:, None] * frequency[None, :]
    cosine_table, sine_table = jnp.cos(angles), jnp.sin(angles)
    pairs = 128 // HEAD_DIM
    return (
        jnp.concatenate([cosine_table, cosine_table] * pairs, axis=1),
        jnp.concatenate([-sine_table, sine_table] * pairs, axis=1),
    )


def norm_back(upstream, normed, inverse, gain_vec):
    scaled = upstream * gain_vec
    return inverse * (scaled - normed * jnp.mean(scaled * normed, axis=1, keepdims=True))


def gather(value, axes):
    return lax.all_gather(value, axes, axis=0, tiled=True)


def scatter_sum(value, axes):
    return lax.psum_scatter(value, axes, scatter_dimension=0, tiled=True)


def place():
    d, f = lax.axis_index("dp"), lax.axis_index("fsdp")
    return d, f // 2, f % 2


def device(d, z, c):
    return {"dp": d, "fsdp": 2 * z + c}


def remote(src, dst, sems, index, target):
    return pltpu.make_async_remote_copy(
        src_ref=src,
        dst_ref=dst,
        send_sem=sems.at[0, index],
        recv_sem=sems.at[1, index],
        device_id=target,
        device_id_type=MESH,
    )


def hop(src, dst, sems, send, recv, target):
    return pltpu.make_async_remote_copy(
        src_ref=src,
        dst_ref=dst,
        send_sem=sems.at[0, send],
        recv_sem=sems.at[1, recv],
        device_id=target,
        device_id_type=MESH,
    )


def chain(z_size, shard, sems, first):
    d, z, c = place()

    def copy(s, to, send=None, src=None):
        src = shard(s) if src is None else src
        return hop(src, shard(s), sems, s if send is None else send, s, device(d, to, c))

    up, down = z < z_size - 1, z > 0

    def start():
        @pl.when(up)
        def _():
            copy(z, z + 1, src=first).start()

        @pl.when(down)
        def _():
            copy(z, z - 1, z_size, first).start()

    def go(arrived, low=1, high=z_size):
        def step(k):
            @pl.when(z - k >= 0)
            def _():
                copy(z - k, z).wait_recv()

                @pl.when(up)
                def _():
                    copy(z - k, z + 1).start()

                arrived(z - k)

            @pl.when(z + k < z_size)
            def _():
                copy(z + k, z).wait_recv()

                @pl.when(down)
                def _():
                    copy(z + k, z - 1).start()

                arrived(z + k)

        loop(low, high, step)

    def finish():
        @pl.when(up)
        def _():
            copy(z, z + 1, src=first).wait_send()

        @pl.when(down)
        def _():
            copy(z, z - 1, z_size, first).wait_send()

        def step(k):
            @pl.when((z - k >= 0) & up)
            def _():
                copy(z - k, z + 1).wait_send()

            @pl.when((z + k < z_size) & down)
            def _():
                copy(z + k, z - 1).wait_send()

        loop(1, z_size, step)

    return start, go, finish


def ring_place(q, size):
    q = (q + size) % size
    return q + (q // 2) * (1 - 2 * (q % 2)) if size == 4 else q


def loop(low, high, body):
    def step(index, carry):
        body(index)
        return carry

    lax.fori_loop(low, high, step, 0)


def greet(sizes, same_core=False, along_dp=False, along_fsdp=False, partner=False):
    dp_size, z_size = sizes
    d, z, c = place()
    barrier = pltpu.get_barrier_semaphore()

    def signal(target):
        pl.semaphore_signal(barrier, inc=1, device_id=target, device_id_type=MESH)

    count = 0
    if same_core:

        def to_chip(p):
            signal(device((d + p // z_size) % dp_size, (z + p % z_size) % z_size, c))

        loop(1, dp_size * z_size, to_chip)
        count += dp_size * z_size - 1
    if along_dp:
        loop(1, dp_size, lambda p: signal(device((d + p) % dp_size, z, c)))
        count += dp_size - 1
    if along_fsdp:
        f_size = 2 * z_size

        def to_line(p):
            signal({"dp": d, "fsdp": (2 * z + c + p) % f_size})

        loop(1, f_size, to_line)
        count += f_size - 1
    if partner:
        signal(device(d, z, 1 - c))
        count += 1
    pl.semaphore_wait(barrier, count)


def call(kernel, sizes, number, micros, outs, scratch, spaces, *args, kept=0):
    far = len(outs) - kept
    return pl.pallas_call(
        functools.partial(kernel, sizes),
        out_shape=tuple(jax.ShapeDtypeStruct(shape, dtype) for shape, dtype in outs),
        in_specs=[pl.BlockSpec(memory_space=space) for space in spaces],
        out_specs=tuple(
            pl.BlockSpec(memory_space=pltpu.HBM if k < far else pltpu.VMEM)
            for k in range(len(outs))
        ),
        scratch_shapes=scratch,
        compiler_params=pltpu.CompilerParams(collective_id=number, has_side_effects=True),
        cost_estimate=pl.CostEstimate(
            flops=int(micros * 1e9), bytes_accessed=0, transcendentals=0
        ),
        name=kernel.__name__,
    )(*args)


def dma(*shape):
    return pltpu.SemaphoreType.DMA(shape)


def start_kernel(sizes, x, seg, gain, wide, out, xs, segs, gains, wides, outs, *sems):
    x_sem, seg_sem, gain_sem, piece_sem, wide_sem, out_sem = sems[:6]
    gain_fwd, wide_fwd, out_fwd, own_sem = sems[6:]
    dp_size, z_size = sizes
    chips = dp_size * z_size
    d, z, c = place()
    f = 2 * z + c
    greet(sizes, same_core=True, partner=True)
    other = device(d, z, 1 - c)

    def piece_copy(p):
        to = (d + p) % dp_size
        return remote(wide.at[to], wides.at[d, f], piece_sem, p, device(to, z, c))

    def gain_copy(p):
        to_d, to_z = (d + p // z_size) % dp_size, (z + p % z_size) % z_size
        return remote(gain, gains.at[d, f], gain_sem, p, device(to_d, to_z, c))

    def x_copy(p):
        return remote(x, xs.at[d], x_sem, p, device((d + p) % dp_size, z, c))

    def seg_copy(p):
        return remote(seg, segs.at[d], seg_sem, p, device((d + p) % dp_size, z, c))

    def out_pass(s):
        slot = outs.at[2 * s + c]
        return remote(slot, slot, out_fwd, s, other)

    def wide_pass(s):
        slot = wides.at[:, 2 * s + c]
        return remote(slot, slot, wide_fwd, s, other)

    def gain_pass(p):
        from_d = (d - p // z_size + dp_size) % dp_size
        slot = gains.at[from_d, 2 * ((z - p % z_size + z_size) % z_size) + c]
        return remote(slot, slot, gain_fwd, p, other)

    out_start, out_go, out_finish = chain(z_size, lambda s: outs.at[2 * s + c], out_sem, out)
    wide_start, wide_go, wide_finish = chain(
        z_size, lambda s: wides.at[:, 2 * s + c], wide_sem, wides.at[:, f]
    )
    own = [
        pltpu.make_async_copy(wide.at[d], wides.at[d, f], own_sem.at[0]),
        pltpu.make_async_copy(x, xs.at[d], own_sem.at[1]),
        pltpu.make_async_copy(seg, segs.at[d], own_sem.at[2]),
        pltpu.make_async_copy(gain, gains.at[d, f], own_sem.at[3]),
        pltpu.make_async_copy(out, outs.at[f], own_sem.at[4]),
    ]
    loop(1, dp_size, lambda p: piece_copy(p).start())
    for copy in own:
        copy.start()
    out_start()
    loop(1, chips, lambda p: gain_copy(p).start())
    loop(1, dp_size, lambda p: seg_copy(p).start())
    loop(1, dp_size, lambda p: x_copy(p).start())
    passed = [
        remote(gain, gains.at[d, f], gain_fwd, 0, other),
        remote(out, outs.at[f], out_fwd, z, other),
    ]
    for copy in passed:
        copy.start()
    own[0].wait()
    loop(1, dp_size, lambda p: piece_copy(p).wait())
    wide_start()
    wide_pass(z).start()
    out_go(lambda s: out_pass(s).start())
    wide_go(lambda s: wide_pass(s).start())

    def pass_gain(p):
        gain_copy(p).wait_recv()
        gain_pass(p).start()

    loop(1, chips, pass_gain)
    loop(1, dp_size, lambda p: seg_copy(p).wait())
    loop(1, dp_size, lambda p: x_copy(p).wait())
    for copy in own[1:]:
        copy.wait()
    for copy in passed:
        copy.wait()
    wide_pass(z).wait()

    def end_pass(k):
        s = (z + k) % z_size
        out_pass(s).wait()
        wide_pass(s).wait()

    loop(1, z_size, end_pass)
    loop(1, chips, lambda p: gain_pass(p).wait())
    loop(1, chips, lambda p: gain_copy(p).wait_send())
    out_finish()
    wide_finish()


def gather_line(sizes, rows, pair, rows_out, pair_out, bounce, *sems):
    rows_sem, pass_sem, pair_sem, own_sem = sems
    dp_size, z_size = sizes
    d, z, c = place()
    f = 2 * z + c
    greet(sizes, along_dp=True, along_fsdp=True)
    q = ring_place(d, dp_size)
    right, left = ring_place(q + 1, dp_size), ring_place(q - 1, dp_size)
    other = device(d, z, 1 - c)
    half = pair.shape[0] // 2

    def rows_pass(s):
        slot = rows_out.at[2 * s + c]
        return remote(slot, slot, pass_sem, s, other)

    def whole_copy(to, index):
        return remote(pair, pair_out.at[d], pair_sem, index, device(to, z, c))

    def half_copy(source, to, low, index):
        slot = pair_out.at[source, pl.ds(low, half)]
        return remote(slot, slot, pair_sem, index, device(to, z, c))

    start, go, finish = chain(z_size, lambda s: rows_out.at[2 * s + c], rows_sem, rows)
    start()
    to_right, to_left = whole_copy(right, 0), whole_copy(left, 1)
    to_right.start()
    to_left.start()
    own = pltpu.make_async_copy(rows, rows_out.at[f], own_sem.at[0])
    own.start()
    passed = remote(rows, rows_out.at[f], pass_sem, z, other)
    passed.start()
    take = pltpu.make_async_copy(pair, bounce, own_sem.at[1])
    take.start()
    take.wait()
    give = pltpu.make_async_copy(bounce, pair_out.at[d], own_sem.at[2])
    give.start()
    go(lambda s: rows_pass(s).start(), 1, z_size - 1)
    to_right.wait_recv()
    on_right = half_copy(left, right, 0, 2)
    on_right.start()
    to_left.wait_recv()
    on_left = half_copy(right, left, half, 3)
    on_left.start()
    go(lambda s: rows_pass(s).start(), z_size - 1)
    give.wait()
    own.wait()
    passed.wait()
    loop(1, z_size, lambda k: rows_pass((z + k) % z_size).wait())
    finish()
    to_right.wait_send()
    to_left.wait_send()
    on_right.wait()
    on_left.wait()


def scatter_line(sizes, part, pair, part_out, pair_out, mine, theirs, pair_own, *sems):
    part_sem, swap_sem, load_sem, own_sem, pair_sem = sems
    dp_size, z_size = sizes
    d, z, c = place()
    greet(sizes, along_dp=True, along_fsdp=True)
    other = device(d, z, 1 - c)

    def swap_copy(p):
        to = (z + p) % z_size
        return remote(part.at[to, 1 - c], theirs.at[to], swap_sem, p, other)

    def load(p):
        to = (z + p) % z_size
        return pltpu.make_async_copy(part.at[to, c], mine.at[to], load_sem.at[p])

    def part_copy(p):
        to = (z + p) % z_size
        return remote(mine.at[to], part_out.at[z], part_sem, p, device(d, to, c))

    def begin(p):
        swap_copy(p).start()
        load(p).start()

    def add(p):
        to = (z + p) % z_size
        swap_copy(p).wait()
        load(p).wait()
        mine[to] = (mine[to].astype(F32) + theirs[to].astype(F32)).astype(BF)

    def send(p):
        add(p)
        part_copy(p).start()

    def pair_copy(p):
        to = (d + p) % dp_size
        return remote(pair.at[to], pair_out.at[d], pair_sem, p, device(to, z, c))

    loop(1, z_size, begin)
    begin(0)
    loop(1, dp_size, lambda p: pair_copy(p).start())
    take = pltpu.make_async_copy(pair.at[d], pair_own, own_sem.at[1])
    take.start()
    loop(1, z_size, send)
    add(0)
    own = pltpu.make_async_copy(mine.at[z], part_out.at[z], own_sem.at[0])
    own.start()
    take.wait()
    give = pltpu.make_async_copy(pair_own, pair_out.at[d], own_sem.at[2])
    give.start()
    own.wait()
    give.wait()
    loop(1, dp_size, lambda p: pair_copy(p).wait())
    loop(1, z_size, lambda p: part_copy(p).wait())


def end_kernel(sizes, rows, wide, out, gain, rows_out, wide_out, out_out, gain_out, *scratch):
    rows_own, wide_mine, wide_theirs, out_mine, out_theirs, gain_mine, gain_theirs = scratch[:7]
    rows_sem, wide_sem, out_sem, gain_sem, swap_sem, own_sem = scratch[7:]
    dp_size, z_size = sizes
    chips = dp_size * z_size
    d, z, c = place()
    greet(sizes, same_core=True, partner=True)
    other = device(d, z, 1 - c)
    swaps = [
        remote(out.at[:, 1 - c], out_theirs, swap_sem, 0, other),
        remote(wide.at[:, :, 1 - c], wide_theirs, swap_sem, 1, other),
        remote(gain.at[:, :, 1 - c], gain_theirs, swap_sem, 2, other),
    ]
    loads = [
        pltpu.make_async_copy(out.at[:, c], out_mine, own_sem.at[0]),
        pltpu.make_async_copy(wide.at[:, :, c], wide_mine, own_sem.at[1]),
        pltpu.make_async_copy(gain.at[:, :, c], gain_mine, own_sem.at[2]),
    ]
    for copy in swaps + loads:
        copy.start()

    def rows_copy(p):
        to = (d + p) % dp_size
        return remote(rows.at[to], rows_out.at[d], rows_sem, p, device(to, z, c))

    loop(1, dp_size, lambda p: rows_copy(p).start())
    rows_in = pltpu.make_async_copy(rows.at[d], rows_own, own_sem.at[3])
    rows_in.start()

    def out_copy(p):
        to = (z + p) % z_size
        return remote(out_mine.at[to], out_out.at[z], out_sem, p, device(d, to, c))

    def target(p):
        return (d + p // z_size) % dp_size, (z + p % z_size) % z_size

    def wide_copy(p):
        to_d, to_z = target(p)
        return remote(
            wide_mine.at[to_d, to_z], wide_out.at[d, z], wide_sem, p, device(to_d, to_z, c)
        )

    def gain_copy(p):
        to_d, to_z = target(p)
        return remote(
            gain_mine.at[to_d, to_z], gain_out.at[d, z], gain_sem, p, device(to_d, to_z, c)
        )

    def add_out(p):
        to = (z + p) % z_size
        out_mine[to] = (out_mine[to].astype(F32) + out_theirs[to].astype(F32)).astype(BF)

    def add_wide(p):
        to_d, to_z = target(p)
        total = wide_mine[to_d, to_z].astype(F32) + wide_theirs[to_d, to_z].astype(F32)
        wide_mine[to_d, to_z] = total.astype(BF)
        gain_mine[to_d, to_z] = gain_mine[to_d, to_z] + gain_theirs[to_d, to_z]

    swaps[0].wait()
    loads[0].wait()

    def send_out(p):
        add_out(p)
        out_copy(p).start()

    loop(1, z_size, send_out)
    add_out(0)
    for copy in swaps[1:] + loads[1:]:
        copy.wait()

    def send_wide(p):
        add_wide(p)
        wide_copy(p).start()
        gain_copy(p).start()

    loop(1, chips, send_wide)
    add_wide(0)
    rows_in.wait()
    own = [
        pltpu.make_async_copy(rows_own, rows_out.at[d], own_sem.at[4]),
        pltpu.make_async_copy(out_mine.at[z], out_out.at[z], own_sem.at[5]),
        pltpu.make_async_copy(wide_mine.at[d, z], wide_out.at[d, z], own_sem.at[6]),
        pltpu.make_async_copy(gain_mine.at[d, z], gain_out.at[d, z], own_sem.at[7]),
    ]
    for copy in own:
        copy.start()
    for copy in own:
        copy.wait()
    loop(1, dp_size, lambda p: rows_copy(p).wait())
    loop(1, z_size, lambda p: out_copy(p).wait())
    loop(1, chips, lambda p: wide_copy(p).wait())
    loop(1, chips, lambda p: gain_copy(p).wait())


def turned(value):
    lane = lax.broadcasted_iota(jnp.int32, value.shape, 1)
    ahead, behind = pltpu.roll(value, 128 - HEAD_DIM // 2, 1), pltpu.roll(value, HEAD_DIM // 2, 1)
    return jnp.where(lane % HEAD_DIM < HEAD_DIM // 2, ahead, behind)


def low_lanes(value):
    lane = lax.broadcasted_iota(jnp.int32, value.shape, 1)
    return jnp.where(lane < HEAD_DIM, value, jnp.zeros_like(value))


def high_lanes(value):
    lane = lax.broadcasted_iota(jnp.int32, value.shape, 1)
    return jnp.where(lane < HEAD_DIM, jnp.zeros_like(value), value)


def both_sides(value):
    low = low_lanes(value)
    return low, pltpu.roll(low, HEAD_DIM, 1)


def attend_forward(sizes, *refs):
    xs, gain, mask, cosine, sine, wides, out, pair = refs[:8]
    rows_out, pair_out, probs, query_out, keyval_out, mixed_out, act_out = refs[8:15]
    parts, pair_own, rows_sem, pair_sem, own_sem = refs[15:]
    dp_size, z_size = sizes
    f_size = 2 * z_size
    d, z, c = place()
    f = 2 * z + c
    pairs = query_out.shape[2] // 128
    greet(sizes, along_dp=True, along_fsdp=True)

    def pair_copy(p):
        to = (f + p) % f_size
        return remote(pair.at[to], pair_out.at[f], pair_sem, p, {"dp": d, "fsdp": to})

    def rows_copy(p):
        to = (d + p) % dp_size
        return remote(parts.at[to], rows_out.at[d], rows_sem, p, device(to, z, c))

    loop(1, f_size, lambda p: pair_copy(p).start())
    take = pltpu.make_async_copy(pair.at[f], pair_own, own_sem.at[0])
    take.start()
    take.wait()
    give = pltpu.make_async_copy(pair_own, pair_out.at[f], own_sem.at[1])
    give.start()

    def block(g):
        source = xs[g].astype(F32)
        inverse = lax.rsqrt(jnp.mean(source * source, axis=1, keepdims=True) + EPSILON)
        act = (source * inverse * gain[...]).astype(BF)
        act_out[g] = act
        rows = matmul(act, wides[...])
        cosine_table, sine_table = cosine[g], sine[g]
        keyval = rows[:, pairs * 128 :]
        key = (keyval * cosine_table + turned(keyval) * sine_table).astype(BF).astype(F32)
        value = keyval.astype(BF).astype(F32)
        keyval_out[g] = jnp.where(
            lax.broadcasted_iota(jnp.int32, key.shape, 1) < HEAD_DIM, key, value
        ).astype(BF)
        keys = [side.astype(BF) for side in both_sides(key)]
        values = [side.astype(BF) for side in both_sides(pltpu.roll(value, HEAD_DIM, 1))]
        allowed = mask[g] > 0
        for pair_index in range(pairs):
            lanes = pl.ds(pair_index * 128, 128)
            query = rows[:, pair_index * 128 : pair_index * 128 + 128]
            query = (query * cosine_table + turned(query) * sine_table).astype(BF)
            query_out[g, :, lanes] = query
            mixed = jnp.zeros(query.shape, F32)
            for side in range(2):
                raw = times_trans(query, keys[side])
                scores = jnp.where(allowed, raw * HEAD_DIM ** (-0.5), -1e30)
                powers = jnp.exp(scores - jnp.max(scores, axis=1, keepdims=True))
                weights = powers / jnp.sum(powers, axis=1, keepdims=True)
                probs[g, 2 * pair_index + side] = weights
                mixed += matmul(weights.astype(BF), values[side])
            mixed_out[g, :, lanes] = mixed.astype(BF)
        parts[g] = matmul(mixed_out[g], out[...]).astype(BF)

    def send(p):
        block((d + p) % dp_size)

        @pl.when(p < dp_size)
        def _():
            rows_copy(p).start()

    loop(1, dp_size + 1, send)
    own = pltpu.make_async_copy(parts.at[d], rows_out.at[d], own_sem.at[2])
    own.start()
    own.wait()
    give.wait()
    loop(1, dp_size, lambda p: rows_copy(p).wait())
    loop(1, f_size, lambda p: pair_copy(p).wait())


def attend_backward(sizes, *refs):
    rows, xs, cosine, sine, wides, out, probs, query_in, keyval_in, pair = refs[:10]
    rows_out, pair_out, grad_wide, grad_act, gain_grad = refs[10:15]
    held, pair_own, rows_sem, pair_sem, own_sem, out_sem = refs[15:]
    dp_size, z_size = sizes
    f_size = 2 * z_size
    d, z, c = place()
    f = 2 * z + c
    pairs = query_in.shape[2] // 128
    greet(sizes, along_dp=True, along_fsdp=True)

    def pair_copy(p):
        to = (f + p) % f_size
        return remote(pair.at[to], pair_out.at[f], pair_sem, p, {"dp": d, "fsdp": to})

    def rows_copy(p):
        return remote(rows, held.at[d], rows_sem, p, device((d + p) % dp_size, z, c))

    loop(1, dp_size, lambda p: rows_copy(p).start())
    loop(1, f_size, lambda p: pair_copy(p).start())
    take = pltpu.make_async_copy(pair.at[f], pair_own, own_sem.at[0])
    take.start()
    own = pltpu.make_async_copy(rows, held.at[d], own_sem.at[2])
    own.start()
    take.wait()
    give = pltpu.make_async_copy(pair_own, pair_out.at[f], own_sem.at[1])
    give.start()
    gain_grad[...] = jnp.zeros_like(gain_grad)

    def keep(p):
        g = (d - p + dp_size) % dp_size
        return pltpu.make_async_copy(held.at[g], rows_out.at[g], out_sem.at[p])

    def block(g):
        grad_mixed = times_trans(held[g], out[...]).astype(BF)
        cosine_table, sine_table = cosine[g], sine[g]
        keyval = keyval_in[g].astype(F32)
        keys = [side.astype(BF) for side in both_sides(keyval)]
        values = [side.astype(BF) for side in both_sides(pltpu.roll(keyval, HEAD_DIM, 1))]
        key_sums = [jnp.zeros(keyval.shape, F32), jnp.zeros(keyval.shape, F32)]
        value_sums = [jnp.zeros(keyval.shape, F32), jnp.zeros(keyval.shape, F32)]
        for pair_index in range(pairs):
            lanes = pl.ds(pair_index * 128, 128)
            up = grad_mixed[:, pair_index * 128 : pair_index * 128 + 128]
            query = query_in[g, :, lanes]
            grad_query = jnp.zeros(query.shape, F32)
            for side in range(2):
                weights = probs[g, 2 * pair_index + side]
                grad_probs = times_trans(up, values[side])
                value_sums[side] += outer_sum(weights.astype(BF), up)
                inner = jnp.sum(weights * grad_probs, axis=1, keepdims=True)
                grad_raw = (HEAD_DIM ** (-0.5) * weights * (grad_probs - inner)).astype(BF)
                grad_query += matmul(grad_raw, keys[side])
                key_sums[side] += outer_sum(grad_raw, query)
            grad_query = grad_query * cosine_table - turned(grad_query) * sine_table
            grad_wide[g, :, lanes] = grad_query.astype(BF)
        grad_key = key_sums[0] + pltpu.roll(key_sums[1], HEAD_DIM, 1)
        grad_key = grad_key * cosine_table - turned(grad_key) * sine_table
        grad_value = value_sums[1] + pltpu.roll(value_sums[0], HEAD_DIM, 1)
        lane = lax.broadcasted_iota(jnp.int32, grad_key.shape, 1)
        grad_wide[g, :, pl.ds(pairs * 128, 128)] = jnp.where(
            lane < HEAD_DIM, grad_key, grad_value
        ).astype(BF)
        grad = times_trans(grad_wide[g], wides[...])
        grad_act[g] = grad.astype(BF)
        source = xs[g].astype(F32)
        inverse = lax.rsqrt(jnp.mean(source * source, axis=1, keepdims=True) + EPSILON)
        gain_grad[...] += jnp.sum(source * inverse * grad, axis=0, keepdims=True)

    def arrive(p):
        @pl.when(p == 0)
        def _():
            own.wait()

        @pl.when(p > 0)
        def _():
            rows_copy(p).wait_recv()

        keep(p).start()
        block((d - p + dp_size) % dp_size)

    loop(0, dp_size, arrive)
    give.wait()
    loop(0, dp_size, lambda p: keep(p).wait())
    loop(1, dp_size, lambda p: rows_copy(p).wait_send())
    loop(1, f_size, lambda p: pair_copy(p).wait())


def pack_kernel(counts, gate, up, packed):
    dp_size, fs_size, unit = counts
    for f in range(fs_size):
        pieces = []
        for weight in (gate, up):
            for g in range(dp_size):
                low = (g * fs_size + f) * unit
                pieces.append(weight[:, low : low + unit].astype(F32))
        packed[f] = jnp.concatenate(pieces, axis=1).astype(BF)


def unpack_kernel(counts, packed, gate, up):
    dp_size, fs_size, unit = counts
    for half, grad in enumerate((gate, up)):
        for g in range(dp_size):
            low = (half * dp_size + g) * unit
            pieces = [packed[f, :, low : low + unit].astype(F32) for f in range(fs_size)]
            grad[:, g * fs_size * unit : (g + 1) * fs_size * unit] = jnp.concatenate(
                pieces, axis=1
            )


def small_call(kernel, outs, *args):
    return pl.pallas_call(
        kernel,
        out_shape=tuple(jax.ShapeDtypeStruct(shape, dtype) for shape, dtype in outs),
        cost_estimate=pl.CostEstimate(flops=int(3e9), bytes_accessed=0, transcendentals=0),
    )(*args)


def local(
    dp_size,
    fs_size,
    inputs,
    segment_ids,
    attn_gain,
    query_weight,
    key_weight,
    value_weight,
    output_weight,
    mlp_gain,
    gate_weight,
    up_weight,
    down_weight,
    cotangent,
):
    z_size = fs_size // 2
    sizes = (dp_size, z_size)
    row_count, width = inputs.shape
    weight_rows, ff_width = gate_weight.shape
    unit = down_weight.shape[0]
    share = dp_size * unit
    heads = HEADS // dp_size
    query_width = heads * HEAD_DIM
    wide_width = query_width + 2 * HEAD_DIM
    vmem, hbm = pltpu.VMEM, pltpu.HBM

    counts = (dp_size, fs_size, unit)
    pair_shape = (fs_size, weight_rows, 2 * share)
    (pair,) = small_call(
        functools.partial(pack_kernel, counts), [(pair_shape, BF)], gate_weight, up_weight
    )
    down_full = gather(down_weight, "dp")
    def by_head(weight):
        return weight.reshape(weight_rows, dp_size, -1).transpose(1, 0, 2)

    wide = jnp.concatenate(
        [by_head(query_weight), by_head(key_weight), by_head(value_weight)], axis=2
    )
    gain = jnp.concatenate([attn_gain, mlp_gain, jnp.zeros((128 - 2 * weight_rows,), BF)])
    gain = jnp.broadcast_to(gain[None, :], (16, 128))
    seg = jnp.broadcast_to(segment_ids[None, :], (8, row_count))
    chips = dp_size * z_size
    xs, segs, gains, wides, out_full = call(
        start_kernel,
        sizes,
        0,
        60,
        [
            ((dp_size, row_count, width), BF),
            ((dp_size, 8, row_count), jnp.int32),
            ((dp_size, fs_size, 16, 128), BF),
            ((dp_size, fs_size, weight_rows, wide_width), BF),
            ((fs_size, weight_rows, width), BF),
        ],
        [
            dma(2, dp_size),
            dma(2, dp_size),
            dma(2, chips),
            dma(2, dp_size),
            dma(2, z_size + 1),
            dma(2, z_size + 1),
            dma(2, chips),
            dma(2, z_size),
            dma(2, z_size),
            dma(5),
        ],
        [vmem] * 5,
        inputs,
        seg,
        gain,
        wide,
        output_weight,
    )
    gains = gains[:, :, 0, :].astype(F32)
    gain_one = gains[:, :, :weight_rows].reshape(width)
    gain_two = gains[:, :, weight_rows : 2 * weight_rows].reshape(width)
    wides = wides.reshape(width, wide_width)
    out_full = out_full.reshape(query_width, width)

    segs = segs[:, 0, :]
    cosine_table, sine_table = jax.vmap(rotary_tables)(segs)
    row_index = jnp.arange(row_count, dtype=jnp.int32)
    allowed = (segs[:, :, None] == segs[:, None, :]) & (
        row_index[:, None] >= row_index[None, :]
    )
    mask = allowed.astype(F32)
    by_row = (dp_size, row_count)
    rows_shape = by_row + (width,)
    cross_sems = [dma(2, dp_size), dma(2, fs_size), dma(3)]
    mixed_parts, pair_rows, probs, query_rot, keyval, mixed_low, act_one = call(
        attend_forward,
        sizes,
        1,
        40,
        [
            (rows_shape, BF),
            (pair_shape, BF),
            ((dp_size, heads, row_count, row_count), F32),
            (by_row + (query_width,), BF),
            (by_row + (128,), BF),
            (by_row + (query_width,), BF),
            (rows_shape, BF),
        ],
        [pltpu.VMEM(rows_shape, BF), pltpu.VMEM(pair_shape[1:], BF)] + cross_sems,
        [vmem] * 7 + [hbm],
        xs,
        gain_one[None, :],
        mask,
        cosine_table,
        sine_table,
        wides,
        out_full,
        pair,
        kept=5,
    )
    mixed_low = mixed_low.reshape(dp_size * row_count, query_width)
    act_one = act_one.reshape(dp_size * row_count, width)
    mixed_parts, cot_late = lax.optimization_barrier((mixed_parts, cotangent))
    cot_full = gather(cot_late, "fsdp")
    source = inputs.astype(F32)
    residual = source + jnp.sum(mixed_parts.astype(F32), axis=0)
    inverse_two = lax.rsqrt(jnp.mean(residual * residual, axis=1, keepdims=True) + EPSILON)
    normed_two = residual * inverse_two
    act_two = (normed_two * gain_two).astype(BF)
    pair_rows = pair_rows.reshape(fs_size * weight_rows, 2 * share)
    act_full, pair_full = call(
        gather_line,
        sizes,
        2,
        55,
        [((fs_size, row_count, width), BF), ((dp_size,) + pair_rows.shape, BF)],
        [
            pltpu.VMEM(pair_rows.shape, BF),
            dma(2, z_size + 1),
            dma(2, z_size),
            dma(2, 4),
            dma(3),
        ],
        [vmem, hbm],
        act_two,
        pair_rows,
    )
    pair_full = pair_full.reshape(width, 2 * share)
    act_full = act_full.reshape(fs_size * row_count, width)

    both = matmul(act_full, pair_full)
    gate_value, up_value = both[:, :share], both[:, share:]
    sigmoid_gate = jax.nn.sigmoid(gate_value)
    hidden_low = (gate_value * sigmoid_gate * up_value).astype(BF)
    grad_hidden = times_trans(cot_full, down_full)
    grad_gate = (
        grad_hidden * up_value * sigmoid_gate * (1.0 + gate_value * (1.0 - sigmoid_gate))
    ).astype(BF)
    grad_up = (grad_hidden * gate_value * sigmoid_gate).astype(BF)
    grad_both = jnp.concatenate([grad_gate, grad_up], axis=1)
    grad_part = times_trans(grad_both, pair_full).astype(BF)
    pair_grad = outer_sum(act_full, grad_both).astype(BF)
    mlp_part = matmul(hidden_low, down_full).astype(BF)
    pair_parts_shape = (dp_size, fs_size * weight_rows, 2 * share)
    grad_parts, pair_parts = call(
        scatter_line,
        sizes,
        3,
        65,
        [((z_size, row_count, width), BF), (pair_parts_shape, BF)],
        [
            pltpu.VMEM((z_size, row_count, width), BF),
            pltpu.VMEM((z_size, row_count, width), BF),
            pltpu.VMEM(pair_parts_shape[1:], BF),
            dma(2, z_size),
            dma(2, z_size),
            dma(z_size),
            dma(3),
            dma(2, dp_size),
        ],
        [hbm, hbm],
        grad_part.reshape(z_size, 2, row_count, width),
        pair_grad.reshape(pair_parts_shape),
    )
    pair_grad = jnp.sum(pair_parts.astype(F32), axis=0).astype(BF)
    mlp_part, grad_parts = lax.optimization_barrier((mlp_part, grad_parts))
    mlp_out = scatter_sum(mlp_part, "fsdp")

    grad_act_two = jnp.sum(grad_parts.astype(F32), axis=0)
    mlp_gain_grad = jnp.sum(normed_two * grad_act_two, axis=0)
    grad_residual = cotangent.astype(F32) + norm_back(
        grad_act_two, normed_two, inverse_two, gain_two
    )
    grad_attn, pair_back, grad_wide, grad_act, gain_grad = call(
        attend_backward,
        sizes,
        4,
        40,
        [
            (rows_shape, BF),
            (pair_shape, BF),
            (by_row + (wide_width,), BF),
            (rows_shape, BF),
            ((1, width), F32),
        ],
        [pltpu.VMEM(rows_shape, BF), pltpu.VMEM(pair_shape[1:], BF)]
        + cross_sems
        + [dma(dp_size)],
        [vmem] * 9 + [hbm],
        grad_residual.astype(BF),
        xs,
        cosine_table,
        sine_table,
        wides,
        out_full,
        probs,
        query_rot,
        keyval,
        pair_grad.reshape(pair_shape),
        kept=3,
    )
    hidden_low, grad_attn, mlp_out = lax.optimization_barrier((hidden_low, grad_attn, mlp_out))
    outputs = (residual + mlp_out.astype(F32)).astype(BF)
    down_grad = scatter_sum(outer_sum(hidden_low, cot_full).astype(BF), "dp").astype(F32)
    gate_grad, up_grad = small_call(
        functools.partial(unpack_kernel, counts), [(gate_weight.shape, F32)] * 2, pair_back
    )
    grad_attn = grad_attn.reshape(dp_size * row_count, width)
    output_grad = outer_sum(mixed_low, grad_attn).astype(BF)
    grad_wide = grad_wide.reshape(dp_size * row_count, wide_width)
    wide_grad = outer_sum(act_one, grad_wide).astype(BF)
    by_owner = (dp_size, fs_size, weight_rows)
    gain_grads = jnp.concatenate(
        [
            gain_grad.reshape(by_owner),
            mlp_gain_grad.reshape(by_owner),
            jnp.zeros((dp_size, fs_size, 128 - 2 * weight_rows), F32),
        ],
        axis=2,
    )
    gain_grads = jnp.broadcast_to(gain_grads[:, :, None, :], (dp_size, fs_size, 8, 128))
    wide_half = (dp_size, z_size, weight_rows, wide_width)
    out_half = (z_size, weight_rows, width)
    gain_half = (dp_size, z_size, 8, 128)
    grad_act_parts, wide_parts, out_parts, gain_parts = call(
        end_kernel,
        sizes,
        5,
        60,
        [(rows_shape, BF), (wide_half, BF), (out_half, BF), (gain_half, F32)],
        [
            pltpu.VMEM((row_count, width), BF),
            pltpu.VMEM(wide_half, BF),
            pltpu.VMEM(wide_half, BF),
            pltpu.VMEM(out_half, BF),
            pltpu.VMEM(out_half, BF),
            pltpu.VMEM(gain_half, F32),
            pltpu.VMEM(gain_half, F32),
            dma(2, dp_size),
            dma(2, chips),
            dma(2, z_size),
            dma(2, chips),
            dma(2, 3),
            dma(8),
        ],
        [hbm] * 4,
        grad_act,
        wide_grad.reshape(dp_size, z_size, 2, weight_rows, wide_width),
        output_grad.reshape(z_size, 2, weight_rows, width),
        gain_grads.reshape(dp_size, z_size, 2, 8, 128),
    )
    grad_act_one = jnp.sum(grad_act_parts.astype(F32), axis=0)
    own_inverse = lax.rsqrt(jnp.mean(source * source, axis=1, keepdims=True) + EPSILON)
    input_grad = (
        grad_residual + norm_back(grad_act_one, source * own_inverse, own_inverse, gain_one)
    ).astype(BF)
    gain_total = jnp.sum(gain_parts[:, :, 0, :], axis=(0, 1))
    wide_total = jnp.sum(wide_parts.astype(F32), axis=1)

    def from_heads(value):
        return value.transpose(1, 0, 2).reshape(weight_rows, -1)

    return (
        outputs,
        input_grad,
        gain_total[:weight_rows],
        from_heads(wide_total[:, :, :query_width]),
        from_heads(wide_total[:, :, query_width : query_width + HEAD_DIM]),
        from_heads(wide_total[:, :, query_width + HEAD_DIM :]),
        jnp.sum(out_parts.astype(F32), axis=0),
        gain_total[weight_rows : 2 * weight_rows],
        gate_grad,
        up_grad,
        down_grad,
    )


def solution(mesh):
    dp_size, fs_size = mesh.shape["dp"], mesh.shape["fsdp"]
    row = P(ALL, None)
    flat = P(ALL)

    def step(*args):
        return local(dp_size, fs_size, *args)

    return jax.shard_map(
        step,
        mesh=mesh,
        in_specs=(row, flat, flat, row, row, row, row, flat, row, row, row, row),
        out_specs=(row, row, flat, row, row, row, row, flat, row, row, row),
        check_vma=False,
    )
```

```python
import functools

import jax
import jax.numpy as jnp
from jax import lax
from jax.experimental import pallas as pl
from jax.experimental.pallas import tpu as pltpu
from jax.sharding import PartitionSpec as P

HEADS = 32
HEAD_DIM = 64
KV_HEADS = 4
EPSILON = 1e-05
ALL = ("dp", "fsdp")
BF = jnp.bfloat16
F32 = jnp.float32
MESH = pl.DeviceIdType.MESH


def matmul(left_side, right_side):
    return jnp.dot(left_side, right_side, preferred_element_type=F32)


def outer_sum(left_side, right_side):
    return lax.dot_general(
        left_side, right_side, (((0,), (0,)), ((), ())), preferred_element_type=F32
    )


def times_trans(left_side, right_side):
    return lax.dot_general(
        left_side, right_side, (((1,), (1,)), ((), ())), preferred_element_type=F32
    )


def rotary_tables(segments):
    row_count = segments.shape[0]
    row_index = jnp.arange(row_count, dtype=jnp.int32)
    earlier = jnp.sum((segments[None, :] < segments[:, None]).astype(jnp.int32), axis=1)
    places = (row_index - earlier).astype(F32)
    halfway = HEAD_DIM // 2
    frequency = 10000.0 ** (jnp.arange(halfway, dtype=F32) * (-2.0 / HEAD_DIM))
    angles = places[:, None] * frequency[None, :]
    cosine_table, sine_table = jnp.cos(angles), jnp.sin(angles)
    pairs = 128 // HEAD_DIM
    return (
        jnp.concatenate([cosine_table, cosine_table] * pairs, axis=1),
        jnp.concatenate([-sine_table, sine_table] * pairs, axis=1),
    )


def norm_back(upstream, normed, inverse, gain_vec):
    scaled = upstream * gain_vec
    return inverse * (scaled - normed * jnp.mean(scaled * normed, axis=1, keepdims=True))


def gather(value, axes):
    return lax.all_gather(value, axes, axis=0, tiled=True)


def scatter_sum(value, axes):
    return lax.psum_scatter(value, axes, scatter_dimension=0, tiled=True)


def place():
    d, f = lax.axis_index("dp"), lax.axis_index("fsdp")
    return d, f // 2, f % 2


def device(d, z, c):
    return {"dp": d, "fsdp": 2 * z + c}


def remote(src, dst, sems, index, target):
    return pltpu.make_async_remote_copy(
        src_ref=src,
        dst_ref=dst,
        send_sem=sems.at[0, index],
        recv_sem=sems.at[1, index],
        device_id=target,
        device_id_type=MESH,
    )


def hop(src, dst, sems, send, recv, target):
    return pltpu.make_async_remote_copy(
        src_ref=src,
        dst_ref=dst,
        send_sem=sems.at[0, send],
        recv_sem=sems.at[1, recv],
        device_id=target,
        device_id_type=MESH,
    )


def chain(z_size, shard, sems, first):
    d, z, c = place()

    def copy(s, to, send=None, src=None):
        src = shard(s) if src is None else src
        return hop(src, shard(s), sems, s if send is None else send, s, device(d, to, c))

    up, down = z < z_size - 1, z > 0

    def start():
        @pl.when(up)
        def _():
            copy(z, z + 1, src=first).start()

        @pl.when(down)
        def _():
            copy(z, z - 1, z_size, first).start()

    def go(arrived, low=1, high=z_size):
        def step(k):
            @pl.when(z - k >= 0)
            def _():
                copy(z - k, z).wait_recv()

                @pl.when(up)
                def _():
                    copy(z - k, z + 1).start()

                arrived(z - k)

            @pl.when(z + k < z_size)
            def _():
                copy(z + k, z).wait_recv()

                @pl.when(down)
                def _():
                    copy(z + k, z - 1).start()

                arrived(z + k)

        loop(low, high, step)

    def finish():
        @pl.when(up)
        def _():
            copy(z, z + 1, src=first).wait_send()

        @pl.when(down)
        def _():
            copy(z, z - 1, z_size, first).wait_send()

        def step(k):
            @pl.when((z - k >= 0) & up)
            def _():
                copy(z - k, z + 1).wait_send()

            @pl.when((z + k < z_size) & down)
            def _():
                copy(z + k, z - 1).wait_send()

        loop(1, z_size, step)

    return start, go, finish


def ring_place(q, size):
    q = (q + size) % size
    return q + (q // 2) * (1 - 2 * (q % 2)) if size == 4 else q


def loop(low, high, body):
    def step(index, carry):
        body(index)
        return carry

    lax.fori_loop(low, high, step, 0)


def greet(sizes, same_core=False, along_dp=False, along_fsdp=False, partner=False):
    dp_size, z_size = sizes
    d, z, c = place()
    barrier = pltpu.get_barrier_semaphore()

    def signal(target):
        pl.semaphore_signal(barrier, inc=1, device_id=target, device_id_type=MESH)

    count = 0
    if same_core:

        def to_chip(p):
            signal(device((d + p // z_size) % dp_size, (z + p % z_size) % z_size, c))

        loop(1, dp_size * z_size, to_chip)
        count += dp_size * z_size - 1
    if along_dp:
        loop(1, dp_size, lambda p: signal(device((d + p) % dp_size, z, c)))
        count += dp_size - 1
    if along_fsdp:
        f_size = 2 * z_size

        def to_line(p):
            signal({"dp": d, "fsdp": (2 * z + c + p) % f_size})

        loop(1, f_size, to_line)
        count += f_size - 1
    if partner:
        signal(device(d, z, 1 - c))
        count += 1
    pl.semaphore_wait(barrier, count)


def call(kernel, sizes, number, micros, outs, scratch, spaces, *args, kept=0):
    far = len(outs) - kept
    return pl.pallas_call(
        functools.partial(kernel, sizes),
        out_shape=tuple(jax.ShapeDtypeStruct(shape, dtype) for shape, dtype in outs),
        in_specs=[pl.BlockSpec(memory_space=space) for space in spaces],
        out_specs=tuple(
            pl.BlockSpec(memory_space=pltpu.HBM if k < far else pltpu.VMEM)
            for k in range(len(outs))
        ),
        scratch_shapes=scratch,
        compiler_params=pltpu.CompilerParams(collective_id=number, has_side_effects=True),
        cost_estimate=pl.CostEstimate(
            flops=int(micros * 1e9), bytes_accessed=0, transcendentals=0
        ),
        name=kernel.__name__,
    )(*args)


def dma(*shape):
    return pltpu.SemaphoreType.DMA(shape)


def start_kernel(sizes, x, seg, gain, wide, out, xs, segs, gains, wides, outs, *sems):
    x_sem, seg_sem, gain_sem, piece_sem, wide_sem, out_sem = sems[:6]
    gain_fwd, wide_fwd, out_fwd, own_sem = sems[6:]
    dp_size, z_size = sizes
    chips = dp_size * z_size
    d, z, c = place()
    f = 2 * z + c
    greet(sizes, same_core=True, partner=True)
    other = device(d, z, 1 - c)

    def piece_copy(p):
        to = (d + p) % dp_size
        return remote(wide.at[to], wides.at[d, f], piece_sem, p, device(to, z, c))

    def gain_copy(p):
        to_d, to_z = (d + p // z_size) % dp_size, (z + p % z_size) % z_size
        return remote(gain, gains.at[d, f], gain_sem, p, device(to_d, to_z, c))

    def x_copy(p):
        return remote(x, xs.at[d], x_sem, p, device((d + p) % dp_size, z, c))

    def seg_copy(p):
        return remote(seg, segs.at[d], seg_sem, p, device((d + p) % dp_size, z, c))

    def out_pass(s):
        slot = outs.at[2 * s + c]
        return remote(slot, slot, out_fwd, s, other)

    def wide_pass(s):
        slot = wides.at[:, 2 * s + c]
        return remote(slot, slot, wide_fwd, s, other)

    def gain_pass(p):
        from_d = (d - p // z_size + dp_size) % dp_size
        slot = gains.at[from_d, 2 * ((z - p % z_size + z_size) % z_size) + c]
        return remote(slot, slot, gain_fwd, p, other)

    out_start, out_go, out_finish = chain(z_size, lambda s: outs.at[2 * s + c], out_sem, out)
    wide_start, wide_go, wide_finish = chain(
        z_size, lambda s: wides.at[:, 2 * s + c], wide_sem, wides.at[:, f]
    )
    own = [
        pltpu.make_async_copy(wide.at[d], wides.at[d, f], own_sem.at[0]),
        pltpu.make_async_copy(x, xs.at[d], own_sem.at[1]),
        pltpu.make_async_copy(seg, segs.at[d], own_sem.at[2]),
        pltpu.make_async_copy(gain, gains.at[d, f], own_sem.at[3]),
        pltpu.make_async_copy(out, outs.at[f], own_sem.at[4]),
    ]
    loop(1, dp_size, lambda p: piece_copy(p).start())
    for copy in own:
        copy.start()
    out_start()
    loop(1, chips, lambda p: gain_copy(p).start())
    loop(1, dp_size, lambda p: seg_copy(p).start())
    loop(1, dp_size, lambda p: x_copy(p).start())
    passed = [
        remote(gain, gains.at[d, f], gain_fwd, 0, other),
        remote(out, outs.at[f], out_fwd, z, other),
    ]
    for copy in passed:
        copy.start()
    own[0].wait()
    loop(1, dp_size, lambda p: piece_copy(p).wait())
    wide_start()
    wide_pass(z).start()
    out_go(lambda s: out_pass(s).start())
    wide_go(lambda s: wide_pass(s).start())

    def pass_gain(p):
        gain_copy(p).wait_recv()
        gain_pass(p).start()

    loop(1, chips, pass_gain)
    loop(1, dp_size, lambda p: seg_copy(p).wait())
    loop(1, dp_size, lambda p: x_copy(p).wait())
    for copy in own[1:]:
        copy.wait()
    for copy in passed:
        copy.wait()
    wide_pass(z).wait()

    def end_pass(k):
        s = (z + k) % z_size
        out_pass(s).wait()
        wide_pass(s).wait()

    loop(1, z_size, end_pass)
    loop(1, chips, lambda p: gain_pass(p).wait())
    loop(1, chips, lambda p: gain_copy(p).wait_send())
    out_finish()
    wide_finish()


def gather_line(sizes, rows, pair, rows_out, pair_out, bounce, *sems):
    rows_sem, pass_sem, pair_sem, own_sem = sems
    dp_size, z_size = sizes
    d, z, c = place()
    f = 2 * z + c
    greet(sizes, along_dp=True, along_fsdp=True)
    q = ring_place(d, dp_size)
    right, left = ring_place(q + 1, dp_size), ring_place(q - 1, dp_size)
    other = device(d, z, 1 - c)
    half = pair.shape[0] // 2

    def rows_pass(s):
        slot = rows_out.at[2 * s + c]
        return remote(slot, slot, pass_sem, s, other)

    def whole_copy(to, index):
        return remote(pair, pair_out.at[d], pair_sem, index, device(to, z, c))

    def half_copy(source, to, low, index):
        slot = pair_out.at[source, pl.ds(low, half)]
        return remote(slot, slot, pair_sem, index, device(to, z, c))

    start, go, finish = chain(z_size, lambda s: rows_out.at[2 * s + c], rows_sem, rows)
    start()
    to_right, to_left = whole_copy(right, 0), whole_copy(left, 1)
    to_right.start()
    to_left.start()
    own = pltpu.make_async_copy(rows, rows_out.at[f], own_sem.at[0])
    own.start()
    passed = remote(rows, rows_out.at[f], pass_sem, z, other)
    passed.start()
    take = pltpu.make_async_copy(pair, bounce, own_sem.at[1])
    take.start()
    take.wait()
    give = pltpu.make_async_copy(bounce, pair_out.at[d], own_sem.at[2])
    give.start()
    go(lambda s: rows_pass(s).start(), 1, z_size - 1)
    to_right.wait_recv()
    on_right = half_copy(left, right, 0, 2)
    on_right.start()
    to_left.wait_recv()
    on_left = half_copy(right, left, half, 3)
    on_left.start()
    go(lambda s: rows_pass(s).start(), z_size - 1)
    give.wait()
    own.wait()
    passed.wait()
    loop(1, z_size, lambda k: rows_pass((z + k) % z_size).wait())
    finish()
    to_right.wait_send()
    to_left.wait_send()
    on_right.wait()
    on_left.wait()


def scatter_line(sizes, *refs):
    part, pair, hid, hid_turned, down, cot = refs[:6]
    part_out, pair_out, mlp_out, grad_out = refs[6:10]
    mine, theirs, got_a, got_b, my_a, my_b, pair_own = refs[10:17]
    hid_v, turned_v, down_v, cot_v, mlp_v, grad_v = refs[17:23]
    part_sem, swap_sem, load_sem, own_sem, pair_sem, mat_sem = refs[23:]
    dp_size, z_size = sizes
    d, z, c = place()
    greet(sizes, along_dp=True, along_fsdp=True)
    other = device(d, z, 1 - c)
    q = ring_place(d, dp_size)
    right, left = ring_place(q + 1, dp_size), ring_place(q - 1, dp_size)
    across = ring_place((q + 2) % dp_size, dp_size)
    to_right, to_left = device(right, z, c), device(left, z, c)
    half = pair.shape[1] // 2
    rows_a, rows_b = pl.ds(0, half), pl.ds(half, half)

    def swap_copy(p):
        to = (z + p) % z_size
        return remote(part.at[to, 1 - c], theirs.at[to], swap_sem, p, other)

    def load(p):
        to = (z + p) % z_size
        return pltpu.make_async_copy(part.at[to, c], mine.at[to], load_sem.at[p])

    def part_copy(p):
        to = (z + p) % z_size
        return remote(mine.at[to], part_out.at[z], part_sem, p, device(d, to, c))

    def begin(p):
        swap_copy(p).start()
        load(p).start()

    def add(p):
        to = (z + p) % z_size
        swap_copy(p).wait()
        load(p).wait()
        mine[to] = (mine[to].astype(F32) + theirs[to].astype(F32)).astype(BF)

    def send(p):
        add(p)
        part_copy(p).start()

    loop(1, z_size, begin)
    begin(0)
    ring = [
        remote(pair.at[across, rows_a], got_a, pair_sem, 0, to_right),
        remote(pair.at[across, rows_b], got_b, pair_sem, 1, to_left),
        remote(pair.at[right, rows_b], pair_out.at[0, rows_b], pair_sem, 2, to_right),
        remote(pair.at[left, rows_a], pair_out.at[1, rows_a], pair_sem, 3, to_left),
        remote(my_a, pair_out.at[0, rows_a], pair_sem, 4, to_right),
        remote(my_b, pair_out.at[1, rows_b], pair_sem, 5, to_left),
    ]
    for copy in ring[:4]:
        copy.start()
    takes = [
        pltpu.make_async_copy(pair.at[right, rows_a], my_a, own_sem.at[1]),
        pltpu.make_async_copy(pair.at[left, rows_b], my_b, own_sem.at[2]),
        pltpu.make_async_copy(pair.at[d], pair_own, own_sem.at[3]),
    ]
    mats = [
        pltpu.make_async_copy(hid, hid_v, mat_sem.at[0]),
        pltpu.make_async_copy(down, down_v, mat_sem.at[1]),
        pltpu.make_async_copy(hid_turned, turned_v, mat_sem.at[2]),
        pltpu.make_async_copy(cot, cot_v, mat_sem.at[3]),
    ]
    loop(1, z_size, send)
    for copy in takes + mats:
        copy.start()
    add(0)
    own = pltpu.make_async_copy(mine.at[z], part_out.at[z], own_sem.at[0])
    own.start()
    takes[2].wait()
    give = pltpu.make_async_copy(pair_own, pair_out.at[2], own_sem.at[4])
    give.start()
    mats[0].wait()
    mats[1].wait()
    tall = 256

    def mlp_tile(i):
        rows = pl.ds(pl.multiple_of(i * tall, tall), tall)
        for low in range(0, mlp_v.shape[1], 512):
            product = matmul(hid_v[rows, :], down_v[:, low : low + 512])
            mlp_v[rows, low : low + 512] = product.astype(BF)

    loop(0, mlp_v.shape[0] // tall, mlp_tile)
    give_mlp = pltpu.make_async_copy(mlp_v, mlp_out, mat_sem.at[4])
    give_mlp.start()

    def merge(total, got):
        def chunk(i):
            rows = pl.ds(pl.multiple_of(i * 32, 32), 32)
            total[rows, :] = (total[rows, :].astype(F32) + got[rows, :].astype(F32)).astype(BF)

        loop(0, half // 32, chunk)

    takes[0].wait()
    ring[0].wait_recv()
    merge(my_a, got_a)
    ring[4].start()
    takes[1].wait()
    ring[1].wait_recv()
    merge(my_b, got_b)
    ring[5].start()
    mats[2].wait()
    mats[3].wait()

    def grad_tile(i):
        lanes = pl.ds(pl.multiple_of(i * 256, 256), 256)
        grad_v[:, lanes] = matmul(turned_v[...], cot_v[:, lanes]).astype(BF)

    loop(0, grad_v.shape[1] // 256, grad_tile)
    give_grad = pltpu.make_async_copy(grad_v, grad_out, mat_sem.at[5])
    give_grad.start()
    own.wait()
    give.wait()
    give_mlp.wait()
    give_grad.wait()
    ring[0].wait_send()
    ring[1].wait_send()
    for copy in ring[2:]:
        copy.wait()
    loop(1, z_size, lambda p: part_copy(p).wait())


def end_kernel(sizes, rows, wide, out, gain, rows_out, wide_out, out_out, gain_out, *scratch):
    rows_own, wide_mine, wide_theirs, out_mine, out_theirs, gain_mine, gain_theirs = scratch[:7]
    rows_sem, wide_sem, out_sem, gain_sem, swap_sem, own_sem = scratch[7:]
    dp_size, z_size = sizes
    chips = dp_size * z_size
    d, z, c = place()
    greet(sizes, same_core=True, partner=True)
    other = device(d, z, 1 - c)
    swaps = [
        remote(out.at[:, 1 - c], out_theirs, swap_sem, 0, other),
        remote(wide.at[:, :, 1 - c], wide_theirs, swap_sem, 1, other),
        remote(gain.at[:, :, 1 - c], gain_theirs, swap_sem, 2, other),
    ]
    loads = [
        pltpu.make_async_copy(out.at[:, c], out_mine, own_sem.at[0]),
        pltpu.make_async_copy(wide.at[:, :, c], wide_mine, own_sem.at[1]),
        pltpu.make_async_copy(gain.at[:, :, c], gain_mine, own_sem.at[2]),
    ]
    for copy in swaps + loads:
        copy.start()

    def rows_copy(p):
        to = (d + p) % dp_size
        return remote(rows.at[to], rows_out.at[d], rows_sem, p, device(to, z, c))

    loop(1, dp_size, lambda p: rows_copy(p).start())
    rows_in = pltpu.make_async_copy(rows.at[d], rows_own, own_sem.at[3])
    rows_in.start()

    def out_copy(p):
        to = (z + p) % z_size
        return remote(out_mine.at[to], out_out.at[z], out_sem, p, device(d, to, c))

    def target(p):
        return (d + p // z_size) % dp_size, (z + p % z_size) % z_size

    def wide_copy(p):
        to_d, to_z = target(p)
        return remote(
            wide_mine.at[to_d, to_z], wide_out.at[d, z], wide_sem, p, device(to_d, to_z, c)
        )

    def gain_copy(p):
        to_d, to_z = target(p)
        return remote(
            gain_mine.at[to_d, to_z], gain_out.at[d, z], gain_sem, p, device(to_d, to_z, c)
        )

    def add_out(p):
        to = (z + p) % z_size
        out_mine[to] = (out_mine[to].astype(F32) + out_theirs[to].astype(F32)).astype(BF)

    def add_wide(p):
        to_d, to_z = target(p)
        total = wide_mine[to_d, to_z].astype(F32) + wide_theirs[to_d, to_z].astype(F32)
        wide_mine[to_d, to_z] = total.astype(BF)
        gain_mine[to_d, to_z] = gain_mine[to_d, to_z] + gain_theirs[to_d, to_z]

    swaps[0].wait()
    loads[0].wait()

    def send_out(p):
        add_out(p)
        out_copy(p).start()

    loop(1, z_size, send_out)
    add_out(0)
    for copy in swaps[1:] + loads[1:]:
        copy.wait()

    def send_wide(p):
        add_wide(p)
        wide_copy(p).start()
        gain_copy(p).start()

    loop(1, chips, send_wide)
    add_wide(0)
    rows_in.wait()
    own = [
        pltpu.make_async_copy(rows_own, rows_out.at[d], own_sem.at[4]),
        pltpu.make_async_copy(out_mine.at[z], out_out.at[z], own_sem.at[5]),
        pltpu.make_async_copy(wide_mine.at[d, z], wide_out.at[d, z], own_sem.at[6]),
        pltpu.make_async_copy(gain_mine.at[d, z], gain_out.at[d, z], own_sem.at[7]),
    ]
    for copy in own:
        copy.start()
    for copy in own:
        copy.wait()
    loop(1, dp_size, lambda p: rows_copy(p).wait())
    loop(1, z_size, lambda p: out_copy(p).wait())
    loop(1, chips, lambda p: wide_copy(p).wait())
    loop(1, chips, lambda p: gain_copy(p).wait())


def turned(value):
    lane = lax.broadcasted_iota(jnp.int32, value.shape, 1)
    ahead, behind = pltpu.roll(value, 128 - HEAD_DIM // 2, 1), pltpu.roll(value, HEAD_DIM // 2, 1)
    return jnp.where(lane % HEAD_DIM < HEAD_DIM // 2, ahead, behind)


def low_lanes(value):
    lane = lax.broadcasted_iota(jnp.int32, value.shape, 1)
    return jnp.where(lane < HEAD_DIM, value, jnp.zeros_like(value))


def high_lanes(value):
    lane = lax.broadcasted_iota(jnp.int32, value.shape, 1)
    return jnp.where(lane < HEAD_DIM, jnp.zeros_like(value), value)


def both_sides(value):
    low = low_lanes(value)
    return low, pltpu.roll(low, HEAD_DIM, 1)


def attend_forward(sizes, *refs):
    xs, gain, mask, cosine, sine, wides, out, pair, down = refs[:9]
    rows_out, pair_out, down_out, probs, query_out, keyval_out, mixed_out, act_out = refs[9:17]
    parts, pair_own, down_own, rows_sem, pair_sem, own_sem, down_sem = refs[17:]
    dp_size, z_size = sizes
    f_size = 2 * z_size
    d, z, c = place()
    f = 2 * z + c
    pairs = query_out.shape[2] // 128
    greet(sizes, along_dp=True, along_fsdp=True)

    def pair_copy(p):
        to = (f + p) % f_size
        return remote(pair.at[to], pair_out.at[f], pair_sem, p, {"dp": d, "fsdp": to})

    def rows_copy(p):
        to = (d + p) % dp_size
        return remote(parts.at[to], rows_out.at[d], rows_sem, p, device(to, z, c))

    def down_copy(p):
        return remote(down, down_out.at[d], down_sem, p, device((d + p) % dp_size, z, c))

    loop(1, f_size, lambda p: pair_copy(p).start())
    loop(1, dp_size, lambda p: down_copy(p).start())
    take = pltpu.make_async_copy(pair.at[f], pair_own, own_sem.at[0])
    take.start()
    take_down = pltpu.make_async_copy(down, down_own, own_sem.at[3])
    take_down.start()
    take.wait()
    give = pltpu.make_async_copy(pair_own, pair_out.at[f], own_sem.at[1])
    give.start()
    take_down.wait()
    give_down = pltpu.make_async_copy(down_own, down_out.at[d], own_sem.at[4])
    give_down.start()

    def block(g):
        source = xs[g].astype(F32)
        inverse = lax.rsqrt(jnp.mean(source * source, axis=1, keepdims=True) + EPSILON)
        act = (source * inverse * gain[...]).astype(BF)
        act_out[g] = act
        rows = matmul(act, wides[...])
        cosine_table, sine_table = cosine[g], sine[g]
        keyval = rows[:, pairs * 128 :]
        key = (keyval * cosine_table + turned(keyval) * sine_table).astype(BF).astype(F32)
        value = keyval.astype(BF).astype(F32)
        keyval_out[g] = jnp.where(
            lax.broadcasted_iota(jnp.int32, key.shape, 1) < HEAD_DIM, key, value
        ).astype(BF)
        keys = [side.astype(BF) for side in both_sides(key)]
        values = [side.astype(BF) for side in both_sides(pltpu.roll(value, HEAD_DIM, 1))]
        allowed = mask[g] > 0
        for pair_index in range(pairs):
            lanes = pl.ds(pair_index * 128, 128)
            query = rows[:, pair_index * 128 : pair_index * 128 + 128]
            query = (query * cosine_table + turned(query) * sine_table).astype(BF)
            query_out[g, :, lanes] = query
            mixed = jnp.zeros(query.shape, F32)
            for side in range(2):
                raw = times_trans(query, keys[side])
                scores = jnp.where(allowed, raw * HEAD_DIM ** (-0.5), -1e30)
                powers = jnp.exp(scores - jnp.max(scores, axis=1, keepdims=True))
                weights = powers / jnp.sum(powers, axis=1, keepdims=True)
                probs[g, 2 * pair_index + side] = weights
                mixed += matmul(weights.astype(BF), values[side])
            mixed_out[g, :, lanes] = mixed.astype(BF)
        parts[g] = matmul(mixed_out[g], out[...]).astype(BF)

    def send(p):
        block((d + p) % dp_size)

        @pl.when(p < dp_size)
        def _():
            rows_copy(p).start()

    loop(1, dp_size + 1, send)
    own = pltpu.make_async_copy(parts.at[d], rows_out.at[d], own_sem.at[2])
    own.start()
    own.wait()
    give.wait()
    give_down.wait()
    loop(1, dp_size, lambda p: rows_copy(p).wait())
    loop(1, dp_size, lambda p: down_copy(p).wait())
    loop(1, f_size, lambda p: pair_copy(p).wait())


def attend_backward(sizes, *refs):
    rows, xs, cosine, sine, wides, out, probs, query_in, keyval_in, pair = refs[:10]
    rows_out, pair_out, grad_wide, grad_act, gain_grad = refs[10:15]
    held, pair_own, rows_sem, pair_sem, own_sem, out_sem = refs[15:]
    dp_size, z_size = sizes
    f_size = 2 * z_size
    d, z, c = place()
    f = 2 * z + c
    pairs = query_in.shape[2] // 128
    greet(sizes, along_dp=True, along_fsdp=True)

    def pair_copy(p):
        to = (f + p) % f_size
        return remote(pair.at[to], pair_out.at[f], pair_sem, p, {"dp": d, "fsdp": to})

    def rows_copy(p):
        return remote(rows, held.at[d], rows_sem, p, device((d + p) % dp_size, z, c))

    loop(1, dp_size, lambda p: rows_copy(p).start())
    loop(1, f_size, lambda p: pair_copy(p).start())
    take = pltpu.make_async_copy(pair.at[f], pair_own, own_sem.at[0])
    take.start()
    own = pltpu.make_async_copy(rows, held.at[d], own_sem.at[2])
    own.start()
    take.wait()
    give = pltpu.make_async_copy(pair_own, pair_out.at[f], own_sem.at[1])
    give.start()
    gain_grad[...] = jnp.zeros_like(gain_grad)

    def keep(p):
        g = (d - p + dp_size) % dp_size
        return pltpu.make_async_copy(held.at[g], rows_out.at[g], out_sem.at[p])

    def block(g):
        grad_mixed = times_trans(held[g], out[...]).astype(BF)
        cosine_table, sine_table = cosine[g], sine[g]
        keyval = keyval_in[g].astype(F32)
        keys = [side.astype(BF) for side in both_sides(keyval)]
        values = [side.astype(BF) for side in both_sides(pltpu.roll(keyval, HEAD_DIM, 1))]
        key_sums = [jnp.zeros(keyval.shape, F32), jnp.zeros(keyval.shape, F32)]
        value_sums = [jnp.zeros(keyval.shape, F32), jnp.zeros(keyval.shape, F32)]
        for pair_index in range(pairs):
            lanes = pl.ds(pair_index * 128, 128)
            up = grad_mixed[:, pair_index * 128 : pair_index * 128 + 128]
            query = query_in[g, :, lanes]
            grad_query = jnp.zeros(query.shape, F32)
            for side in range(2):
                weights = probs[g, 2 * pair_index + side]
                grad_probs = times_trans(up, values[side])
                value_sums[side] += outer_sum(weights.astype(BF), up)
                inner = jnp.sum(weights * grad_probs, axis=1, keepdims=True)
                grad_raw = (HEAD_DIM ** (-0.5) * weights * (grad_probs - inner)).astype(BF)
                grad_query += matmul(grad_raw, keys[side])
                key_sums[side] += outer_sum(grad_raw, query)
            grad_query = grad_query * cosine_table - turned(grad_query) * sine_table
            grad_wide[g, :, lanes] = grad_query.astype(BF)
        grad_key = key_sums[0] + pltpu.roll(key_sums[1], HEAD_DIM, 1)
        grad_key = grad_key * cosine_table - turned(grad_key) * sine_table
        grad_value = value_sums[1] + pltpu.roll(value_sums[0], HEAD_DIM, 1)
        lane = lax.broadcasted_iota(jnp.int32, grad_key.shape, 1)
        grad_wide[g, :, pl.ds(pairs * 128, 128)] = jnp.where(
            lane < HEAD_DIM, grad_key, grad_value
        ).astype(BF)
        grad = times_trans(grad_wide[g], wides[...])
        grad_act[g] = grad.astype(BF)
        source = xs[g].astype(F32)
        inverse = lax.rsqrt(jnp.mean(source * source, axis=1, keepdims=True) + EPSILON)
        gain_grad[...] += jnp.sum(source * inverse * grad, axis=0, keepdims=True)

    def arrive(p):
        @pl.when(p == 0)
        def _():
            own.wait()

        @pl.when(p > 0)
        def _():
            rows_copy(p).wait_recv()

        keep(p).start()
        block((d - p + dp_size) % dp_size)

    loop(0, dp_size, arrive)
    give.wait()
    loop(0, dp_size, lambda p: keep(p).wait())
    loop(1, dp_size, lambda p: rows_copy(p).wait_send())
    loop(1, f_size, lambda p: pair_copy(p).wait())


def pack_kernel(counts, gate, up, packed):
    dp_size, fs_size, unit = counts
    for f in range(fs_size):
        pieces = []
        for weight in (gate, up):
            for g in range(dp_size):
                low = (g * fs_size + f) * unit
                pieces.append(weight[:, low : low + unit].astype(F32))
        packed[f] = jnp.concatenate(pieces, axis=1).astype(BF)


def unpack_kernel(counts, packed, gate, up):
    dp_size, fs_size, unit = counts
    for half, grad in enumerate((gate, up)):
        for g in range(dp_size):
            low = (half * dp_size + g) * unit
            pieces = [packed[f, :, low : low + unit].astype(F32) for f in range(fs_size)]
            grad[:, g * fs_size * unit : (g + 1) * fs_size * unit] = jnp.concatenate(
                pieces, axis=1
            )


def small_call(kernel, outs, *args):
    return pl.pallas_call(
        kernel,
        out_shape=tuple(jax.ShapeDtypeStruct(shape, dtype) for shape, dtype in outs),
        cost_estimate=pl.CostEstimate(flops=int(3e9), bytes_accessed=0, transcendentals=0),
    )(*args)


def local(
    dp_size,
    fs_size,
    inputs,
    segment_ids,
    attn_gain,
    query_weight,
    key_weight,
    value_weight,
    output_weight,
    mlp_gain,
    gate_weight,
    up_weight,
    down_weight,
    cotangent,
):
    z_size = fs_size // 2
    sizes = (dp_size, z_size)
    row_count, width = inputs.shape
    weight_rows, ff_width = gate_weight.shape
    unit = down_weight.shape[0]
    share = dp_size * unit
    heads = HEADS // dp_size
    query_width = heads * HEAD_DIM
    wide_width = query_width + 2 * HEAD_DIM
    vmem, hbm = pltpu.VMEM, pltpu.HBM

    counts = (dp_size, fs_size, unit)
    pair_shape = (fs_size, weight_rows, 2 * share)
    (pair,) = small_call(
        functools.partial(pack_kernel, counts), [(pair_shape, BF)], gate_weight, up_weight
    )
    def by_head(weight):
        return weight.reshape(weight_rows, dp_size, -1).transpose(1, 0, 2)

    wide = jnp.concatenate(
        [by_head(query_weight), by_head(key_weight), by_head(value_weight)], axis=2
    )
    gain = jnp.concatenate([attn_gain, mlp_gain, jnp.zeros((128 - 2 * weight_rows,), BF)])
    gain = jnp.broadcast_to(gain[None, :], (16, 128))
    seg = jnp.broadcast_to(segment_ids[None, :], (8, row_count))
    chips = dp_size * z_size
    xs, segs, gains, wides, out_full = call(
        start_kernel,
        sizes,
        0,
        60,
        [
            ((dp_size, row_count, width), BF),
            ((dp_size, 8, row_count), jnp.int32),
            ((dp_size, fs_size, 16, 128), BF),
            ((dp_size, fs_size, weight_rows, wide_width), BF),
            ((fs_size, weight_rows, width), BF),
        ],
        [
            dma(2, dp_size),
            dma(2, dp_size),
            dma(2, chips),
            dma(2, dp_size),
            dma(2, z_size + 1),
            dma(2, z_size + 1),
            dma(2, chips),
            dma(2, z_size),
            dma(2, z_size),
            dma(5),
        ],
        [vmem] * 5,
        inputs,
        seg,
        gain,
        wide,
        output_weight,
    )
    cot_late, xs = lax.optimization_barrier((cotangent, xs))
    cot_full = gather(cot_late, "fsdp")
    gains = gains[:, :, 0, :].astype(F32)
    gain_one = gains[:, :, :weight_rows].reshape(width)
    gain_two = gains[:, :, weight_rows : 2 * weight_rows].reshape(width)
    wides = wides.reshape(width, wide_width)
    out_full = out_full.reshape(query_width, width)

    segs = segs[:, 0, :]
    cosine_table, sine_table = jax.vmap(rotary_tables)(segs)
    row_index = jnp.arange(row_count, dtype=jnp.int32)
    allowed = (segs[:, :, None] == segs[:, None, :]) & (
        row_index[:, None] >= row_index[None, :]
    )
    mask = allowed.astype(F32)
    by_row = (dp_size, row_count)
    rows_shape = by_row + (width,)
    cross_sems = [dma(2, dp_size), dma(2, fs_size), dma(5)]
    mixed_parts, pair_rows, down_full, probs, query_rot, keyval, mixed_low, act_one = call(
        attend_forward,
        sizes,
        1,
        40,
        [
            (rows_shape, BF),
            (pair_shape, BF),
            ((dp_size,) + down_weight.shape, BF),
            ((dp_size, heads, row_count, row_count), F32),
            (by_row + (query_width,), BF),
            (by_row + (128,), BF),
            (by_row + (query_width,), BF),
            (rows_shape, BF),
        ],
        [
            pltpu.VMEM(rows_shape, BF),
            pltpu.VMEM(pair_shape[1:], BF),
            pltpu.VMEM(down_weight.shape, BF),
        ]
        + cross_sems
        + [dma(2, dp_size)],
        [vmem] * 7 + [hbm] * 2,
        xs,
        gain_one[None, :],
        mask,
        cosine_table,
        sine_table,
        wides,
        out_full,
        pair,
        down_weight,
        kept=5,
    )
    down_full = down_full.reshape(share, width)
    mixed_low = mixed_low.reshape(dp_size * row_count, query_width)
    act_one = act_one.reshape(dp_size * row_count, width)
    source = inputs.astype(F32)
    residual = source + jnp.sum(mixed_parts.astype(F32), axis=0)
    inverse_two = lax.rsqrt(jnp.mean(residual * residual, axis=1, keepdims=True) + EPSILON)
    normed_two = residual * inverse_two
    act_two = (normed_two * gain_two).astype(BF)
    grad_hidden = times_trans(cot_full, down_full)
    act_two, grad_hidden = lax.optimization_barrier((act_two, grad_hidden))
    pair_rows = pair_rows.reshape(fs_size * weight_rows, 2 * share)
    act_full, pair_full = call(
        gather_line,
        sizes,
        2,
        55,
        [((fs_size, row_count, width), BF), ((dp_size,) + pair_rows.shape, BF)],
        [
            pltpu.VMEM(pair_rows.shape, BF),
            dma(2, z_size + 1),
            dma(2, z_size),
            dma(2, 4),
            dma(3),
        ],
        [vmem, hbm],
        act_two,
        pair_rows,
    )
    pair_full = pair_full.reshape(width, 2 * share)
    act_full = act_full.reshape(fs_size * row_count, width)

    both = matmul(act_full, pair_full)
    gate_value, up_value = both[:, :share], both[:, share:]
    sigmoid_gate = jax.nn.sigmoid(gate_value)
    hidden_low = (gate_value * sigmoid_gate * up_value).astype(BF)
    grad_gate = (
        grad_hidden * up_value * sigmoid_gate * (1.0 + gate_value * (1.0 - sigmoid_gate))
    ).astype(BF)
    grad_up = (grad_hidden * gate_value * sigmoid_gate).astype(BF)
    grad_both = jnp.concatenate([grad_gate, grad_up], axis=1)
    grad_part = times_trans(grad_both, pair_full).astype(BF)
    pair_grad = outer_sum(act_full, grad_both).astype(BF)
    pair_block = (fs_size * weight_rows, 2 * share)
    pair_half = (fs_size * weight_rows // 2, 2 * share)
    tokens = fs_size * row_count
    grad_parts, pair_parts, mlp_part, down_part = call(
        scatter_line,
        sizes,
        3,
        60,
        [
            ((z_size, row_count, width), BF),
            ((3,) + pair_block, BF),
            ((tokens, width), BF),
            ((share, width), BF),
        ],
        [pltpu.VMEM((z_size, row_count, width), BF)] * 2
        + [pltpu.VMEM(pair_half, BF)] * 4
        + [
            pltpu.VMEM(pair_block, BF),
            pltpu.VMEM((tokens, share), BF),
            pltpu.VMEM((share, tokens), BF),
            pltpu.VMEM((share, width), BF),
            pltpu.VMEM((tokens, width), BF),
            pltpu.VMEM((tokens, width), BF),
            pltpu.VMEM((share, width), BF),
            dma(2, z_size),
            dma(2, z_size),
            dma(z_size),
            dma(5),
            dma(2, 6),
            dma(6),
        ],
        [hbm] * 6,
        grad_part.reshape(z_size, 2, row_count, width),
        pair_grad.reshape((dp_size,) + pair_block),
        hidden_low,
        hidden_low.T,
        down_full,
        cot_full,
    )
    pair_grad = jnp.sum(pair_parts.astype(F32), axis=0).astype(BF)
    mlp_out = scatter_sum(mlp_part, "fsdp")

    grad_act_two = jnp.sum(grad_parts.astype(F32), axis=0)
    mlp_gain_grad = jnp.sum(normed_two * grad_act_two, axis=0)
    grad_residual = cotangent.astype(F32) + norm_back(
        grad_act_two, normed_two, inverse_two, gain_two
    )
    grad_attn, pair_back, grad_wide, grad_act, gain_grad = call(
        attend_backward,
        sizes,
        4,
        40,
        [
            (rows_shape, BF),
            (pair_shape, BF),
            (by_row + (wide_width,), BF),
            (rows_shape, BF),
            ((1, width), F32),
        ],
        [pltpu.VMEM(rows_shape, BF), pltpu.VMEM(pair_shape[1:], BF)]
        + cross_sems
        + [dma(dp_size)],
        [vmem] * 9 + [hbm],
        grad_residual.astype(BF),
        xs,
        cosine_table,
        sine_table,
        wides,
        out_full,
        probs,
        query_rot,
        keyval,
        pair_grad.reshape(pair_shape),
        kept=3,
    )
    down_part, grad_attn, mlp_out = lax.optimization_barrier((down_part, grad_attn, mlp_out))
    outputs = (residual + mlp_out.astype(F32)).astype(BF)
    down_grad = scatter_sum(down_part, "dp").astype(F32)
    gate_grad, up_grad = small_call(
        functools.partial(unpack_kernel, counts), [(gate_weight.shape, F32)] * 2, pair_back
    )
    grad_attn = grad_attn.reshape(dp_size * row_count, width)
    output_grad = outer_sum(mixed_low, grad_attn).astype(BF)
    grad_wide = grad_wide.reshape(dp_size * row_count, wide_width)
    wide_grad = outer_sum(act_one, grad_wide).astype(BF)
    by_owner = (dp_size, fs_size, weight_rows)
    gain_grads = jnp.concatenate(
        [
            gain_grad.reshape(by_owner),
            mlp_gain_grad.reshape(by_owner),
            jnp.zeros((dp_size, fs_size, 128 - 2 * weight_rows), F32),
        ],
        axis=2,
    )
    gain_grads = jnp.broadcast_to(gain_grads[:, :, None, :], (dp_size, fs_size, 8, 128))
    wide_half = (dp_size, z_size, weight_rows, wide_width)
    out_half = (z_size, weight_rows, width)
    gain_half = (dp_size, z_size, 8, 128)
    grad_act_parts, wide_parts, out_parts, gain_parts = call(
        end_kernel,
        sizes,
        5,
        60,
        [(rows_shape, BF), (wide_half, BF), (out_half, BF), (gain_half, F32)],
        [
            pltpu.VMEM((row_count, width), BF),
            pltpu.VMEM(wide_half, BF),
            pltpu.VMEM(wide_half, BF),
            pltpu.VMEM(out_half, BF),
            pltpu.VMEM(out_half, BF),
            pltpu.VMEM(gain_half, F32),
            pltpu.VMEM(gain_half, F32),
            dma(2, dp_size),
            dma(2, chips),
            dma(2, z_size),
            dma(2, chips),
            dma(2, 3),
            dma(8),
        ],
        [hbm] * 4,
        grad_act,
        wide_grad.reshape(dp_size, z_size, 2, weight_rows, wide_width),
        output_grad.reshape(z_size, 2, weight_rows, width),
        gain_grads.reshape(dp_size, z_size, 2, 8, 128),
    )
    grad_act_one = jnp.sum(grad_act_parts.astype(F32), axis=0)
    own_inverse = lax.rsqrt(jnp.mean(source * source, axis=1, keepdims=True) + EPSILON)
    input_grad = (
        grad_residual + norm_back(grad_act_one, source * own_inverse, own_inverse, gain_one)
    ).astype(BF)
    gain_total = jnp.sum(gain_parts[:, :, 0, :], axis=(0, 1))
    wide_total = jnp.sum(wide_parts.astype(F32), axis=1)

    def from_heads(value):
        return value.transpose(1, 0, 2).reshape(weight_rows, -1)

    return (
        outputs,
        input_grad,
        gain_total[:weight_rows],
        from_heads(wide_total[:, :, :query_width]),
        from_heads(wide_total[:, :, query_width : query_width + HEAD_DIM]),
        from_heads(wide_total[:, :, query_width + HEAD_DIM :]),
        jnp.sum(out_parts.astype(F32), axis=0),
        gain_total[weight_rows : 2 * weight_rows],
        gate_grad,
        up_grad,
        down_grad,
    )


def solution(mesh):
    dp_size, fs_size = mesh.shape["dp"], mesh.shape["fsdp"]
    row = P(ALL, None)
    flat = P(ALL)

    def step(*args):
        return local(dp_size, fs_size, *args)

    return jax.shard_map(
        step,
        mesh=mesh,
        in_specs=(row, flat, flat, row, row, row, row, flat, row, row, row, row),
        out_specs=(row, row, flat, row, row, row, row, flat, row, row, row),
        check_vma=False,
    )
```

```python
import functools

import jax
import jax.numpy as jnp
from jax import lax
from jax.experimental import pallas as pl
from jax.experimental.pallas import tpu as pltpu
from jax.sharding import PartitionSpec as P

HEADS = 32
HEAD_DIM = 64
KV_HEADS = 4
EPSILON = 1e-05
ALL = ("dp", "fsdp")
BF = jnp.bfloat16
F32 = jnp.float32
MESH = pl.DeviceIdType.MESH


def matmul(left_side, right_side):
    return jnp.dot(left_side, right_side, preferred_element_type=F32)


def outer_sum(left_side, right_side):
    return lax.dot_general(
        left_side, right_side, (((0,), (0,)), ((), ())), preferred_element_type=F32
    )


def times_trans(left_side, right_side):
    return lax.dot_general(
        left_side, right_side, (((1,), (1,)), ((), ())), preferred_element_type=F32
    )


def rotary_tables(segments):
    row_count = segments.shape[0]
    row_index = jnp.arange(row_count, dtype=jnp.int32)
    earlier = jnp.sum((segments[None, :] < segments[:, None]).astype(jnp.int32), axis=1)
    places = (row_index - earlier).astype(F32)
    halfway = HEAD_DIM // 2
    frequency = 10000.0 ** (jnp.arange(halfway, dtype=F32) * (-2.0 / HEAD_DIM))
    angles = places[:, None] * frequency[None, :]
    cosine_table, sine_table = jnp.cos(angles), jnp.sin(angles)
    pairs = 128 // HEAD_DIM
    return (
        jnp.concatenate([cosine_table, cosine_table] * pairs, axis=1),
        jnp.concatenate([-sine_table, sine_table] * pairs, axis=1),
    )


def norm_back(upstream, normed, inverse, gain_vec):
    scaled = upstream * gain_vec
    return inverse * (scaled - normed * jnp.mean(scaled * normed, axis=1, keepdims=True))


def gather(value, axes):
    return lax.all_gather(value, axes, axis=0, tiled=True)


def scatter_sum(value, axes):
    return lax.psum_scatter(value, axes, scatter_dimension=0, tiled=True)


def place():
    d, f = lax.axis_index("dp"), lax.axis_index("fsdp")
    return d, f // 2, f % 2


def device(d, z, c):
    return {"dp": d, "fsdp": 2 * z + c}


def remote(src, dst, sems, index, target):
    return pltpu.make_async_remote_copy(
        src_ref=src,
        dst_ref=dst,
        send_sem=sems.at[0, index],
        recv_sem=sems.at[1, index],
        device_id=target,
        device_id_type=MESH,
    )


def hop(src, dst, sems, send, recv, target):
    return pltpu.make_async_remote_copy(
        src_ref=src,
        dst_ref=dst,
        send_sem=sems.at[0, send],
        recv_sem=sems.at[1, recv],
        device_id=target,
        device_id_type=MESH,
    )


def chain(z_size, shard, sems, first):
    d, z, c = place()

    def copy(s, to, send=None, src=None):
        src = shard(s) if src is None else src
        return hop(src, shard(s), sems, s if send is None else send, s, device(d, to, c))

    up, down = z < z_size - 1, z > 0

    def start():
        @pl.when(up)
        def _():
            copy(z, z + 1, src=first).start()

        @pl.when(down)
        def _():
            copy(z, z - 1, z_size, first).start()

    def go(arrived, low=1, high=z_size):
        def step(k):
            @pl.when(z - k >= 0)
            def _():
                copy(z - k, z).wait_recv()

                @pl.when(up)
                def _():
                    copy(z - k, z + 1).start()

                arrived(z - k)

            @pl.when(z + k < z_size)
            def _():
                copy(z + k, z).wait_recv()

                @pl.when(down)
                def _():
                    copy(z + k, z - 1).start()

                arrived(z + k)

        loop(low, high, step)

    def finish():
        @pl.when(up)
        def _():
            copy(z, z + 1, src=first).wait_send()

        @pl.when(down)
        def _():
            copy(z, z - 1, z_size, first).wait_send()

        def step(k):
            @pl.when((z - k >= 0) & up)
            def _():
                copy(z - k, z + 1).wait_send()

            @pl.when((z + k < z_size) & down)
            def _():
                copy(z + k, z - 1).wait_send()

        loop(1, z_size, step)

    return start, go, finish


def ring_place(q, size):
    q = (q + size) % size
    return q + (q // 2) * (1 - 2 * (q % 2)) if size == 4 else q


def loop(low, high, body):
    def step(index, carry):
        body(index)
        return carry

    lax.fori_loop(low, high, step, 0)


def greet(sizes, same_core=False, along_dp=False, along_fsdp=False, partner=False):
    dp_size, z_size = sizes
    d, z, c = place()
    barrier = pltpu.get_barrier_semaphore()

    def signal(target):
        pl.semaphore_signal(barrier, inc=1, device_id=target, device_id_type=MESH)

    count = 0
    if same_core:

        def to_chip(p):
            signal(device((d + p // z_size) % dp_size, (z + p % z_size) % z_size, c))

        loop(1, dp_size * z_size, to_chip)
        count += dp_size * z_size - 1
    if along_dp:
        loop(1, dp_size, lambda p: signal(device((d + p) % dp_size, z, c)))
        count += dp_size - 1
    if along_fsdp:
        f_size = 2 * z_size

        def to_line(p):
            signal({"dp": d, "fsdp": (2 * z + c + p) % f_size})

        loop(1, f_size, to_line)
        count += f_size - 1
    if partner:
        signal(device(d, z, 1 - c))
        count += 1
    pl.semaphore_wait(barrier, count)


def call(kernel, sizes, number, micros, outs, scratch, spaces, *args, kept=0):
    far = len(outs) - kept
    return pl.pallas_call(
        functools.partial(kernel, sizes),
        out_shape=tuple(jax.ShapeDtypeStruct(shape, dtype) for shape, dtype in outs),
        in_specs=[pl.BlockSpec(memory_space=space) for space in spaces],
        out_specs=tuple(
            pl.BlockSpec(memory_space=pltpu.HBM if k < far else pltpu.VMEM)
            for k in range(len(outs))
        ),
        scratch_shapes=scratch,
        compiler_params=pltpu.CompilerParams(collective_id=number, has_side_effects=True),
        cost_estimate=pl.CostEstimate(
            flops=int(micros * 1e9), bytes_accessed=0, transcendentals=0
        ),
        name=kernel.__name__,
    )(*args)


def dma(*shape):
    return pltpu.SemaphoreType.DMA(shape)


def start_kernel(sizes, *refs):
    x, seg_row, first_gain, second_gain, query, key, value, out, gate, up = refs[:10]
    xs, segs, gains, wides, outs, packed, seg, gain, wide = refs[10:19]
    sems = refs[19:]
    x_sem, seg_sem, gain_sem, piece_sem, wide_sem, out_sem = sems[:6]
    gain_fwd, wide_fwd, out_fwd, own_sem = sems[6:]
    dp_size, z_size = sizes
    chips = dp_size * z_size
    d, z, c = place()
    f = 2 * z + c
    rows, share = query.shape[0], query.shape[1] // dp_size
    for g in range(dp_size):
        low = g * HEAD_DIM
        ends = [part[:, low : low + HEAD_DIM].astype(F32) for part in (key, value)]
        wide[g, :, :share] = query[:, g * share : (g + 1) * share]
        wide[g, :, share:] = jnp.concatenate(ends, axis=1).astype(BF)
    gain_row = jnp.concatenate(
        [
            first_gain[...].astype(F32),
            second_gain[...].astype(F32),
            jnp.zeros((1, 128 - 2 * rows), F32),
        ][: 2 if rows == 64 else 3],
        axis=1,
    )
    gain[...] = jnp.broadcast_to(gain_row, gain.shape).astype(BF)
    seg[...] = jnp.broadcast_to(seg_row[...], seg.shape)
    greet(sizes, same_core=True, partner=True)
    other = device(d, z, 1 - c)

    def piece_copy(p):
        to = (d + p) % dp_size
        return remote(wide.at[to], wides.at[d, f], piece_sem, p, device(to, z, c))

    def gain_copy(p):
        to_d, to_z = (d + p // z_size) % dp_size, (z + p % z_size) % z_size
        return remote(gain, gains.at[d, f], gain_sem, p, device(to_d, to_z, c))

    def x_copy(p):
        return remote(x, xs.at[d], x_sem, p, device((d + p) % dp_size, z, c))

    def seg_copy(p):
        return remote(seg, segs.at[d], seg_sem, p, device((d + p) % dp_size, z, c))

    def out_pass(s):
        slot = outs.at[2 * s + c]
        return remote(slot, slot, out_fwd, s, other)

    def wide_pass(s):
        slot = wides.at[:, 2 * s + c]
        return remote(slot, slot, wide_fwd, s, other)

    def gain_pass(p):
        from_d = (d - p // z_size + dp_size) % dp_size
        slot = gains.at[from_d, 2 * ((z - p % z_size + z_size) % z_size) + c]
        return remote(slot, slot, gain_fwd, p, other)

    out_start, out_go, out_finish = chain(z_size, lambda s: outs.at[2 * s + c], out_sem, out)
    wide_start, wide_go, wide_finish = chain(
        z_size, lambda s: wides.at[:, 2 * s + c], wide_sem, wides.at[:, f]
    )
    own = [
        pltpu.make_async_copy(wide.at[d], wides.at[d, f], own_sem.at[0]),
        pltpu.make_async_copy(x, xs.at[d], own_sem.at[1]),
        pltpu.make_async_copy(seg, segs.at[d], own_sem.at[2]),
        pltpu.make_async_copy(gain, gains.at[d, f], own_sem.at[3]),
        pltpu.make_async_copy(out, outs.at[f], own_sem.at[4]),
    ]
    loop(1, dp_size, lambda p: piece_copy(p).start())
    for copy in own:
        copy.start()
    out_start()
    loop(1, chips, lambda p: gain_copy(p).start())
    loop(1, dp_size, lambda p: seg_copy(p).start())
    loop(1, dp_size, lambda p: x_copy(p).start())
    passed = [
        remote(gain, gains.at[d, f], gain_fwd, 0, other),
        remote(out, outs.at[f], out_fwd, z, other),
    ]
    for copy in passed:
        copy.start()
    own[0].wait()
    loop(1, dp_size, lambda p: piece_copy(p).wait())
    wide_start()
    wide_pass(z).start()
    pack((dp_size, 2 * z_size, gate.shape[1] // (2 * chips)), gate, up, packed)
    out_go(lambda s: out_pass(s).start())
    wide_go(lambda s: wide_pass(s).start())

    def pass_gain(p):
        gain_copy(p).wait_recv()
        gain_pass(p).start()

    loop(1, chips, pass_gain)
    loop(1, dp_size, lambda p: seg_copy(p).wait())
    loop(1, dp_size, lambda p: x_copy(p).wait())
    for copy in own[1:]:
        copy.wait()
    for copy in passed:
        copy.wait()
    wide_pass(z).wait()

    def end_pass(k):
        s = (z + k) % z_size
        out_pass(s).wait()
        wide_pass(s).wait()

    loop(1, z_size, end_pass)
    loop(1, chips, lambda p: gain_pass(p).wait())
    loop(1, chips, lambda p: gain_copy(p).wait_send())
    out_finish()
    wide_finish()


def gather_line(sizes, *refs):
    rows, pair, cot, down = refs[:4]
    rows_out, pair_out, hid_out, grad_out = refs[4:8]
    act_v, pair_v, cot_v, down_v, both, hidden = refs[8:14]
    rows_sem, pass_sem, pair_sem, own_sem = refs[14:]
    dp_size, z_size = sizes
    d, z, c = place()
    f = 2 * z + c
    greet(sizes, along_dp=True, along_fsdp=True)
    q = ring_place(d, dp_size)
    right, left = ring_place(q + 1, dp_size), ring_place(q - 1, dp_size)
    across = ring_place((q + 2) % dp_size, dp_size)
    other = device(d, z, 1 - c)
    depth = pair.shape[0]
    half = depth // 2

    def rows_pass(s):
        slot = act_v.at[2 * s + c]
        return remote(slot, slot, pass_sem, s, other)

    def whole_copy(to, index):
        return remote(pair, pair_v.at[d], pair_sem, index, device(to, z, c))

    def half_copy(source, to, low, index):
        slot = pair_v.at[source, pl.ds(low, half)]
        return remote(slot, slot, pair_sem, index, device(to, z, c))

    start, go, finish = chain(z_size, lambda s: act_v.at[2 * s + c], rows_sem, rows)
    start()
    to_right, to_left = whole_copy(right, 0), whole_copy(left, 1)
    to_right.start()
    to_left.start()
    takes = [
        pltpu.make_async_copy(rows, act_v.at[f], own_sem.at[0]),
        pltpu.make_async_copy(cot, cot_v, own_sem.at[1]),
        pltpu.make_async_copy(down, down_v, own_sem.at[2]),
        pltpu.make_async_copy(pair, pair_v.at[d], own_sem.at[3]),
    ]
    for copy in takes:
        copy.start()
    passed = remote(rows, act_v.at[f], pass_sem, z, other)
    passed.start()
    for copy in takes:
        copy.wait()
    tall = 256

    def tile(i):
        return pl.ds(pl.multiple_of(i * tall, tall), tall)

    def hidden_tile(i):
        hidden[tile(i), :] = times_trans(cot_v[tile(i), :], down_v[...])

    loop(0, cot.shape[0] // tall, hidden_tile)
    go(lambda s: rows_pass(s).start(), 1, z_size - 1)
    to_right.wait_recv()
    on_right = half_copy(left, right, 0, 2)
    on_right.start()
    to_left.wait_recv()
    on_left = half_copy(right, left, half, 3)
    on_left.start()
    go(lambda s: rows_pass(s).start(), z_size - 1)
    passed.wait()
    loop(1, z_size, lambda k: rows_pass((z + k) % z_size).wait())
    give_rows = pltpu.make_async_copy(act_v, rows_out, own_sem.at[4])
    give_rows.start()

    def product(i, block, low, high):
        lanes = pl.ds(pl.multiple_of(block * depth, depth), depth)
        left_side = act_v[pl.ds(2 * i, 2), :, lanes].reshape(tall, depth)
        return matmul(left_side, pair_v[block, :, low:high])

    columns = pair.shape[1]
    cuts = [(low, min(low + 256, columns)) for low in range(0, columns, 256)]

    def first_tile(i):
        for low, high in cuts:
            both[tile(i), low:high] = (
                product(i, d, low, high)
                + product(i, left, low, high)
                + product(i, right, low, high)
            )

    def last_tile(i):
        for low, high in cuts:
            both[tile(i), low:high] = both[tile(i), low:high] + product(i, across, low, high)

    loop(0, both.shape[0] // tall, first_tile)
    on_right.wait_recv()
    on_left.wait_recv()
    give_pair = pltpu.make_async_copy(pair_v, pair_out, own_sem.at[5])
    give_pair.start()
    loop(0, both.shape[0] // tall, last_tile)
    share = columns // 2

    def unit(i):
        at = pl.ds(pl.multiple_of(i * 64, 64), 64)
        values = both[at, :]
        gate, up, upstream = values[:, :share], values[:, share:], hidden[at, :]
        sigmoid = jax.nn.sigmoid(gate)
        hid_out[at, :] = (gate * sigmoid * up).astype(BF)
        grad_gate = upstream * up * sigmoid * (1.0 + gate * (1.0 - sigmoid))
        grad_up = upstream * gate * sigmoid
        grad_out[at, :] = jnp.concatenate([grad_gate, grad_up], axis=1).astype(BF)

    loop(0, both.shape[0] // 64, unit)
    give_rows.wait()
    give_pair.wait()
    finish()
    to_right.wait_send()
    to_left.wait_send()
    on_right.wait_send()
    on_left.wait_send()


def scatter_line(sizes, *refs):
    part, pair, hid, hid_turned, down, cot = refs[:6]
    part_out, pair_out, mlp_out, grad_out = refs[6:10]
    mine, theirs, got_a, got_b, my_a, my_b, pair_own = refs[10:17]
    hid_v, turned_v, down_v, cot_v, mlp_v, grad_v = refs[17:23]
    part_sem, swap_sem, load_sem, own_sem, pair_sem, mat_sem = refs[23:]
    dp_size, z_size = sizes
    d, z, c = place()
    greet(sizes, along_dp=True, along_fsdp=True)
    other = device(d, z, 1 - c)
    q = ring_place(d, dp_size)
    right, left = ring_place(q + 1, dp_size), ring_place(q - 1, dp_size)
    across = ring_place((q + 2) % dp_size, dp_size)
    to_right, to_left = device(right, z, c), device(left, z, c)
    half = pair.shape[1] // 2
    rows_a, rows_b = pl.ds(0, half), pl.ds(half, half)

    def swap_copy(p):
        to = (z + p) % z_size
        return remote(part.at[to, 1 - c], theirs.at[to], swap_sem, p, other)

    def load(p):
        to = (z + p) % z_size
        return pltpu.make_async_copy(part.at[to, c], mine.at[to], load_sem.at[p])

    def part_copy(p):
        to = (z + p) % z_size
        return remote(mine.at[to], part_out.at[z], part_sem, p, device(d, to, c))

    def begin(p):
        swap_copy(p).start()
        load(p).start()

    def add(p):
        to = (z + p) % z_size
        swap_copy(p).wait()
        load(p).wait()
        mine[to] = (mine[to].astype(F32) + theirs[to].astype(F32)).astype(BF)

    def send(p):
        add(p)
        part_copy(p).start()

    loop(1, z_size, begin)
    begin(0)
    ring = [
        remote(pair.at[across, rows_a], got_a, pair_sem, 0, to_right),
        remote(pair.at[across, rows_b], got_b, pair_sem, 1, to_left),
        remote(pair.at[right, rows_b], pair_out.at[0, rows_b], pair_sem, 2, to_right),
        remote(pair.at[left, rows_a], pair_out.at[1, rows_a], pair_sem, 3, to_left),
        remote(my_a, pair_out.at[0, rows_a], pair_sem, 4, to_right),
        remote(my_b, pair_out.at[1, rows_b], pair_sem, 5, to_left),
    ]
    for copy in ring[:4]:
        copy.start()
    takes = [
        pltpu.make_async_copy(pair.at[right, rows_a], my_a, own_sem.at[1]),
        pltpu.make_async_copy(pair.at[left, rows_b], my_b, own_sem.at[2]),
        pltpu.make_async_copy(pair.at[d], pair_own, own_sem.at[3]),
    ]
    mats = [
        pltpu.make_async_copy(hid, hid_v, mat_sem.at[0]),
        pltpu.make_async_copy(down, down_v, mat_sem.at[1]),
        pltpu.make_async_copy(hid_turned, turned_v, mat_sem.at[2]),
        pltpu.make_async_copy(cot, cot_v, mat_sem.at[3]),
    ]
    loop(1, z_size, send)
    for copy in takes + mats:
        copy.start()
    add(0)
    own = pltpu.make_async_copy(mine.at[z], part_out.at[z], own_sem.at[0])
    own.start()
    takes[2].wait()
    give = pltpu.make_async_copy(pair_own, pair_out.at[2], own_sem.at[4])
    give.start()
    mats[0].wait()
    mats[1].wait()
    tall = 256

    def mlp_tile(i):
        rows = pl.ds(pl.multiple_of(i * tall, tall), tall)
        for low in range(0, mlp_v.shape[1], 512):
            product = matmul(hid_v[rows, :], down_v[:, low : low + 512])
            mlp_v[rows, low : low + 512] = product.astype(BF)

    loop(0, mlp_v.shape[0] // tall, mlp_tile)
    give_mlp = pltpu.make_async_copy(mlp_v, mlp_out, mat_sem.at[4])
    give_mlp.start()

    def merge(total, got):
        def chunk(i):
            rows = pl.ds(pl.multiple_of(i * 32, 32), 32)
            total[rows, :] = (total[rows, :].astype(F32) + got[rows, :].astype(F32)).astype(BF)

        loop(0, half // 32, chunk)

    takes[0].wait()
    ring[0].wait_recv()
    merge(my_a, got_a)
    ring[4].start()
    takes[1].wait()
    ring[1].wait_recv()
    merge(my_b, got_b)
    ring[5].start()
    mats[2].wait()
    mats[3].wait()

    def grad_tile(i):
        lanes = pl.ds(pl.multiple_of(i * 256, 256), 256)
        grad_v[:, lanes] = matmul(turned_v[...], cot_v[:, lanes]).astype(BF)

    loop(0, grad_v.shape[1] // 256, grad_tile)
    give_grad = pltpu.make_async_copy(grad_v, grad_out, mat_sem.at[5])
    give_grad.start()
    own.wait()
    give.wait()
    give_mlp.wait()
    give_grad.wait()
    ring[0].wait_send()
    ring[1].wait_send()
    for copy in ring[2:]:
        copy.wait()
    loop(1, z_size, lambda p: part_copy(p).wait())


def end_kernel(sizes, rows, wide, out, gain, rows_out, wide_out, out_out, gain_out, *scratch):
    rows_own, wide_mine, wide_theirs, out_mine, out_theirs, gain_mine, gain_theirs = scratch[:7]
    rows_sem, wide_sem, out_sem, gain_sem, swap_sem, own_sem = scratch[7:]
    dp_size, z_size = sizes
    chips = dp_size * z_size
    d, z, c = place()
    greet(sizes, same_core=True, partner=True)
    other = device(d, z, 1 - c)
    swaps = [
        remote(out.at[:, 1 - c], out_theirs, swap_sem, 0, other),
        remote(wide.at[:, :, 1 - c], wide_theirs, swap_sem, 1, other),
        remote(gain.at[:, :, 1 - c], gain_theirs, swap_sem, 2, other),
    ]
    loads = [
        pltpu.make_async_copy(out.at[:, c], out_mine, own_sem.at[0]),
        pltpu.make_async_copy(wide.at[:, :, c], wide_mine, own_sem.at[1]),
        pltpu.make_async_copy(gain.at[:, :, c], gain_mine, own_sem.at[2]),
    ]
    for copy in swaps + loads:
        copy.start()

    def rows_copy(p):
        to = (d + p) % dp_size
        return remote(rows.at[to], rows_out.at[d], rows_sem, p, device(to, z, c))

    loop(1, dp_size, lambda p: rows_copy(p).start())
    rows_in = pltpu.make_async_copy(rows.at[d], rows_own, own_sem.at[3])
    rows_in.start()

    def out_copy(p):
        to = (z + p) % z_size
        return remote(out_mine.at[to], out_out.at[z], out_sem, p, device(d, to, c))

    def target(p):
        return (d + p // z_size) % dp_size, (z + p % z_size) % z_size

    def wide_copy(p):
        to_d, to_z = target(p)
        return remote(
            wide_mine.at[to_d, to_z], wide_out.at[d, z], wide_sem, p, device(to_d, to_z, c)
        )

    def gain_copy(p):
        to_d, to_z = target(p)
        return remote(
            gain_mine.at[to_d, to_z], gain_out.at[d, z], gain_sem, p, device(to_d, to_z, c)
        )

    def add_out(p):
        to = (z + p) % z_size
        out_mine[to] = (out_mine[to].astype(F32) + out_theirs[to].astype(F32)).astype(BF)

    def add_wide(p):
        to_d, to_z = target(p)
        total = wide_mine[to_d, to_z].astype(F32) + wide_theirs[to_d, to_z].astype(F32)
        wide_mine[to_d, to_z] = total.astype(BF)
        gain_mine[to_d, to_z] = gain_mine[to_d, to_z] + gain_theirs[to_d, to_z]

    swaps[0].wait()
    loads[0].wait()

    def send_out(p):
        add_out(p)
        out_copy(p).start()

    loop(1, z_size, send_out)
    add_out(0)
    for copy in swaps[1:] + loads[1:]:
        copy.wait()

    def send_wide(p):
        add_wide(p)
        wide_copy(p).start()
        gain_copy(p).start()

    loop(1, chips, send_wide)
    add_wide(0)
    rows_in.wait()
    own = [
        pltpu.make_async_copy(rows_own, rows_out.at[d], own_sem.at[4]),
        pltpu.make_async_copy(out_mine.at[z], out_out.at[z], own_sem.at[5]),
        pltpu.make_async_copy(wide_mine.at[d, z], wide_out.at[d, z], own_sem.at[6]),
        pltpu.make_async_copy(gain_mine.at[d, z], gain_out.at[d, z], own_sem.at[7]),
    ]
    for copy in own:
        copy.start()
    for copy in own:
        copy.wait()
    loop(1, dp_size, lambda p: rows_copy(p).wait())
    loop(1, z_size, lambda p: out_copy(p).wait())
    loop(1, chips, lambda p: wide_copy(p).wait())
    loop(1, chips, lambda p: gain_copy(p).wait())


def turned(value):
    lane = lax.broadcasted_iota(jnp.int32, value.shape, 1)
    ahead, behind = pltpu.roll(value, 128 - HEAD_DIM // 2, 1), pltpu.roll(value, HEAD_DIM // 2, 1)
    return jnp.where(lane % HEAD_DIM < HEAD_DIM // 2, ahead, behind)


def low_lanes(value):
    lane = lax.broadcasted_iota(jnp.int32, value.shape, 1)
    return jnp.where(lane < HEAD_DIM, value, jnp.zeros_like(value))


def high_lanes(value):
    lane = lax.broadcasted_iota(jnp.int32, value.shape, 1)
    return jnp.where(lane < HEAD_DIM, jnp.zeros_like(value), value)


def both_sides(value):
    low = low_lanes(value)
    return low, pltpu.roll(low, HEAD_DIM, 1)


def attend_forward(sizes, *refs):
    xs, gain, mask, cosine, sine, wides, out, pair, down = refs[:9]
    rows_out, pair_out, down_out, probs, query_out, keyval_out, mixed_out, act_out = refs[9:17]
    mixed_v = refs[-1]
    parts, pair_own, down_own, rows_sem, pair_sem, own_sem, down_sem = refs[17:-1]
    dp_size, z_size = sizes
    f_size = 2 * z_size
    d, z, c = place()
    f = 2 * z + c
    pairs = query_out.shape[2] // 128
    greet(sizes, along_dp=True, along_fsdp=True)

    def pair_copy(p):
        to = (f + p) % f_size
        return remote(pair.at[to], pair_out.at[f], pair_sem, p, {"dp": d, "fsdp": to})

    def rows_copy(p):
        to = (d + p) % dp_size
        return remote(parts.at[to], rows_out.at[d], rows_sem, p, device(to, z, c))

    def down_copy(p):
        return remote(down, down_out.at[d], down_sem, p, device((d + p) % dp_size, z, c))

    loop(1, f_size, lambda p: pair_copy(p).start())
    loop(1, dp_size, lambda p: down_copy(p).start())
    take = pltpu.make_async_copy(pair.at[f], pair_own, own_sem.at[0])
    take.start()
    take_down = pltpu.make_async_copy(down, down_own, own_sem.at[3])
    take_down.start()
    take.wait()
    give = pltpu.make_async_copy(pair_own, pair_out.at[f], own_sem.at[1])
    give.start()
    take_down.wait()
    give_down = pltpu.make_async_copy(down_own, down_out.at[d], own_sem.at[4])
    give_down.start()

    def block(g):
        source = xs[g].astype(F32)
        inverse = lax.rsqrt(jnp.mean(source * source, axis=1, keepdims=True) + EPSILON)
        act = (source * inverse * gain[...]).astype(BF)
        tokens = pl.ds(pl.multiple_of(g * act.shape[0], act.shape[0]), act.shape[0])
        act_out[:, tokens] = act.T
        rows = matmul(act, wides[...])
        cosine_table, sine_table = cosine[g], sine[g]
        keyval = rows[:, pairs * 128 :]
        key = (keyval * cosine_table + turned(keyval) * sine_table).astype(BF).astype(F32)
        value = keyval.astype(BF).astype(F32)
        keyval_out[g] = jnp.where(
            lax.broadcasted_iota(jnp.int32, key.shape, 1) < HEAD_DIM, key, value
        ).astype(BF)
        keys = [side.astype(BF) for side in both_sides(key)]
        values = [side.astype(BF) for side in both_sides(pltpu.roll(value, HEAD_DIM, 1))]
        allowed = mask[g] > 0
        for pair_index in range(pairs):
            lanes = pl.ds(pair_index * 128, 128)
            query = rows[:, pair_index * 128 : pair_index * 128 + 128]
            query = (query * cosine_table + turned(query) * sine_table).astype(BF)
            query_out[g, :, lanes] = query
            mixed = jnp.zeros(query.shape, F32)
            for side in range(2):
                raw = times_trans(query, keys[side])
                scores = jnp.where(allowed, raw * HEAD_DIM ** (-0.5), -1e30)
                powers = jnp.exp(scores - jnp.max(scores, axis=1, keepdims=True))
                weights = powers / jnp.sum(powers, axis=1, keepdims=True)
                probs[g, 2 * pair_index + side] = weights
                mixed += matmul(weights.astype(BF), values[side])
            mixed_v[:, lanes] = mixed.astype(BF)
        parts[g] = matmul(mixed_v[...], out[...]).astype(BF)
        mixed_out[:, tokens] = mixed_v[...].T

    def send(p):
        block((d + p) % dp_size)

        @pl.when(p < dp_size)
        def _():
            rows_copy(p).start()

    loop(1, dp_size + 1, send)
    own = pltpu.make_async_copy(parts.at[d], rows_out.at[d], own_sem.at[2])
    own.start()
    own.wait()
    give.wait()
    give_down.wait()
    loop(1, dp_size, lambda p: rows_copy(p).wait())
    loop(1, dp_size, lambda p: down_copy(p).wait())
    loop(1, f_size, lambda p: pair_copy(p).wait())


def attend_backward(sizes, *refs):
    rows, xs, cosine, sine, wides, out, probs, query_in, keyval_in, mixed, act = refs[:11]
    pair, pair_out, wide_grad, output_grad, grad_act, gain_grad = refs[11:17]
    held, pair_own, grad_wide, rows_sem, pair_sem, own_sem = refs[17:]
    dp_size, z_size = sizes
    f_size = 2 * z_size
    d, z, c = place()
    f = 2 * z + c
    pairs = query_in.shape[2] // 128
    greet(sizes, along_dp=True, along_fsdp=True)

    def pair_copy(p):
        to = (f + p) % f_size
        return remote(pair.at[to], pair_out.at[f], pair_sem, p, {"dp": d, "fsdp": to})

    def rows_copy(p):
        return remote(rows, held.at[d], rows_sem, p, device((d + p) % dp_size, z, c))

    loop(1, dp_size, lambda p: rows_copy(p).start())
    loop(1, f_size, lambda p: pair_copy(p).start())
    take = pltpu.make_async_copy(pair.at[f], pair_own, own_sem.at[0])
    take.start()
    own = pltpu.make_async_copy(rows, held.at[d], own_sem.at[2])
    own.start()
    take.wait()
    give = pltpu.make_async_copy(pair_own, pair_out.at[f], own_sem.at[1])
    give.start()
    gain_grad[...] = jnp.zeros_like(gain_grad)

    def block(g):
        tokens = pl.ds(pl.multiple_of(g * rows.shape[0], rows.shape[0]), rows.shape[0])
        grad_mixed = times_trans(held[g], out[...]).astype(BF)
        cosine_table, sine_table = cosine[g], sine[g]
        keyval = keyval_in[g].astype(F32)
        keys = [side.astype(BF) for side in both_sides(keyval)]
        values = [side.astype(BF) for side in both_sides(pltpu.roll(keyval, HEAD_DIM, 1))]
        key_sums = [jnp.zeros(keyval.shape, F32), jnp.zeros(keyval.shape, F32)]
        value_sums = [jnp.zeros(keyval.shape, F32), jnp.zeros(keyval.shape, F32)]
        for pair_index in range(pairs):
            lanes = pl.ds(pair_index * 128, 128)
            up = grad_mixed[:, pair_index * 128 : pair_index * 128 + 128]
            query = query_in[g, :, lanes]
            grad_query = jnp.zeros(query.shape, F32)
            for side in range(2):
                weights = probs[g, 2 * pair_index + side]
                grad_probs = times_trans(up, values[side])
                value_sums[side] += outer_sum(weights.astype(BF), up)
                inner = jnp.sum(weights * grad_probs, axis=1, keepdims=True)
                grad_raw = (HEAD_DIM ** (-0.5) * weights * (grad_probs - inner)).astype(BF)
                grad_query += matmul(grad_raw, keys[side])
                key_sums[side] += outer_sum(grad_raw, query)
            grad_query = grad_query * cosine_table - turned(grad_query) * sine_table
            grad_wide[tokens, lanes] = grad_query.astype(BF)
        grad_key = key_sums[0] + pltpu.roll(key_sums[1], HEAD_DIM, 1)
        grad_key = grad_key * cosine_table - turned(grad_key) * sine_table
        grad_value = value_sums[1] + pltpu.roll(value_sums[0], HEAD_DIM, 1)
        lane = lax.broadcasted_iota(jnp.int32, grad_key.shape, 1)
        grad_wide[tokens, pl.ds(pairs * 128, 128)] = jnp.where(
            lane < HEAD_DIM, grad_key, grad_value
        ).astype(BF)
        grad = times_trans(grad_wide[tokens, :], wides[...])
        grad_act[g] = grad.astype(BF)
        source = xs[g].astype(F32)
        inverse = lax.rsqrt(jnp.mean(source * source, axis=1, keepdims=True) + EPSILON)
        gain_grad[...] += jnp.sum(source * inverse * grad, axis=0, keepdims=True)

    def arrive(p):
        @pl.when(p == 0)
        def _():
            own.wait()

        @pl.when(p > 0)
        def _():
            rows_copy(p).wait_recv()

        block((d - p + dp_size) % dp_size)

    loop(0, dp_size, arrive)

    def wide_tile(i):
        rows_at = pl.ds(pl.multiple_of(i * 256, 256), 256)
        wide_grad[rows_at, :] = matmul(act[rows_at, :], grad_wide[...]).astype(BF)

    def output_tile(i):
        lanes = pl.ds(pl.multiple_of(i * 256, 256), 256)
        upstream = held[:, :, lanes].reshape(mixed.shape[1], 256)
        output_grad[:, lanes] = matmul(mixed[...], upstream).astype(BF)

    loop(0, act.shape[0] // 256, wide_tile)
    loop(0, rows.shape[1] // 256, output_tile)
    give.wait()
    loop(1, dp_size, lambda p: rows_copy(p).wait_send())
    loop(1, f_size, lambda p: pair_copy(p).wait())


def pack(counts, gate, up, packed):
    dp_size, fs_size, unit = counts
    for f in range(fs_size):
        pieces = []
        for weight in (gate, up):
            for g in range(dp_size):
                low = (g * fs_size + f) * unit
                pieces.append(weight[:, low : low + unit].astype(F32))
        packed[f] = jnp.concatenate(pieces, axis=1).astype(BF)


def unpack_kernel(counts, packed, gate, up):
    dp_size, fs_size, unit = counts
    for half, grad in enumerate((gate, up)):
        for g in range(dp_size):
            low = (half * dp_size + g) * unit
            pieces = [packed[f, :, low : low + unit].astype(F32) for f in range(fs_size)]
            grad[:, g * fs_size * unit : (g + 1) * fs_size * unit] = jnp.concatenate(
                pieces, axis=1
            )


def small_call(kernel, outs, *args):
    return pl.pallas_call(
        kernel,
        out_shape=tuple(jax.ShapeDtypeStruct(shape, dtype) for shape, dtype in outs),
        cost_estimate=pl.CostEstimate(flops=int(3e9), bytes_accessed=0, transcendentals=0),
    )(*args)


def local(
    dp_size,
    fs_size,
    inputs,
    segment_ids,
    attn_gain,
    query_weight,
    key_weight,
    value_weight,
    output_weight,
    mlp_gain,
    gate_weight,
    up_weight,
    down_weight,
    cotangent,
):
    z_size = fs_size // 2
    sizes = (dp_size, z_size)
    row_count, width = inputs.shape
    weight_rows, ff_width = gate_weight.shape
    unit = down_weight.shape[0]
    share = dp_size * unit
    heads = HEADS // dp_size
    query_width = heads * HEAD_DIM
    wide_width = query_width + 2 * HEAD_DIM
    vmem, hbm = pltpu.VMEM, pltpu.HBM

    counts = (dp_size, fs_size, unit)
    pair_shape = (fs_size, weight_rows, 2 * share)
    chips = dp_size * z_size
    xs, segs, gains, wides, out_full, pair = call(
        start_kernel,
        sizes,
        0,
        50,
        [
            ((dp_size, row_count, width), BF),
            ((dp_size, 8, row_count), jnp.int32),
            ((dp_size, fs_size, 16, 128), BF),
            ((dp_size, fs_size, weight_rows, wide_width), BF),
            ((fs_size, weight_rows, width), BF),
            (pair_shape, BF),
        ],
        [
            pltpu.VMEM((8, row_count), jnp.int32),
            pltpu.VMEM((16, 128), BF),
            pltpu.VMEM((dp_size, weight_rows, wide_width), BF),
            dma(2, dp_size),
            dma(2, dp_size),
            dma(2, chips),
            dma(2, dp_size),
            dma(2, z_size + 1),
            dma(2, z_size + 1),
            dma(2, chips),
            dma(2, z_size),
            dma(2, z_size),
            dma(5),
        ],
        [vmem] * 10,
        inputs,
        segment_ids[None, :],
        attn_gain[None, :],
        mlp_gain[None, :],
        query_weight,
        key_weight,
        value_weight,
        output_weight,
        gate_weight,
        up_weight,
        kept=1,
    )
    cot_late, xs = lax.optimization_barrier((cotangent, xs))
    cot_full = gather(cot_late, "fsdp")
    gains = gains[:, :, 0, :].astype(F32)
    gain_one = gains[:, :, :weight_rows].reshape(width)
    gain_two = gains[:, :, weight_rows : 2 * weight_rows].reshape(width)
    wides = wides.reshape(width, wide_width)
    out_full = out_full.reshape(query_width, width)

    segs = segs[:, 0, :]
    cosine_table, sine_table = jax.vmap(rotary_tables)(segs)
    row_index = jnp.arange(row_count, dtype=jnp.int32)
    allowed = (segs[:, :, None] == segs[:, None, :]) & (
        row_index[:, None] >= row_index[None, :]
    )
    mask = allowed.astype(F32)
    by_row = (dp_size, row_count)
    rows_shape = by_row + (width,)
    cross_sems = [dma(2, dp_size), dma(2, fs_size), dma(5)]
    mixed_parts, pair_rows, down_full, probs, query_rot, keyval, mixed_low, act_one = call(
        attend_forward,
        sizes,
        1,
        40,
        [
            (rows_shape, BF),
            (pair_shape, BF),
            ((dp_size,) + down_weight.shape, BF),
            ((dp_size, heads, row_count, row_count), F32),
            (by_row + (query_width,), BF),
            (by_row + (128,), BF),
            ((query_width, dp_size * row_count), BF),
            ((width, dp_size * row_count), BF),
        ],
        [
            pltpu.VMEM(rows_shape, BF),
            pltpu.VMEM(pair_shape[1:], BF),
            pltpu.VMEM(down_weight.shape, BF),
        ]
        + cross_sems
        + [dma(2, dp_size), pltpu.VMEM((row_count, query_width), BF)],
        [vmem] * 7 + [hbm] * 2,
        xs,
        gain_one[None, :],
        mask,
        cosine_table,
        sine_table,
        wides,
        out_full,
        pair,
        down_weight,
        kept=5,
    )
    down_full = down_full.reshape(share, width)
    source = inputs.astype(F32)
    residual = source + jnp.sum(mixed_parts.astype(F32), axis=0)
    inverse_two = lax.rsqrt(jnp.mean(residual * residual, axis=1, keepdims=True) + EPSILON)
    normed_two = residual * inverse_two
    act_two = (normed_two * gain_two).astype(BF)
    pair_rows = pair_rows.reshape(fs_size * weight_rows, 2 * share)
    tokens = fs_size * row_count
    act_full, pair_full, hidden_low, grad_both = call(
        gather_line,
        sizes,
        2,
        55,
        [
            ((fs_size, row_count, width), BF),
            ((dp_size,) + pair_rows.shape, BF),
            ((tokens, share), BF),
            ((tokens, 2 * share), BF),
        ],
        [
            pltpu.VMEM((fs_size, row_count, width), BF),
            pltpu.VMEM((dp_size,) + pair_rows.shape, BF),
            pltpu.VMEM((tokens, width), BF),
            pltpu.VMEM((share, width), BF),
            pltpu.VMEM((tokens, 2 * share), F32),
            pltpu.VMEM((tokens, share), F32),
            dma(2, z_size + 1),
            dma(2, z_size),
            dma(2, 4),
            dma(6),
        ],
        [vmem, hbm, hbm, hbm],
        act_two,
        pair_rows,
        cot_full,
        down_full,
        kept=2,
    )
    pair_full = pair_full.reshape(width, 2 * share)
    act_full = act_full.reshape(tokens, width)

    grad_part = times_trans(grad_both, pair_full).astype(BF)
    pair_grad = outer_sum(act_full, grad_both).astype(BF)
    pair_block = (fs_size * weight_rows, 2 * share)
    pair_half = (fs_size * weight_rows // 2, 2 * share)
    grad_parts, pair_parts, mlp_part, down_part = call(
        scatter_line,
        sizes,
        3,
        60,
        [
            ((z_size, row_count, width), BF),
            ((3,) + pair_block, BF),
            ((tokens, width), BF),
            ((share, width), BF),
        ],
        [pltpu.VMEM((z_size, row_count, width), BF)] * 2
        + [pltpu.VMEM(pair_half, BF)] * 4
        + [
            pltpu.VMEM(pair_block, BF),
            pltpu.VMEM((tokens, share), BF),
            pltpu.VMEM((share, tokens), BF),
            pltpu.VMEM((share, width), BF),
            pltpu.VMEM((tokens, width), BF),
            pltpu.VMEM((tokens, width), BF),
            pltpu.VMEM((share, width), BF),
            dma(2, z_size),
            dma(2, z_size),
            dma(z_size),
            dma(5),
            dma(2, 6),
            dma(6),
        ],
        [hbm] * 6,
        grad_part.reshape(z_size, 2, row_count, width),
        pair_grad.reshape((dp_size,) + pair_block),
        hidden_low,
        hidden_low.T,
        down_full,
        cot_full,
    )
    pair_grad = jnp.sum(pair_parts.astype(F32), axis=0).astype(BF)
    mlp_out = scatter_sum(mlp_part, "fsdp")

    grad_act_two = jnp.sum(grad_parts.astype(F32), axis=0)
    mlp_gain_grad = jnp.sum(normed_two * grad_act_two, axis=0)
    grad_residual = cotangent.astype(F32) + norm_back(
        grad_act_two, normed_two, inverse_two, gain_two
    )
    pair_back, wide_grad, output_grad, grad_act, gain_grad = call(
        attend_backward,
        sizes,
        4,
        50,
        [
            (pair_shape, BF),
            ((width, wide_width), BF),
            ((query_width, width), BF),
            (rows_shape, BF),
            ((1, width), F32),
        ],
        [
            pltpu.VMEM(rows_shape, BF),
            pltpu.VMEM(pair_shape[1:], BF),
            pltpu.VMEM((dp_size * row_count, wide_width), BF),
        ]
        + cross_sems,
        [vmem] * 11 + [hbm],
        grad_residual.astype(BF),
        xs,
        cosine_table,
        sine_table,
        wides,
        out_full,
        probs,
        query_rot,
        keyval,
        mixed_low,
        act_one,
        pair_grad.reshape(pair_shape),
        kept=4,
    )
    down_part, pair_back, mlp_out = lax.optimization_barrier((down_part, pair_back, mlp_out))
    outputs = (residual + mlp_out.astype(F32)).astype(BF)
    down_grad = scatter_sum(down_part, "dp").astype(F32)
    gate_grad, up_grad = small_call(
        functools.partial(unpack_kernel, counts), [(gate_weight.shape, F32)] * 2, pair_back
    )
    by_owner = (dp_size, fs_size, weight_rows)
    gain_grads = jnp.concatenate(
        [
            gain_grad.reshape(by_owner),
            mlp_gain_grad.reshape(by_owner),
            jnp.zeros((dp_size, fs_size, 128 - 2 * weight_rows), F32),
        ],
        axis=2,
    )
    gain_grads = jnp.broadcast_to(gain_grads[:, :, None, :], (dp_size, fs_size, 8, 128))
    wide_half = (dp_size, z_size, weight_rows, wide_width)
    out_half = (z_size, weight_rows, width)
    gain_half = (dp_size, z_size, 8, 128)
    grad_act_parts, wide_parts, out_parts, gain_parts = call(
        end_kernel,
        sizes,
        5,
        60,
        [(rows_shape, BF), (wide_half, BF), (out_half, BF), (gain_half, F32)],
        [
            pltpu.VMEM((row_count, width), BF),
            pltpu.VMEM(wide_half, BF),
            pltpu.VMEM(wide_half, BF),
            pltpu.VMEM(out_half, BF),
            pltpu.VMEM(out_half, BF),
            pltpu.VMEM(gain_half, F32),
            pltpu.VMEM(gain_half, F32),
            dma(2, dp_size),
            dma(2, chips),
            dma(2, z_size),
            dma(2, chips),
            dma(2, 3),
            dma(8),
        ],
        [hbm] * 4,
        grad_act,
        wide_grad.reshape(dp_size, z_size, 2, weight_rows, wide_width),
        output_grad.reshape(z_size, 2, weight_rows, width),
        gain_grads.reshape(dp_size, z_size, 2, 8, 128),
    )
    grad_act_one = jnp.sum(grad_act_parts.astype(F32), axis=0)
    own_inverse = lax.rsqrt(jnp.mean(source * source, axis=1, keepdims=True) + EPSILON)
    input_grad = (
        grad_residual + norm_back(grad_act_one, source * own_inverse, own_inverse, gain_one)
    ).astype(BF)
    gain_total = jnp.sum(gain_parts[:, :, 0, :], axis=(0, 1))
    wide_total = jnp.sum(wide_parts.astype(F32), axis=1)

    def from_heads(value):
        return value.transpose(1, 0, 2).reshape(weight_rows, -1)

    return (
        outputs,
        input_grad,
        gain_total[:weight_rows],
        from_heads(wide_total[:, :, :query_width]),
        from_heads(wide_total[:, :, query_width : query_width + HEAD_DIM]),
        from_heads(wide_total[:, :, query_width + HEAD_DIM :]),
        jnp.sum(out_parts.astype(F32), axis=0),
        gain_total[weight_rows : 2 * weight_rows],
        gate_grad,
        up_grad,
        down_grad,
    )


def solution(mesh):
    dp_size, fs_size = mesh.shape["dp"], mesh.shape["fsdp"]
    row = P(ALL, None)
    flat = P(ALL)

    def step(*args):
        return local(dp_size, fs_size, *args)

    return jax.shard_map(
        step,
        mesh=mesh,
        in_specs=(row, flat, flat, row, row, row, row, flat, row, row, row, row),
        out_specs=(row, row, flat, row, row, row, row, flat, row, row, row),
        check_vma=False,
    )
```

```python
import functools

import jax
import jax.numpy as jnp
from jax import lax
from jax.experimental import pallas as pl
from jax.experimental.pallas import tpu as pltpu
from jax.sharding import PartitionSpec as P

HEADS = 32
HEAD_DIM = 64
KV_HEADS = 4
EPSILON = 1e-05
ALL = ("dp", "fsdp")
BF = jnp.bfloat16
F32 = jnp.float32
MESH = pl.DeviceIdType.MESH


def matmul(left_side, right_side):
    return jnp.dot(left_side, right_side, preferred_element_type=F32)


def outer_sum(left_side, right_side):
    return lax.dot_general(
        left_side, right_side, (((0,), (0,)), ((), ())), preferred_element_type=F32
    )


def times_trans(left_side, right_side):
    return lax.dot_general(
        left_side, right_side, (((1,), (1,)), ((), ())), preferred_element_type=F32
    )


def rotary_tables(segments):
    row_count = segments.shape[0]
    row_index = jnp.arange(row_count, dtype=jnp.int32)
    earlier = jnp.sum((segments[None, :] < segments[:, None]).astype(jnp.int32), axis=1)
    places = (row_index - earlier).astype(F32)
    halfway = HEAD_DIM // 2
    frequency = 10000.0 ** (jnp.arange(halfway, dtype=F32) * (-2.0 / HEAD_DIM))
    angles = places[:, None] * frequency[None, :]
    cosine_table, sine_table = jnp.cos(angles), jnp.sin(angles)
    pairs = 128 // HEAD_DIM
    return (
        jnp.concatenate([cosine_table, cosine_table] * pairs, axis=1),
        jnp.concatenate([-sine_table, sine_table] * pairs, axis=1),
    )


def norm_back(upstream, normed, inverse, gain_vec):
    scaled = upstream * gain_vec
    return inverse * (scaled - normed * jnp.mean(scaled * normed, axis=1, keepdims=True))


def gather(value, axes):
    return lax.all_gather(value, axes, axis=0, tiled=True)


def scatter_sum(value, axes):
    return lax.psum_scatter(value, axes, scatter_dimension=0, tiled=True)


def place():
    d, f = lax.axis_index("dp"), lax.axis_index("fsdp")
    return d, f // 2, f % 2


def device(d, z, c):
    return {"dp": d, "fsdp": 2 * z + c}


def remote(src, dst, sems, index, target):
    return pltpu.make_async_remote_copy(
        src_ref=src,
        dst_ref=dst,
        send_sem=sems.at[0, index],
        recv_sem=sems.at[1, index],
        device_id=target,
        device_id_type=MESH,
    )


def hop(src, dst, sems, send, recv, target):
    return pltpu.make_async_remote_copy(
        src_ref=src,
        dst_ref=dst,
        send_sem=sems.at[0, send],
        recv_sem=sems.at[1, recv],
        device_id=target,
        device_id_type=MESH,
    )


def chain(z_size, shard, sems, first):
    d, z, c = place()

    def copy(s, to, send=None, src=None):
        src = shard(s) if src is None else src
        return hop(src, shard(s), sems, s if send is None else send, s, device(d, to, c))

    up, down = z < z_size - 1, z > 0

    def start():
        @pl.when(up)
        def _():
            copy(z, z + 1, src=first).start()

        @pl.when(down)
        def _():
            copy(z, z - 1, z_size, first).start()

    def go(arrived, low=1, high=z_size):
        def step(k):
            @pl.when(z - k >= 0)
            def _():
                copy(z - k, z).wait_recv()

                @pl.when(up)
                def _():
                    copy(z - k, z + 1).start()

                arrived(z - k)

            @pl.when(z + k < z_size)
            def _():
                copy(z + k, z).wait_recv()

                @pl.when(down)
                def _():
                    copy(z + k, z - 1).start()

                arrived(z + k)

        loop(low, high, step)

    def finish():
        @pl.when(up)
        def _():
            copy(z, z + 1, src=first).wait_send()

        @pl.when(down)
        def _():
            copy(z, z - 1, z_size, first).wait_send()

        def step(k):
            @pl.when((z - k >= 0) & up)
            def _():
                copy(z - k, z + 1).wait_send()

            @pl.when((z + k < z_size) & down)
            def _():
                copy(z + k, z - 1).wait_send()

        loop(1, z_size, step)

    return start, go, finish


def ring_place(q, size):
    q = (q + size) % size
    return q + (q // 2) * (1 - 2 * (q % 2)) if size == 4 else q


def loop(low, high, body):
    def step(index, carry):
        body(index)
        return carry

    lax.fori_loop(low, high, step, 0)


def greet(sizes, same_core=False, along_dp=False, along_fsdp=False, partner=False):
    dp_size, z_size = sizes
    d, z, c = place()
    barrier = pltpu.get_barrier_semaphore()

    def signal(target):
        pl.semaphore_signal(barrier, inc=1, device_id=target, device_id_type=MESH)

    count = 0
    if same_core:

        def to_chip(p):
            signal(device((d + p // z_size) % dp_size, (z + p % z_size) % z_size, c))

        loop(1, dp_size * z_size, to_chip)
        count += dp_size * z_size - 1
    if along_dp:
        loop(1, dp_size, lambda p: signal(device((d + p) % dp_size, z, c)))
        count += dp_size - 1
    if along_fsdp:
        f_size = 2 * z_size

        def to_line(p):
            signal({"dp": d, "fsdp": (2 * z + c + p) % f_size})

        loop(1, f_size, to_line)
        count += f_size - 1
    if partner:
        signal(device(d, z, 1 - c))
        count += 1
    pl.semaphore_wait(barrier, count)


def call(kernel, sizes, number, micros, outs, scratch, spaces, *args, kept=0):
    far = len(outs) - kept
    return pl.pallas_call(
        functools.partial(kernel, sizes),
        out_shape=tuple(jax.ShapeDtypeStruct(shape, dtype) for shape, dtype in outs),
        in_specs=[pl.BlockSpec(memory_space=space) for space in spaces],
        out_specs=tuple(
            pl.BlockSpec(memory_space=pltpu.HBM if k < far else pltpu.VMEM)
            for k in range(len(outs))
        ),
        scratch_shapes=scratch,
        compiler_params=pltpu.CompilerParams(collective_id=number, has_side_effects=True),
        cost_estimate=pl.CostEstimate(
            flops=int(micros * 1e9), bytes_accessed=0, transcendentals=0
        ),
        name=kernel.__name__,
    )(*args)


def dma(*shape):
    return pltpu.SemaphoreType.DMA(shape)


def start_kernel(sizes, *refs):
    x, seg_row, first_gain, second_gain, query, key, value, out, gate, up = refs[:10]
    xs, segs, gains, wides, outs, packed, seg, gain, wide = refs[10:19]
    sems = refs[19:]
    x_sem, seg_sem, gain_sem, piece_sem, wide_sem, out_sem = sems[:6]
    gain_fwd, wide_fwd, out_fwd, own_sem = sems[6:]
    dp_size, z_size = sizes
    chips = dp_size * z_size
    d, z, c = place()
    f = 2 * z + c
    rows, share = query.shape[0], query.shape[1] // dp_size
    for g in range(dp_size):
        low = g * HEAD_DIM
        ends = [part[:, low : low + HEAD_DIM].astype(F32) for part in (key, value)]
        wide[g, :, :share] = query[:, g * share : (g + 1) * share]
        wide[g, :, share:] = jnp.concatenate(ends, axis=1).astype(BF)
    gain_row = jnp.concatenate(
        [
            first_gain[...].astype(F32),
            second_gain[...].astype(F32),
            jnp.zeros((1, 128 - 2 * rows), F32),
        ][: 2 if rows == 64 else 3],
        axis=1,
    )
    gain[...] = jnp.broadcast_to(gain_row, gain.shape).astype(BF)
    seg[...] = jnp.broadcast_to(seg_row[...], seg.shape)
    greet(sizes, same_core=True, partner=True)
    other = device(d, z, 1 - c)

    def piece_copy(p):
        to = (d + p) % dp_size
        return remote(wide.at[to], wides.at[d, f], piece_sem, p, device(to, z, c))

    def gain_copy(p):
        to_d, to_z = (d + p // z_size) % dp_size, (z + p % z_size) % z_size
        return remote(gain, gains.at[d, f], gain_sem, p, device(to_d, to_z, c))

    def x_copy(p):
        return remote(x, xs.at[d], x_sem, p, device((d + p) % dp_size, z, c))

    def seg_copy(p):
        return remote(seg, segs.at[d], seg_sem, p, device((d + p) % dp_size, z, c))

    def out_pass(s):
        slot = outs.at[2 * s + c]
        return remote(slot, slot, out_fwd, s, other)

    def wide_pass(s):
        slot = wides.at[:, 2 * s + c]
        return remote(slot, slot, wide_fwd, s, other)

    def gain_pass(p):
        from_d = (d - p // z_size + dp_size) % dp_size
        slot = gains.at[from_d, 2 * ((z - p % z_size + z_size) % z_size) + c]
        return remote(slot, slot, gain_fwd, p, other)

    out_start, out_go, out_finish = chain(z_size, lambda s: outs.at[2 * s + c], out_sem, out)
    wide_start, wide_go, wide_finish = chain(
        z_size, lambda s: wides.at[:, 2 * s + c], wide_sem, wides.at[:, f]
    )
    own = [
        pltpu.make_async_copy(wide.at[d], wides.at[d, f], own_sem.at[0]),
        pltpu.make_async_copy(x, xs.at[d], own_sem.at[1]),
        pltpu.make_async_copy(seg, segs.at[d], own_sem.at[2]),
        pltpu.make_async_copy(gain, gains.at[d, f], own_sem.at[3]),
        pltpu.make_async_copy(out, outs.at[f], own_sem.at[4]),
    ]
    loop(1, dp_size, lambda p: piece_copy(p).start())
    for copy in own:
        copy.start()
    out_start()
    loop(1, chips, lambda p: gain_copy(p).start())
    loop(1, dp_size, lambda p: seg_copy(p).start())
    loop(1, dp_size, lambda p: x_copy(p).start())
    passed = [
        remote(gain, gains.at[d, f], gain_fwd, 0, other),
        remote(out, outs.at[f], out_fwd, z, other),
    ]
    for copy in passed:
        copy.start()
    own[0].wait()
    loop(1, dp_size, lambda p: piece_copy(p).wait())
    wide_start()
    wide_pass(z).start()
    pack((dp_size, 2 * z_size, gate.shape[1] // (2 * chips)), gate, up, packed)
    out_go(lambda s: out_pass(s).start())
    wide_go(lambda s: wide_pass(s).start())

    def pass_gain(p):
        gain_copy(p).wait_recv()
        gain_pass(p).start()

    loop(1, chips, pass_gain)
    loop(1, dp_size, lambda p: seg_copy(p).wait())
    loop(1, dp_size, lambda p: x_copy(p).wait())
    for copy in own[1:]:
        copy.wait()
    for copy in passed:
        copy.wait()
    wide_pass(z).wait()

    def end_pass(k):
        s = (z + k) % z_size
        out_pass(s).wait()
        wide_pass(s).wait()

    loop(1, z_size, end_pass)
    loop(1, chips, lambda p: gain_pass(p).wait())
    loop(1, chips, lambda p: gain_copy(p).wait_send())
    out_finish()
    wide_finish()


def gather_line(sizes, *refs):
    rows, pair, cot, down = refs[:4]
    rows_out, pair_out, hid_out, grad_out = refs[4:8]
    act_v, pair_v, cot_v, down_v, both, hidden = refs[8:14]
    rows_sem, pass_sem, pair_sem, own_sem = refs[14:]
    dp_size, z_size = sizes
    d, z, c = place()
    f = 2 * z + c
    greet(sizes, along_dp=True, along_fsdp=True)
    q = ring_place(d, dp_size)
    right, left = ring_place(q + 1, dp_size), ring_place(q - 1, dp_size)
    across = ring_place((q + 2) % dp_size, dp_size)
    other = device(d, z, 1 - c)
    depth = pair.shape[0]
    half = depth // 2

    def rows_pass(s):
        slot = act_v.at[2 * s + c]
        return remote(slot, slot, pass_sem, s, other)

    def whole_copy(to, index):
        return remote(pair, pair_v.at[d], pair_sem, index, device(to, z, c))

    def half_copy(source, to, low, index):
        slot = pair_v.at[source, pl.ds(low, half)]
        return remote(slot, slot, pair_sem, index, device(to, z, c))

    start, go, finish = chain(z_size, lambda s: act_v.at[2 * s + c], rows_sem, rows)
    start()
    to_right, to_left = whole_copy(right, 0), whole_copy(left, 1)
    to_right.start()
    to_left.start()
    takes = [
        pltpu.make_async_copy(rows, act_v.at[f], own_sem.at[0]),
        pltpu.make_async_copy(cot, cot_v, own_sem.at[1]),
        pltpu.make_async_copy(down, down_v, own_sem.at[2]),
        pltpu.make_async_copy(pair, pair_v.at[d], own_sem.at[3]),
    ]
    for copy in takes:
        copy.start()
    passed = remote(rows, act_v.at[f], pass_sem, z, other)
    passed.start()
    for copy in takes:
        copy.wait()
    tall = 256

    def tile(i):
        return pl.ds(pl.multiple_of(i * tall, tall), tall)

    def hidden_tile(i):
        hidden[tile(i), :] = times_trans(cot_v[tile(i), :], down_v[...])

    loop(0, cot.shape[0] // tall, hidden_tile)
    go(lambda s: rows_pass(s).start(), 1, z_size - 1)
    to_right.wait_recv()
    on_right = half_copy(left, right, 0, 2)
    on_right.start()
    to_left.wait_recv()
    on_left = half_copy(right, left, half, 3)
    on_left.start()
    go(lambda s: rows_pass(s).start(), z_size - 1)
    passed.wait()
    loop(1, z_size, lambda k: rows_pass((z + k) % z_size).wait())
    give_rows = pltpu.make_async_copy(act_v, rows_out, own_sem.at[4])
    give_rows.start()

    def product(i, block, low, high):
        lanes = pl.ds(pl.multiple_of(block * depth, depth), depth)
        left_side = act_v[pl.ds(2 * i, 2), :, lanes].reshape(tall, depth)
        return matmul(left_side, pair_v[block, :, low:high])

    columns = pair.shape[1]
    cuts = [(low, min(low + 256, columns)) for low in range(0, columns, 256)]

    def first_tile(i):
        for low, high in cuts:
            both[tile(i), low:high] = (
                product(i, d, low, high)
                + product(i, left, low, high)
                + product(i, right, low, high)
            )

    def last_tile(i):
        for low, high in cuts:
            both[tile(i), low:high] = both[tile(i), low:high] + product(i, across, low, high)

    loop(0, both.shape[0] // tall, first_tile)
    on_right.wait_recv()
    on_left.wait_recv()
    give_pair = pltpu.make_async_copy(pair_v, pair_out, own_sem.at[5])
    give_pair.start()
    loop(0, both.shape[0] // tall, last_tile)
    share = columns // 2

    def unit(i):
        at = pl.ds(pl.multiple_of(i * 64, 64), 64)
        values = both[at, :]
        gate, up, upstream = values[:, :share], values[:, share:], hidden[at, :]
        sigmoid = jax.nn.sigmoid(gate)
        hid_out[at, :] = (gate * sigmoid * up).astype(BF)
        grad_gate = upstream * up * sigmoid * (1.0 + gate * (1.0 - sigmoid))
        grad_up = upstream * gate * sigmoid
        grad_out[at, :] = jnp.concatenate([grad_gate, grad_up], axis=1).astype(BF)

    loop(0, both.shape[0] // 64, unit)
    give_rows.wait()
    give_pair.wait()
    finish()
    to_right.wait_send()
    to_left.wait_send()
    on_right.wait_send()
    on_left.wait_send()


def scatter_line(sizes, *refs):
    part, pair, hid, hid_turned, down, cot = refs[:6]
    part_out, pair_out, mlp_out, grad_out = refs[6:10]
    mine, theirs, got_a, got_b, my_a, my_b, pair_own = refs[10:17]
    hid_v, turned_v, down_v, cot_v, mlp_v, grad_v = refs[17:23]
    part_sem, swap_sem, load_sem, own_sem, pair_sem, mat_sem = refs[23:]
    dp_size, z_size = sizes
    d, z, c = place()
    greet(sizes, along_dp=True, along_fsdp=True)
    other = device(d, z, 1 - c)
    q = ring_place(d, dp_size)
    right, left = ring_place(q + 1, dp_size), ring_place(q - 1, dp_size)
    across = ring_place((q + 2) % dp_size, dp_size)
    to_right, to_left = device(right, z, c), device(left, z, c)
    half = pair.shape[1] // 2
    rows_a, rows_b = pl.ds(0, half), pl.ds(half, half)

    def swap_copy(p):
        to = (z + p) % z_size
        return remote(part.at[to, 1 - c], theirs.at[to], swap_sem, p, other)

    def load(p):
        to = (z + p) % z_size
        return pltpu.make_async_copy(part.at[to, c], mine.at[to], load_sem.at[p])

    def part_copy(p):
        to = (z + p) % z_size
        return remote(mine.at[to], part_out.at[z], part_sem, p, device(d, to, c))

    def begin(p):
        swap_copy(p).start()
        load(p).start()

    def add(p):
        to = (z + p) % z_size
        swap_copy(p).wait()
        load(p).wait()
        mine[to] = (mine[to].astype(F32) + theirs[to].astype(F32)).astype(BF)

    def send(p):
        add(p)
        part_copy(p).start()

    loop(1, z_size, begin)
    begin(0)
    ring = [
        remote(pair.at[across, rows_a], got_a, pair_sem, 0, to_right),
        remote(pair.at[across, rows_b], got_b, pair_sem, 1, to_left),
        remote(pair.at[right, rows_b], pair_out.at[0, rows_b], pair_sem, 2, to_right),
        remote(pair.at[left, rows_a], pair_out.at[1, rows_a], pair_sem, 3, to_left),
        remote(my_a, pair_out.at[0, rows_a], pair_sem, 4, to_right),
        remote(my_b, pair_out.at[1, rows_b], pair_sem, 5, to_left),
    ]
    for copy in ring[:4]:
        copy.start()
    takes = [
        pltpu.make_async_copy(pair.at[right, rows_a], my_a, own_sem.at[1]),
        pltpu.make_async_copy(pair.at[left, rows_b], my_b, own_sem.at[2]),
        pltpu.make_async_copy(pair.at[d], pair_own, own_sem.at[3]),
    ]
    mats = [
        pltpu.make_async_copy(hid, hid_v, mat_sem.at[0]),
        pltpu.make_async_copy(down, down_v, mat_sem.at[1]),
        pltpu.make_async_copy(hid_turned, turned_v, mat_sem.at[2]),
        pltpu.make_async_copy(cot, cot_v, mat_sem.at[3]),
    ]
    loop(1, z_size, send)
    for copy in takes + mats:
        copy.start()
    add(0)
    own = pltpu.make_async_copy(mine.at[z], part_out.at[z], own_sem.at[0])
    own.start()
    takes[2].wait()
    give = pltpu.make_async_copy(pair_own, pair_out.at[2], own_sem.at[4])
    give.start()
    mats[0].wait()
    mats[1].wait()
    tall = 256

    def mlp_tile(i):
        rows = pl.ds(pl.multiple_of(i * tall, tall), tall)
        for low in range(0, mlp_v.shape[1], 512):
            product = matmul(hid_v[rows, :], down_v[:, low : low + 512])
            mlp_v[rows, low : low + 512] = product.astype(BF)

    loop(0, mlp_v.shape[0] // tall, mlp_tile)
    give_mlp = pltpu.make_async_copy(mlp_v, mlp_out, mat_sem.at[4])
    give_mlp.start()

    def merge(total, got):
        def chunk(i):
            rows = pl.ds(pl.multiple_of(i * 32, 32), 32)
            total[rows, :] = (total[rows, :].astype(F32) + got[rows, :].astype(F32)).astype(BF)

        loop(0, half // 32, chunk)

    takes[0].wait()
    ring[0].wait_recv()
    merge(my_a, got_a)
    ring[4].start()
    takes[1].wait()
    ring[1].wait_recv()
    merge(my_b, got_b)
    ring[5].start()
    mats[2].wait()
    mats[3].wait()

    def grad_tile(i):
        lanes = pl.ds(pl.multiple_of(i * 256, 256), 256)
        grad_v[:, lanes] = matmul(turned_v[...], cot_v[:, lanes]).astype(BF)

    loop(0, grad_v.shape[1] // 256, grad_tile)
    give_grad = pltpu.make_async_copy(grad_v, grad_out, mat_sem.at[5])
    give_grad.start()
    own.wait()
    give.wait()
    give_mlp.wait()
    give_grad.wait()
    ring[0].wait_send()
    ring[1].wait_send()
    for copy in ring[2:]:
        copy.wait()
    loop(1, z_size, lambda p: part_copy(p).wait())


def end_kernel(sizes, rows, wide, out, gain, rows_out, wide_out, out_out, gain_out, *scratch):
    rows_own = scratch[0]
    groups = [scratch[1:5], scratch[5:9], scratch[9:13]]
    rows_sem, wide_sem, gain_sem, swap_sem, load_sem, line_sem, own_sem = scratch[13:]
    dp_size, z_size = sizes
    d, z, c = place()
    greet(sizes, along_dp=True, along_fsdp=True)
    other = device(d, z, 1 - c)

    def source(kind, t, core):
        return (out.at[t, core], wide.at[:, t, core], gain.at[:, t, core])[kind]

    def swap_copy(kind, t):
        theirs = groups[kind][1].at[t]
        return remote(source(kind, t, 1 - c), theirs, swap_sem, kind * z_size + t, other)

    def load(kind, t):
        sem = load_sem.at[kind * z_size + t]
        return pltpu.make_async_copy(source(kind, t, c), groups[kind][0].at[t], sem)

    def begin(k):
        t = (z + k) % z_size
        for kind in range(3):
            swap_copy(kind, t).start()
            load(kind, t).start()

    def rows_copy(p):
        to = (d + p) % dp_size
        return remote(rows.at[to], rows_out.at[d], rows_sem, p, device(to, z, c))

    loop(1, z_size + 1, begin)
    loop(1, dp_size, lambda p: rows_copy(p).start())
    rows_in = pltpu.make_async_copy(rows.at[d], rows_own, own_sem.at[0])
    rows_in.start()

    def merge(t, k):
        for mine, got in ((group[0], group[k]) for group in groups):
            if len(mine.shape) == 3:
                mine[t] = (mine[t].astype(F32) + got[t].astype(F32)).astype(mine.dtype)
            else:

                def part(g):
                    mine[t, g] = (mine[t, g].astype(F32) + got[t, g].astype(F32)).astype(mine.dtype)

                loop(0, dp_size, part)

    def line_copy(kind, t, way):
        mine, got = groups[kind][0].at[t], groups[kind][way].at[t]
        index = (2 * kind + way - 2) * z_size + t
        to = z + 1 if way == 2 else z - 1
        return remote(mine, got, line_sem, index, device(d, to, c))

    def ready(t):
        for kind in range(3):
            swap_copy(kind, t).wait()
            load(kind, t).wait()
        merge(t, 1)

    def take(t, way):
        for kind in range(3):
            line_copy(kind, t, way).wait_recv()
        merge(t, way)

    def give(t, way):
        for kind in range(3):
            line_copy(kind, t, way).start()

    def rise(high):
        @pl.when(high > z)
        def _():
            ready(high)

            @pl.when(z > 0)
            def _():
                take(high, 2)

            give(high, 2)

    def fall(low):
        @pl.when(low < z)
        def _():
            ready(low)

            @pl.when(z < z_size - 1)
            def _():
                take(low, 3)

            give(low, 3)

    def step(k):
        near_top = z >= z_size // 2

        @pl.when(near_top)
        def _():
            fall(k - 1)

        rise(z_size - k)

        @pl.when(jnp.logical_not(near_top))
        def _():
            fall(k - 1)

    loop(1, z_size, step)
    ready(z)

    @pl.when(z > 0)
    def _():
        take(z, 2)

    @pl.when(z < z_size - 1)
    def _():
        take(z, 3)

    out_mine, wide_mine, gain_mine = (group[0] for group in groups)

    def wide_copy(p):
        to = (d + p) % dp_size
        return remote(wide_mine.at[z, to], wide_out.at[d], wide_sem, p, device(to, z, c))

    def gain_copy(p):
        to = (d + p) % dp_size
        return remote(gain_mine.at[z, to], gain_out.at[d], gain_sem, p, device(to, z, c))

    loop(1, dp_size, lambda p: wide_copy(p).start())
    loop(1, dp_size, lambda p: gain_copy(p).start())
    rows_in.wait()
    own = [
        pltpu.make_async_copy(rows_own, rows_out.at[d], own_sem.at[1]),
        pltpu.make_async_copy(out_mine.at[z], out_out, own_sem.at[2]),
        pltpu.make_async_copy(wide_mine.at[z, d], wide_out.at[d], own_sem.at[3]),
        pltpu.make_async_copy(gain_mine.at[z, d], gain_out.at[d], own_sem.at[4]),
    ]
    for copy in own:
        copy.start()
    for copy in own:
        copy.wait()

    def sent(k):
        high, low = z_size - k, k - 1

        @pl.when(high > z)
        def _():
            for kind in range(3):
                line_copy(kind, high, 2).wait_send()

        @pl.when(low < z)
        def _():
            for kind in range(3):
                line_copy(kind, low, 3).wait_send()

    loop(1, z_size, sent)
    loop(1, dp_size, lambda p: rows_copy(p).wait())
    loop(1, dp_size, lambda p: wide_copy(p).wait())
    loop(1, dp_size, lambda p: gain_copy(p).wait())


def turned(value):
    lane = lax.broadcasted_iota(jnp.int32, value.shape, 1)
    ahead, behind = pltpu.roll(value, 128 - HEAD_DIM // 2, 1), pltpu.roll(value, HEAD_DIM // 2, 1)
    return jnp.where(lane % HEAD_DIM < HEAD_DIM // 2, ahead, behind)


def low_lanes(value):
    lane = lax.broadcasted_iota(jnp.int32, value.shape, 1)
    return jnp.where(lane < HEAD_DIM, value, jnp.zeros_like(value))


def high_lanes(value):
    lane = lax.broadcasted_iota(jnp.int32, value.shape, 1)
    return jnp.where(lane < HEAD_DIM, jnp.zeros_like(value), value)


def both_sides(value):
    low = low_lanes(value)
    return low, pltpu.roll(low, HEAD_DIM, 1)


def attend_forward(sizes, *refs):
    xs, gain, mask, cosine, sine, wides, out, pair, down = refs[:9]
    rows_out, pair_out, down_out, probs, query_out, keyval_out, mixed_out, act_out = refs[9:17]
    mixed_v = refs[-1]
    parts, pair_own, down_own, rows_sem, pair_sem, own_sem, down_sem = refs[17:-1]
    dp_size, z_size = sizes
    f_size = 2 * z_size
    d, z, c = place()
    f = 2 * z + c
    pairs = query_out.shape[2] // 128
    greet(sizes, along_dp=True, along_fsdp=True)

    def pair_copy(p):
        to = (f + p) % f_size
        return remote(pair.at[to], pair_out.at[f], pair_sem, p, {"dp": d, "fsdp": to})

    def rows_copy(p):
        to = (d + p) % dp_size
        return remote(parts.at[to], rows_out.at[d], rows_sem, p, device(to, z, c))

    def down_copy(p):
        return remote(down, down_out.at[d], down_sem, p, device((d + p) % dp_size, z, c))

    loop(1, f_size, lambda p: pair_copy(p).start())
    loop(1, dp_size, lambda p: down_copy(p).start())
    take = pltpu.make_async_copy(pair.at[f], pair_own, own_sem.at[0])
    take.start()
    take_down = pltpu.make_async_copy(down, down_own, own_sem.at[3])
    take_down.start()
    take.wait()
    give = pltpu.make_async_copy(pair_own, pair_out.at[f], own_sem.at[1])
    give.start()
    take_down.wait()
    give_down = pltpu.make_async_copy(down_own, down_out.at[d], own_sem.at[4])
    give_down.start()

    def block(g):
        source = xs[g].astype(F32)
        inverse = lax.rsqrt(jnp.mean(source * source, axis=1, keepdims=True) + EPSILON)
        act = (source * inverse * gain[...]).astype(BF)
        tokens = pl.ds(pl.multiple_of(g * act.shape[0], act.shape[0]), act.shape[0])
        act_out[:, tokens] = act.T
        rows = matmul(act, wides[...])
        cosine_table, sine_table = cosine[g], sine[g]
        keyval = rows[:, pairs * 128 :]
        key = (keyval * cosine_table + turned(keyval) * sine_table).astype(BF).astype(F32)
        value = keyval.astype(BF).astype(F32)
        keyval_out[g] = jnp.where(
            lax.broadcasted_iota(jnp.int32, key.shape, 1) < HEAD_DIM, key, value
        ).astype(BF)
        keys = [side.astype(BF) for side in both_sides(key)]
        values = [side.astype(BF) for side in both_sides(pltpu.roll(value, HEAD_DIM, 1))]
        allowed = mask[g] > 0
        for pair_index in range(pairs):
            lanes = pl.ds(pair_index * 128, 128)
            query = rows[:, pair_index * 128 : pair_index * 128 + 128]
            query = (query * cosine_table + turned(query) * sine_table).astype(BF)
            query_out[g, :, lanes] = query
            mixed = jnp.zeros(query.shape, F32)
            for side in range(2):
                raw = times_trans(query, keys[side])
                scores = jnp.where(allowed, raw * HEAD_DIM ** (-0.5), -1e30)
                powers = jnp.exp(scores - jnp.max(scores, axis=1, keepdims=True))
                weights = powers / jnp.sum(powers, axis=1, keepdims=True)
                probs[g, 2 * pair_index + side] = weights
                mixed += matmul(weights.astype(BF), values[side])
            mixed_v[:, lanes] = mixed.astype(BF)
        parts[g] = matmul(mixed_v[...], out[...]).astype(BF)
        mixed_out[:, tokens] = mixed_v[...].T

    def send(p):
        block((d + p) % dp_size)

        @pl.when(p < dp_size)
        def _():
            rows_copy(p).start()

    loop(1, dp_size + 1, send)
    own = pltpu.make_async_copy(parts.at[d], rows_out.at[d], own_sem.at[2])
    own.start()
    own.wait()
    give.wait()
    give_down.wait()
    loop(1, dp_size, lambda p: rows_copy(p).wait())
    loop(1, dp_size, lambda p: down_copy(p).wait())
    loop(1, f_size, lambda p: pair_copy(p).wait())


def attend_backward(sizes, *refs):
    rows, xs, cosine, sine, wides, out, probs, query_in, keyval_in, mixed, act = refs[:11]
    pair, down, pair_out, down_out, wide_grad, output_grad, grad_act, gain_grad = refs[11:19]
    held, pair_own, down_own, grad_wide, rows_sem, pair_sem, own_sem, down_sem = refs[19:]
    dp_size, z_size = sizes
    f_size = 2 * z_size
    d, z, c = place()
    f = 2 * z + c
    pairs = query_in.shape[2] // 128
    greet(sizes, along_dp=True, along_fsdp=True)

    def pair_copy(p):
        to = (f + p) % f_size
        return remote(pair.at[to], pair_out.at[f], pair_sem, p, {"dp": d, "fsdp": to})

    def rows_copy(p):
        return remote(rows, held.at[d], rows_sem, p, device((d + p) % dp_size, z, c))

    def down_copy(p):
        to = (d + p) % dp_size
        return remote(down.at[to], down_out.at[d], down_sem, p, device(to, z, c))

    loop(1, dp_size, lambda p: rows_copy(p).start())
    loop(1, f_size, lambda p: pair_copy(p).start())
    loop(1, dp_size, lambda p: down_copy(p).start())
    take_down = pltpu.make_async_copy(down.at[d], down_own, own_sem.at[3])
    take_down.start()
    take = pltpu.make_async_copy(pair.at[f], pair_own, own_sem.at[0])
    take.start()
    own = pltpu.make_async_copy(rows, held.at[d], own_sem.at[2])
    own.start()
    take.wait()
    give = pltpu.make_async_copy(pair_own, pair_out.at[f], own_sem.at[1])
    give.start()
    take_down.wait()
    give_down = pltpu.make_async_copy(down_own, down_out.at[d], own_sem.at[4])
    give_down.start()
    gain_grad[...] = jnp.zeros_like(gain_grad)

    def block(g):
        tokens = pl.ds(pl.multiple_of(g * rows.shape[0], rows.shape[0]), rows.shape[0])
        grad_mixed = times_trans(held[g], out[...]).astype(BF)
        cosine_table, sine_table = cosine[g], sine[g]
        keyval = keyval_in[g].astype(F32)
        keys = [side.astype(BF) for side in both_sides(keyval)]
        values = [side.astype(BF) for side in both_sides(pltpu.roll(keyval, HEAD_DIM, 1))]
        key_sums = [jnp.zeros(keyval.shape, F32), jnp.zeros(keyval.shape, F32)]
        value_sums = [jnp.zeros(keyval.shape, F32), jnp.zeros(keyval.shape, F32)]
        for pair_index in range(pairs):
            lanes = pl.ds(pair_index * 128, 128)
            up = grad_mixed[:, pair_index * 128 : pair_index * 128 + 128]
            query = query_in[g, :, lanes]
            grad_query = jnp.zeros(query.shape, F32)
            for side in range(2):
                weights = probs[g, 2 * pair_index + side]
                grad_probs = times_trans(up, values[side])
                value_sums[side] += outer_sum(weights.astype(BF), up)
                inner = jnp.sum(weights * grad_probs, axis=1, keepdims=True)
                grad_raw = (HEAD_DIM ** (-0.5) * weights * (grad_probs - inner)).astype(BF)
                grad_query += matmul(grad_raw, keys[side])
                key_sums[side] += outer_sum(grad_raw, query)
            grad_query = grad_query * cosine_table - turned(grad_query) * sine_table
            grad_wide[tokens, lanes] = grad_query.astype(BF)
        grad_key = key_sums[0] + pltpu.roll(key_sums[1], HEAD_DIM, 1)
        grad_key = grad_key * cosine_table - turned(grad_key) * sine_table
        grad_value = value_sums[1] + pltpu.roll(value_sums[0], HEAD_DIM, 1)
        lane = lax.broadcasted_iota(jnp.int32, grad_key.shape, 1)
        grad_wide[tokens, pl.ds(pairs * 128, 128)] = jnp.where(
            lane < HEAD_DIM, grad_key, grad_value
        ).astype(BF)
        grad = times_trans(grad_wide[tokens, :], wides[...])
        grad_act[g] = grad.astype(BF)
        source = xs[g].astype(F32)
        inverse = lax.rsqrt(jnp.mean(source * source, axis=1, keepdims=True) + EPSILON)
        gain_grad[...] += jnp.sum(source * inverse * grad, axis=0, keepdims=True)

    def arrive(p):
        @pl.when(p == 0)
        def _():
            own.wait()

        @pl.when(p > 0)
        def _():
            rows_copy(p).wait_recv()

        block((d - p + dp_size) % dp_size)

    loop(0, dp_size, arrive)

    def wide_tile(i):
        rows_at = pl.ds(pl.multiple_of(i * 256, 256), 256)
        wide_grad[rows_at, :] = matmul(act[rows_at, :], grad_wide[...]).astype(BF)

    def output_tile(i):
        lanes = pl.ds(pl.multiple_of(i * 256, 256), 256)
        upstream = held[:, :, lanes].reshape(mixed.shape[1], 256)
        output_grad[:, lanes] = matmul(mixed[...], upstream).astype(BF)

    loop(0, act.shape[0] // 256, wide_tile)
    loop(0, rows.shape[1] // 256, output_tile)
    give.wait()
    give_down.wait()
    loop(1, dp_size, lambda p: down_copy(p).wait())
    loop(1, dp_size, lambda p: rows_copy(p).wait_send())
    loop(1, f_size, lambda p: pair_copy(p).wait())


def pack(counts, gate, up, packed):
    dp_size, fs_size, unit = counts
    for f in range(fs_size):
        pieces = []
        for weight in (gate, up):
            for g in range(dp_size):
                low = (g * fs_size + f) * unit
                pieces.append(weight[:, low : low + unit].astype(F32))
        packed[f] = jnp.concatenate(pieces, axis=1).astype(BF)


def unpack_kernel(counts, packed, gate, up):
    dp_size, fs_size, unit = counts
    for half, grad in enumerate((gate, up)):
        for g in range(dp_size):
            low = (half * dp_size + g) * unit
            pieces = [packed[f, :, low : low + unit].astype(F32) for f in range(fs_size)]
            grad[:, g * fs_size * unit : (g + 1) * fs_size * unit] = jnp.concatenate(
                pieces, axis=1
            )


def small_call(kernel, outs, *args):
    return pl.pallas_call(
        kernel,
        out_shape=tuple(jax.ShapeDtypeStruct(shape, dtype) for shape, dtype in outs),
        cost_estimate=pl.CostEstimate(flops=int(3e9), bytes_accessed=0, transcendentals=0),
    )(*args)


def local(
    dp_size,
    fs_size,
    inputs,
    segment_ids,
    attn_gain,
    query_weight,
    key_weight,
    value_weight,
    output_weight,
    mlp_gain,
    gate_weight,
    up_weight,
    down_weight,
    cotangent,
):
    z_size = fs_size // 2
    sizes = (dp_size, z_size)
    row_count, width = inputs.shape
    weight_rows, ff_width = gate_weight.shape
    unit = down_weight.shape[0]
    share = dp_size * unit
    heads = HEADS // dp_size
    query_width = heads * HEAD_DIM
    wide_width = query_width + 2 * HEAD_DIM
    vmem, hbm = pltpu.VMEM, pltpu.HBM

    counts = (dp_size, fs_size, unit)
    pair_shape = (fs_size, weight_rows, 2 * share)
    chips = dp_size * z_size
    xs, segs, gains, wides, out_full, pair = call(
        start_kernel,
        sizes,
        0,
        50,
        [
            ((dp_size, row_count, width), BF),
            ((dp_size, 8, row_count), jnp.int32),
            ((dp_size, fs_size, 16, 128), BF),
            ((dp_size, fs_size, weight_rows, wide_width), BF),
            ((fs_size, weight_rows, width), BF),
            (pair_shape, BF),
        ],
        [
            pltpu.VMEM((8, row_count), jnp.int32),
            pltpu.VMEM((16, 128), BF),
            pltpu.VMEM((dp_size, weight_rows, wide_width), BF),
            dma(2, dp_size),
            dma(2, dp_size),
            dma(2, chips),
            dma(2, dp_size),
            dma(2, z_size + 1),
            dma(2, z_size + 1),
            dma(2, chips),
            dma(2, z_size),
            dma(2, z_size),
            dma(5),
        ],
        [vmem] * 10,
        inputs,
        segment_ids[None, :],
        attn_gain[None, :],
        mlp_gain[None, :],
        query_weight,
        key_weight,
        value_weight,
        output_weight,
        gate_weight,
        up_weight,
        kept=1,
    )
    cot_late, xs = lax.optimization_barrier((cotangent, xs))
    cot_full = gather(cot_late, "fsdp")
    gains = gains[:, :, 0, :].astype(F32)
    gain_one = gains[:, :, :weight_rows].reshape(width)
    gain_two = gains[:, :, weight_rows : 2 * weight_rows].reshape(width)
    wides = wides.reshape(width, wide_width)
    out_full = out_full.reshape(query_width, width)

    segs = segs[:, 0, :]
    cosine_table, sine_table = jax.vmap(rotary_tables)(segs)
    row_index = jnp.arange(row_count, dtype=jnp.int32)
    allowed = (segs[:, :, None] == segs[:, None, :]) & (
        row_index[:, None] >= row_index[None, :]
    )
    mask = allowed.astype(F32)
    by_row = (dp_size, row_count)
    rows_shape = by_row + (width,)
    cross_sems = [dma(2, dp_size), dma(2, fs_size), dma(5)]
    mixed_parts, pair_rows, down_full, probs, query_rot, keyval, mixed_low, act_one = call(
        attend_forward,
        sizes,
        1,
        40,
        [
            (rows_shape, BF),
            (pair_shape, BF),
            ((dp_size,) + down_weight.shape, BF),
            ((dp_size, heads, row_count, row_count), F32),
            (by_row + (query_width,), BF),
            (by_row + (128,), BF),
            ((query_width, dp_size * row_count), BF),
            ((width, dp_size * row_count), BF),
        ],
        [
            pltpu.VMEM(rows_shape, BF),
            pltpu.VMEM(pair_shape[1:], BF),
            pltpu.VMEM(down_weight.shape, BF),
        ]
        + cross_sems
        + [dma(2, dp_size), pltpu.VMEM((row_count, query_width), BF)],
        [vmem] * 7 + [hbm] * 2,
        xs,
        gain_one[None, :],
        mask,
        cosine_table,
        sine_table,
        wides,
        out_full,
        pair,
        down_weight,
        kept=5,
    )
    down_full = down_full.reshape(share, width)
    source = inputs.astype(F32)
    residual = source + jnp.sum(mixed_parts.astype(F32), axis=0)
    inverse_two = lax.rsqrt(jnp.mean(residual * residual, axis=1, keepdims=True) + EPSILON)
    normed_two = residual * inverse_two
    act_two = (normed_two * gain_two).astype(BF)
    pair_rows = pair_rows.reshape(fs_size * weight_rows, 2 * share)
    tokens = fs_size * row_count
    act_full, pair_full, hidden_low, grad_both = call(
        gather_line,
        sizes,
        2,
        55,
        [
            ((fs_size, row_count, width), BF),
            ((dp_size,) + pair_rows.shape, BF),
            ((tokens, share), BF),
            ((tokens, 2 * share), BF),
        ],
        [
            pltpu.VMEM((fs_size, row_count, width), BF),
            pltpu.VMEM((dp_size,) + pair_rows.shape, BF),
            pltpu.VMEM((tokens, width), BF),
            pltpu.VMEM((share, width), BF),
            pltpu.VMEM((tokens, 2 * share), F32),
            pltpu.VMEM((tokens, share), F32),
            dma(2, z_size + 1),
            dma(2, z_size),
            dma(2, 4),
            dma(6),
        ],
        [vmem, hbm, hbm, hbm],
        act_two,
        pair_rows,
        cot_full,
        down_full,
        kept=2,
    )
    pair_full = pair_full.reshape(width, 2 * share)
    act_full = act_full.reshape(tokens, width)

    grad_part = times_trans(grad_both, pair_full).astype(BF)
    pair_grad = outer_sum(act_full, grad_both).astype(BF)
    pair_block = (fs_size * weight_rows, 2 * share)
    pair_half = (fs_size * weight_rows // 2, 2 * share)
    grad_parts, pair_parts, mlp_part, down_part = call(
        scatter_line,
        sizes,
        3,
        60,
        [
            ((z_size, row_count, width), BF),
            ((3,) + pair_block, BF),
            ((tokens, width), BF),
            ((share, width), BF),
        ],
        [pltpu.VMEM((z_size, row_count, width), BF)] * 2
        + [pltpu.VMEM(pair_half, BF)] * 4
        + [
            pltpu.VMEM(pair_block, BF),
            pltpu.VMEM((tokens, share), BF),
            pltpu.VMEM((share, tokens), BF),
            pltpu.VMEM((share, width), BF),
            pltpu.VMEM((tokens, width), BF),
            pltpu.VMEM((tokens, width), BF),
            pltpu.VMEM((share, width), BF),
            dma(2, z_size),
            dma(2, z_size),
            dma(z_size),
            dma(5),
            dma(2, 6),
            dma(6),
        ],
        [hbm] * 6,
        grad_part.reshape(z_size, 2, row_count, width),
        pair_grad.reshape((dp_size,) + pair_block),
        hidden_low,
        hidden_low.T,
        down_full,
        cot_full,
    )
    pair_grad = jnp.sum(pair_parts.astype(F32), axis=0).astype(BF)
    mlp_out = scatter_sum(mlp_part, "fsdp")

    grad_act_two = jnp.sum(grad_parts.astype(F32), axis=0)
    mlp_gain_grad = jnp.sum(normed_two * grad_act_two, axis=0)
    grad_residual = cotangent.astype(F32) + norm_back(
        grad_act_two, normed_two, inverse_two, gain_two
    )
    down_parts_shape = (dp_size,) + down_weight.shape
    pair_back, down_parts, wide_grad, output_grad, grad_act, gain_grad = call(
        attend_backward,
        sizes,
        4,
        50,
        [
            (pair_shape, BF),
            (down_parts_shape, BF),
            ((width, wide_width), BF),
            ((query_width, width), BF),
            (rows_shape, BF),
            ((1, width), F32),
        ],
        [
            pltpu.VMEM(rows_shape, BF),
            pltpu.VMEM(pair_shape[1:], BF),
            pltpu.VMEM(down_weight.shape, BF),
            pltpu.VMEM((dp_size * row_count, wide_width), BF),
        ]
        + cross_sems
        + [dma(2, dp_size)],
        [vmem] * 11 + [hbm] * 2,
        grad_residual.astype(BF),
        xs,
        cosine_table,
        sine_table,
        wides,
        out_full,
        probs,
        query_rot,
        keyval,
        mixed_low,
        act_one,
        pair_grad.reshape(pair_shape),
        down_part.reshape(down_parts_shape),
        kept=4,
    )
    down_grad = jnp.sum(down_parts.astype(F32), axis=0)
    gate_grad, up_grad = small_call(
        functools.partial(unpack_kernel, counts), [(gate_weight.shape, F32)] * 2, pair_back
    )
    by_owner = (dp_size, fs_size, weight_rows)
    gain_grads = jnp.concatenate(
        [
            gain_grad.reshape(by_owner),
            mlp_gain_grad.reshape(by_owner),
            jnp.zeros((dp_size, fs_size, 128 - 2 * weight_rows), F32),
        ],
        axis=2,
    )
    gain_grads = jnp.broadcast_to(gain_grads[:, :, None, :], (dp_size, fs_size, 8, 128))
    wide_piece = (dp_size, weight_rows, wide_width)
    out_piece = (weight_rows, width)
    gain_piece = (dp_size, 8, 128)
    wide_grad, mlp_out = lax.optimization_barrier((wide_grad, mlp_out))
    grad_act_parts, wide_parts, out_sum, gain_parts = call(
        end_kernel,
        sizes,
        5,
        60,
        [(rows_shape, BF), (wide_piece, BF), (out_piece, BF), (gain_piece, F32)],
        [pltpu.VMEM((row_count, width), BF)]
        + [pltpu.VMEM((z_size,) + out_piece, BF)] * 4
        + [pltpu.VMEM((z_size,) + wide_piece, BF)] * 4
        + [pltpu.VMEM((z_size,) + gain_piece, F32)] * 4
        + [
            dma(2, dp_size),
            dma(2, dp_size),
            dma(2, dp_size),
            dma(2, 3 * z_size),
            dma(3 * z_size),
            dma(2, 6 * z_size),
            dma(5),
        ],
        [hbm] * 4,
        grad_act,
        wide_grad.reshape(dp_size, z_size, 2, weight_rows, wide_width),
        output_grad.reshape(z_size, 2, weight_rows, width),
        gain_grads.reshape(dp_size, z_size, 2, 8, 128),
    )
    grad_act_one = jnp.sum(grad_act_parts.astype(F32), axis=0)
    own_inverse = lax.rsqrt(jnp.mean(source * source, axis=1, keepdims=True) + EPSILON)
    input_grad = (
        grad_residual + norm_back(grad_act_one, source * own_inverse, own_inverse, gain_one)
    ).astype(BF)
    outputs = (residual + mlp_out.astype(F32)).astype(BF)
    gain_total = jnp.sum(gain_parts[:, 0, :], axis=0)
    wide_total = wide_parts.astype(F32)

    def from_heads(value):
        return value.transpose(1, 0, 2).reshape(weight_rows, -1)

    return (
        outputs,
        input_grad,
        gain_total[:weight_rows],
        from_heads(wide_total[:, :, :query_width]),
        from_heads(wide_total[:, :, query_width : query_width + HEAD_DIM]),
        from_heads(wide_total[:, :, query_width + HEAD_DIM :]),
        out_sum.astype(F32),
        gain_total[weight_rows : 2 * weight_rows],
        gate_grad,
        up_grad,
        down_grad,
    )


def solution(mesh):
    dp_size, fs_size = mesh.shape["dp"], mesh.shape["fsdp"]
    row = P(ALL, None)
    flat = P(ALL)

    def step(*args):
        return local(dp_size, fs_size, *args)

    return jax.shard_map(
        step,
        mesh=mesh,
        in_specs=(row, flat, flat, row, row, row, row, flat, row, row, row, row),
        out_specs=(row, row, flat, row, row, row, row, flat, row, row, row),
        check_vma=False,
    )
```
